128 devices in a mesh: wide: 16 (over y_lo, z, core), narrow: 8 (over y_hi, x).
Axes of the slice: x: 4, y: 4 (y_hi: 2, y_lo: 2; y = y_hi * 2 + y_lo), z: 4, core: 2. Of those that a mesh axis runs over, the one named last changes fastest.
Arguments:
- coeffs: bfloat16 [1, 2048, 16, 2048], P(None, 'wide', None, 'narrow'), may hold values from -6 to 6
- ham_one: bfloat16 [2048, 2048], replicated, may hold values from -0.125 to 0.125
- grid_one: bfloat16 [2048, 2048], replicated, may hold values from -0.125 to 0.125
- ham_two: bfloat16 [2048, 2048], P('wide'), may hold values from -0.125 to 0.125
- grid_two: bfloat16 [2048, 2048], P('wide'), may hold values from -0.125 to 0.125
- pair_potential: float32 [2048, 2048], P(None, ('wide', 'narrow')), may hold values from 0.1 to 3
- third_energy: float32 [16], replicated, may hold values from 0.5 to 3
Outputs:
- result: bfloat16 [1, 2048, 16, 2048], P(None, ('wide', 'narrow'))
The draws below stay inside these ranges and needn't reach their ends.
All inputs are finite; a program needn't handle non-finite values.
Results may differ from the reference program's by a relative error of at most 0.0055.
Values may be sent and summed in bfloat16 or wider, within the bound.
No kernel may reach another device: no remote copies, remote signals or barrier semaphores. Data moves between devices by JAX's collectives and lax.ppermute only.
A program may use at most 256 MiB of HBM per device.

```python
import math
import jax
import jax.numpy as jnp
from jax import lax

N1 = 2048
N2 = 2048
K = 16
NV = 1


def steps_of(stream_key, dims, split, least, high):
    factor_of, own = 1.0, jax.random.fold_in(stream_key, 6)
    for dim, blocks in split:
        heights = jnp.exp(jax.random.uniform(jax.random.fold_in(own, dim), (blocks,), jnp.float32, least / len(split), high / len(split)))
        factor_of = factor_of * jnp.repeat(heights, dims[dim] // blocks).reshape([-1 if axis == dim else 1 for axis in range(len(dims))])
    return factor_of


def centred(stream_key, dims, width, bound, split=(), kind=jnp.bfloat16):
    gain = steps_of(stream_key, dims, split, -0.22, 0.18) if split else 1.0
    drawn = jax.random.normal(stream_key, dims, jnp.float32) * width * gain
    return jnp.minimum(jnp.maximum(drawn, -bound), bound).astype(kind)


def setup_inputs(seed: int = 0) -> dict:
    splits = jax.random.split(jax.random.key(seed), 8)
    return {
        "coeffs": centred(splits[0], (NV, N1, K, N2), 1.0, 6.0, ((1, 16), (3, 8))),
        "ham_one": centred(splits[1], (N1, N1), N1 ** -0.5, 0.125),
        "grid_one": centred(splits[2], (N1, N1), N1 ** -0.5, 0.125),
        "ham_two": centred(splits[3], (N2, N2), N2 ** -0.5, 0.125, ((0, 16),)),
        "grid_two": centred(splits[4], (N2, N2), N2 ** -0.5, 0.125, ((0, 16),)),
        "pair_potential": jnp.clip(jnp.exp(math.log(3.0) - 3.4011974 * jax.random.uniform(splits[5], (N1, N2), jnp.float32) ** steps_of(splits[5], (N1, N2), ((1, 128),), -0.2, 0.2)), 0.1, 3.0),
        "third_energy": jnp.clip(jax.random.uniform(splits[6], (K,), jnp.float32, 0.5, 3.0), 0.5, 3.0),
    }


def reference(coeffs, ham_one, grid_one, ham_two, grid_two, pair_potential, third_energy):
    def one_vector(block):
        flat = block.reshape(N1 * K, N2)
        applied = lax.dot_general(flat, ham_two, (((1,), (1,)), ((), ())), preferred_element_type=jnp.float32)
        forward = lax.dot_general(flat, grid_two, (((1,), (1,)), ((), ())), preferred_element_type=jnp.float32).astype(jnp.bfloat16)
        across = jnp.dot(ham_one, block.reshape(N1, K * N2), preferred_element_type=jnp.float32).astype(jnp.bfloat16)
        grid_vals = jnp.dot(grid_one, forward.reshape(N1, K * N2), preferred_element_type=jnp.float32).reshape(N1, K, N2)
        weighted = (grid_vals * pair_potential[:, None, :]).astype(jnp.bfloat16)
        back_one = lax.dot_general(grid_one, weighted.reshape(N1, K * N2), (((0,), (0,)), ((), ())), preferred_element_type=jnp.float32).astype(jnp.bfloat16)
        back_two = jnp.dot(back_one.reshape(N1 * K, N2), grid_two, preferred_element_type=jnp.float32)
        energy = (third_energy[None, :, None] * block.astype(jnp.float32)).reshape(N1 * K, N2)
        total = applied + across.astype(jnp.float32).reshape(N1 * K, N2) + back_two + energy
        return total.astype(jnp.bfloat16).reshape(N1, K, N2)

    return lax.map(one_vector, coeffs)
```

```python
import jax
import jax.numpy as jnp
from jax import lax
from jax.experimental import pallas as pl
from jax.experimental.pallas import tpu as pltpu
from jax.sharding import PartitionSpec as P

MIB = 1 << 20


def dot_f32(left, right, contract):
    return lax.dot_general(
        left, right, (contract, ((), ())), preferred_element_type=jnp.float32
    )


def potential_step(p_ref, g_ref, v_ref, q_ref, acc_ref):
    step = pl.program_id(0)
    blocks, rows, width = p_ref.shape

    @pl.when(step == 0)
    def _():
        acc_ref[...] = jnp.zeros_like(acc_ref)

    vals = dot_f32(p_ref[0], g_ref[:, :width], ((1,), (1,)))
    for part in range(1, blocks):
        cols = slice(part * width, (part + 1) * width)
        vals += dot_f32(p_ref[part], g_ref[:, cols], ((1,), (1,)))
    weighted = (vals * v_ref[...].astype(jnp.float32)).astype(jnp.bfloat16)
    acc_ref[...] += dot_f32(weighted, g_ref[...], ((1,), (0,)))

    @pl.when(step == pl.num_programs(0) - 1)
    def _():
        for part in range(blocks):
            cols = slice(part * width, (part + 1) * width)
            q_ref[part] = acc_ref[:, cols].astype(q_ref.dtype)


def grid_two_pass(values, grid_two, potential, tile=512):
    blocks, rows, width = values.shape
    points = grid_two.shape[0]
    cols = blocks * width
    return pl.pallas_call(
        potential_step,
        grid=(points // tile,),
        in_specs=[
            pl.BlockSpec((blocks, rows, width), lambda b: (0, 0, 0)),
            pl.BlockSpec((tile, cols), lambda b: (b, 0)),
            pl.BlockSpec((rows, tile), lambda b: (0, b)),
        ],
        out_specs=pl.BlockSpec((blocks, rows, width), lambda b: (0, 0, 0)),
        out_shape=jax.ShapeDtypeStruct(values.shape, jnp.bfloat16),
        scratch_shapes=[pltpu.VMEM((rows, cols), jnp.float32)],
        compiler_params=pltpu.CompilerParams(vmem_limit_bytes=32 * MIB),
        cost_estimate=pl.CostEstimate(
            flops=4 * rows * cols * points,
            bytes_accessed=2 * (points * cols + rows * points + 2 * rows * cols),
            transcendentals=0,
        ),
        name="grid_two_pass",
    )(values, grid_two, potential)


def finish_step(s_ref, a_ref, o_ref):
    moved = jnp.swapaxes(s_ref[:, 0].astype(jnp.float32), 0, 1)
    total = moved + a_ref[...].reshape(moved.shape)
    o_ref[...] = total.astype(o_ref.dtype)


def finish(back, applied):
    states, blocks, rows, width = back.shape
    return pl.pallas_call(
        finish_step,
        grid=(blocks,),
        in_specs=[
            pl.BlockSpec((states, 1, rows, width), lambda j: (0, j, 0, 0)),
            pl.BlockSpec((rows * states, width), lambda j: (0, j)),
        ],
        out_specs=pl.BlockSpec((rows, states, width), lambda j: (0, 0, j)),
        out_shape=jax.ShapeDtypeStruct((rows, states, blocks * width), jnp.bfloat16),
        cost_estimate=pl.CostEstimate(
            flops=2 * applied.size, bytes_accessed=8 * applied.size, transcendentals=0
        ),
        name="finish",
    )(back, applied)


def on_device(coeffs, ham_one, grid_one, ham_two, grid_two, pair_potential, third_energy):
    n_wide = lax.axis_size("wide")
    n_narrow = lax.axis_size("narrow")
    both = ("wide", "narrow")
    local = coeffs[0]
    rows, states, width = local.shape
    n_one, own_points = pair_potential.shape
    part = n_one // n_narrow
    assert states == n_wide

    full_grid = lax.all_gather(grid_two, "wide", axis=0, tiled=True)
    by_state = lax.all_to_all(jnp.swapaxes(local, 0, 1), "wide", 0, 0, tiled=True)
    one_state = by_state.reshape(n_one, width)
    own_rows = lax.all_to_all(
        local.reshape(n_narrow, rows // n_narrow * states, width), "narrow", 0, 0, tiled=True
    )
    full_ham = lax.all_gather(ham_two, "wide", axis=0, tiled=True)

    slim = pair_potential.astype(jnp.bfloat16).reshape(n_narrow, part, own_points)
    slim = jnp.swapaxes(slim, 1, 2)
    slim = jnp.broadcast_to(slim[None], (n_wide,) + slim.shape)
    slim = lax.all_to_all(
        slim.reshape(n_wide * n_narrow, own_points, part), both, 0, 0, tiled=True
    )
    potential = slim.reshape(n_wide * n_narrow * own_points, part).T

    energy = third_energy[lax.axis_index("wide")]
    up = dot_f32(grid_one, one_state, ((1,), (0,))).astype(jnp.bfloat16)
    side = dot_f32(ham_one, one_state, ((1,), (0,))) + energy * one_state.astype(jnp.float32)

    up_rows = lax.all_to_all(up.reshape(n_narrow, part, width), "narrow", 0, 0, tiled=True)
    down_rows = grid_two_pass(up_rows, full_grid, potential)
    down = lax.all_to_all(down_rows, "narrow", 0, 0, tiled=True).reshape(n_one, width)
    back = (dot_f32(grid_one, down, ((0,), (0,))) + side).astype(jnp.bfloat16)
    count = n_one // (n_wide * n_narrow)
    back = lax.all_to_all(back.reshape(n_wide * n_narrow, count, width), both, 0, 0, tiled=True)

    shape = own_rows.shape
    flat = jnp.swapaxes(own_rows, 0, 1).reshape(shape[1], n_narrow * width)
    applied = dot_f32(flat, full_ham, ((1,), (1,)))
    out = finish(back.reshape(n_wide, n_narrow, count, width), applied)
    return out[None]


def solution(mesh):
    return jax.shard_map(
        on_device,
        mesh=mesh,
        in_specs=(
            P(None, "wide", None, "narrow"),
            P(),
            P(),
            P("wide", None),
            P("wide", None),
            P(None, ("wide", "narrow")),
            P(),
        ),
        out_specs=P(None, ("wide", "narrow"), None, None),
        check_vma=False,
    )
```

```python
import functools

import jax
import jax.numpy as jnp
from jax import lax
from jax.experimental import pallas as pl
from jax.experimental.pallas import tpu as pltpu
from jax.sharding import PartitionSpec as P

MIB = 1 << 20
NN = ((1,), (0,))
NT = ((1,), (1,))
TN = ((0,), (0,))


def dot_f32(left, right, contract):
    return lax.dot_general(
        left, right, (contract, ((), ())), preferred_element_type=jnp.float32
    )


def params(mib):
    return pltpu.CompilerParams(vmem_limit_bytes=mib * MIB)


def cost(flops, moved):
    return pl.CostEstimate(flops=flops, bytes_accessed=moved, transcendentals=0)


def by_blocks(rows_ref, right_ref):
    width = rows_ref.shape[2]
    right = right_ref[...].reshape(-1, right_ref.shape[-1])
    total = dot_f32(rows_ref[0], right[:, :width], NT)
    for part in range(1, rows_ref.shape[0]):
        total += dot_f32(rows_ref[part], right[:, part * width : (part + 1) * width], NT)
    return total


def forward_step(rows_ref, grid_ref, out_ref):
    out_ref[...] = by_blocks(rows_ref, grid_ref).astype(out_ref.dtype).reshape(out_ref.shape)


def forward_pass(rows, gathered, n_wide, count):
    n_narrow, height, width = rows.shape
    inner = height // n_wide
    points = gathered.shape[0] * count
    cols = gathered.shape[2]
    return pl.pallas_call(
        forward_step,
        grid=(n_narrow,),
        in_specs=[
            pl.BlockSpec(rows.shape, lambda n: (0, 0, 0)),
            pl.BlockSpec((gathered.shape[0], count, cols), lambda n: (0, n, 0)),
        ],
        out_specs=pl.BlockSpec((n_wide, 1, inner, points), lambda n: (0, n, 0, 0)),
        out_shape=jax.ShapeDtypeStruct((n_wide, n_narrow, inner, points), jnp.bfloat16),
        compiler_params=params(48),
        cost_estimate=cost(2 * height * cols * points * n_narrow, 10 * MIB),
        name="forward_pass",
    )(rows, gathered)


def middle_step(values_ref, grid_ref, potential_ref, across_ref, out_ref, acc_ref):
    step = pl.program_id(0)
    width = values_ref.shape[1]

    @pl.when(step == 0)
    def _():
        acc_ref[...] = jnp.zeros_like(acc_ref)

    vals = dot_f32(grid_ref[...], values_ref[...], NN)
    weighted = (vals * potential_ref[...].astype(jnp.float32)).astype(jnp.bfloat16)
    acc_ref[...] += dot_f32(weighted, grid_ref[...], TN)

    @pl.when(step == pl.num_programs(0) - 1)
    def _():
        out_ref[:, :width] = acc_ref[...].T.astype(out_ref.dtype)
        out_ref[:, width:] = across_ref[...]


def middle_pass(values, grid_one, potential, across, tile=256):
    n_one, width = values.shape
    return pl.pallas_call(
        middle_step,
        grid=(n_one // tile,),
        in_specs=[
            pl.BlockSpec((n_one, width), lambda a: (0, 0)),
            pl.BlockSpec((tile, n_one), lambda a: (a, 0)),
            pl.BlockSpec((tile, width), lambda a: (a, 0)),
            pl.BlockSpec((n_one, width), lambda a: (0, 0)),
        ],
        out_specs=pl.BlockSpec((n_one, 2 * width), lambda a: (0, 0)),
        out_shape=jax.ShapeDtypeStruct((n_one, 2 * width), jnp.bfloat16),
        scratch_shapes=[pltpu.VMEM((width, n_one), jnp.float32)],
        compiler_params=params(48),
        cost_estimate=cost(4 * n_one * n_one * width, 13 * MIB),
        name="middle_pass",
    )(values, grid_one, potential, across)


def applied_step(rows_ref, ham_ref, energy_ref, out_ref):
    own = rows_ref[pl.program_id(0)].astype(jnp.float32)
    out_ref[...] = by_blocks(rows_ref, ham_ref) + energy_ref[...] * own


def applied_pass(rows, full_ham, energy):
    n_narrow, height, width = rows.shape
    cols = n_narrow * width
    return pl.pallas_call(
        applied_step,
        grid=(n_narrow,),
        in_specs=[
            pl.BlockSpec(rows.shape, lambda n: (0, 0, 0)),
            pl.BlockSpec((width, cols), lambda n: (n, 0)),
            pl.BlockSpec((height, 1), lambda n: (0, 0)),
        ],
        out_specs=pl.BlockSpec((height, width), lambda n: (0, n)),
        out_shape=jax.ShapeDtypeStruct((height, cols), jnp.float32),
        compiler_params=params(48),
        cost_estimate=cost(2 * height * cols * cols, 11 * MIB),
        name="applied_pass",
    )(rows, full_ham, energy)


def final_step(back_ref, grid_ref, across_ref, applied_ref, swap_ref, out_ref):
    states, blocks, rows, width = back_ref.shape
    total = applied_ref[...] + across_ref[...].astype(jnp.float32).reshape(applied_ref.shape)
    for part in range(blocks):
        left = back_ref[:, part].reshape(states * rows, width)
        right = grid_ref[:, part * rows : (part + 1) * rows].reshape(width, -1)
        total += dot_f32(left, right, NN)
    swapped = dot_f32(swap_ref[...], total.astype(jnp.bfloat16), NN)
    out_ref[...] = swapped.astype(out_ref.dtype).reshape(out_ref.shape)


def final_pass(received, gathered, applied, swap):
    states, blocks, rows, double = received.shape
    width = double // 2
    height = states * rows
    cols = applied.shape[1]
    shards = gathered.shape[0]
    return pl.pallas_call(
        final_step,
        grid=(blocks,),
        in_specs=[
            pl.BlockSpec((states, blocks, rows, width), lambda n: (0, 0, 0, 0)),
            pl.BlockSpec((shards, blocks * rows, width), lambda n: (0, 0, n)),
            pl.BlockSpec((states, 1, rows, width), lambda n: (0, n, 0, 1)),
            pl.BlockSpec((height, width), lambda n: (0, n)),
            pl.BlockSpec((height, height), lambda n: (0, 0)),
        ],
        out_specs=pl.BlockSpec((rows, states, width), lambda n: (0, 0, n)),
        out_shape=jax.ShapeDtypeStruct((rows, states, cols), jnp.bfloat16),
        compiler_params=params(48),
        cost_estimate=cost(2 * height * cols * (cols + height), 14 * MIB),
        name="final_pass",
    )(received, gathered, received, applied, swap)


def on_device(coeffs, ham_one, grid_one, ham_two, grid_two, pair_potential, third_energy):
    n_wide = lax.axis_size("wide")
    n_narrow = lax.axis_size("narrow")
    both = ("wide", "narrow")
    local = coeffs[0]
    rows, states, width = local.shape
    n_one, count = pair_potential.shape
    inner = rows // n_narrow
    height = inner * states
    assert states == n_wide and inner == count and n_wide * count == width

    slim = pair_potential.T.astype(jnp.bfloat16)
    gathered = lax.all_gather(jnp.concatenate([grid_two, slim], 0), "wide", axis=0, tiled=False)
    full_ham = lax.all_gather(ham_two, "wide", axis=0, tiled=True)

    own = local.reshape(n_narrow, inner, states, width).swapaxes(1, 2)
    own = lax.all_to_all(own.reshape(n_narrow, height, width), "narrow", 0, 0, tiled=True)
    by_state = lax.all_to_all(jnp.swapaxes(local, 0, 1), "wide", 0, 0, tiled=True)
    across = dot_f32(ham_one, by_state.reshape(n_one, width), NN).astype(jnp.bfloat16)
    own, across = lax.optimization_barrier((own, across))

    values = forward_pass(own, gathered, n_wide, count)
    values = lax.all_to_all(
        values.reshape(n_wide * n_narrow, inner, width), both, 0, 0, tiled=True
    )
    potential = gathered[:, -count:].reshape(width, n_one).T
    pair = middle_pass(values.reshape(n_one, width), grid_one, potential, across)
    pair = lax.all_to_all(
        pair.reshape(n_wide * n_narrow, inner, 2 * width), both, 0, 0, tiled=True
    )

    energy = jnp.repeat(third_energy, inner)[:, None]
    applied = applied_pass(own, full_ham, energy)
    target = jnp.arange(height)
    source = target % states * inner + target // states
    swap = (source[:, None] == jnp.arange(height)[None, :]).astype(jnp.bfloat16)
    out = final_pass(
        pair.reshape(n_wide, n_narrow, inner, 2 * width), gathered, applied, swap
    )
    return out[None]


def solution(mesh):
    return jax.shard_map(
        on_device,
        mesh=mesh,
        in_specs=(
            P(None, "wide", None, "narrow"),
            P(),
            P(),
            P("wide", None),
            P("wide", None),
            P(None, ("wide", "narrow")),
            P(),
        ),
        out_specs=P(None, ("wide", "narrow"), None, None),
        check_vma=False,
    )
```

```python
import jax
import jax.numpy as jnp
from jax import lax
from jax.experimental import pallas as pl
from jax.experimental.pallas import tpu as pltpu
from jax.sharding import PartitionSpec as P

MIB = 1 << 20
NN = ((1,), (0,))
NT = ((1,), (1,))


def dot_f32(left, right, contract):
    return lax.dot_general(
        left, right, (contract, ((), ())), preferred_element_type=jnp.float32
    )


def params():
    return pltpu.CompilerParams(vmem_limit_bytes=56 * MIB)


def cost(flops, moved):
    return pl.CostEstimate(flops=flops, bytes_accessed=moved, transcendentals=0)


def flatten(ref):
    return ref[...].reshape(-1, ref.shape[-1])


def side_by_side(refs, out_ref):
    height, width = refs[0].shape[1:]
    for slot, ref in enumerate(refs):
        for part in range(ref.shape[0]):
            rows = slice(slot * height, (slot + 1) * height)
            out_ref[rows, part * width : (part + 1) * width] = ref[part]


def forward_step(own_ref, mate_ref, first_ref, second_ref, out_ref, rows_ref):
    @pl.when(pl.program_id(0) == 0)
    def _():
        side_by_side((own_ref, mate_ref), rows_ref)

    right = jnp.concatenate([flatten(first_ref), flatten(second_ref)], 0)
    vals = dot_f32(rows_ref[...], right, NT).astype(out_ref.dtype)
    states, _, _, inner, points = out_ref.shape
    vals = vals.reshape(2, states, inner, 2 * points)
    for block in range(2):
        for slot in range(2):
            out_ref[:, block, slot] = vals[slot, :, :, block * points : (block + 1) * points]


def forward_pass(own, mate, gathered, states, piece):
    n_narrow, height, width = own.shape
    shards, _, cols = gathered.shape
    inner = height // states
    points = shards * piece
    resident = pl.BlockSpec(own.shape, lambda s: (0, 0, 0))
    return pl.pallas_call(
        forward_step,
        grid=(n_narrow // 2,),
        in_specs=[
            resident,
            resident,
            pl.BlockSpec((shards, piece, cols), lambda s: (0, 2 * s, 0)),
            pl.BlockSpec((shards, piece, cols), lambda s: (0, 2 * s + 1, 0)),
        ],
        out_specs=pl.BlockSpec((states, 2, 2, inner, points), lambda s: (0, s, 0, 0, 0)),
        out_shape=jax.ShapeDtypeStruct((states, n_narrow, 2, inner, points), jnp.bfloat16),
        scratch_shapes=[pltpu.VMEM((2 * height, cols), jnp.bfloat16)],
        compiler_params=params(),
        cost_estimate=cost(4 * height * cols * points * n_narrow, 8 * MIB),
        name="forward_pass",
    )(own, mate, gathered, gathered)


def middle_step(
    values_ref, grid_ref, turned_ref, potential_ref, across_ref, out_ref, rows_ref, kept_ref
):
    step = pl.program_id(0)
    half = pl.num_programs(0) // 2
    tile = grid_ref.shape[0]
    points = values_ref.shape[-1]
    width = 2 * points

    @pl.when(step == 0)
    def _():
        rows_ref[:, :, :, :points] = values_ref[:, 0]
        for slot in range(2):
            rows_ref[:, slot, :, points:] = values_ref[:, 1, 1 - slot]

    @pl.when(step < half)
    def _():
        vals = dot_f32(grid_ref[...], rows_ref[...].reshape(-1, width), NN)
        weighted = vals * potential_ref[...].astype(jnp.float32)
        kept_ref[pl.ds(pl.multiple_of(step * tile, tile), tile)] = weighted.astype(jnp.bfloat16)

    @pl.when(step >= half)
    def _():
        out_ref[:, :width] = dot_f32(turned_ref[...], kept_ref[...], NN).astype(out_ref.dtype)
        out_ref[:, width:] = across_ref[...]


def middle_pass(values, grid_one, turned, potential, across, tile=512):
    n_one, width = across.shape
    half = n_one // tile
    early = lambda s: (jnp.minimum(s, half - 1), 0)
    late = lambda s: (jnp.maximum(s - half, 0), 0)
    groups, _, _, inner, points = values.shape
    return pl.pallas_call(
        middle_step,
        grid=(2 * half,),
        in_specs=[
            pl.BlockSpec(values.shape, lambda s: (0, 0, 0, 0, 0)),
            pl.BlockSpec((tile, n_one), early),
            pl.BlockSpec((tile, n_one), late),
            pl.BlockSpec((tile, width), early),
            pl.BlockSpec((tile, width), late),
        ],
        out_specs=pl.BlockSpec((tile, 2 * width), late),
        out_shape=jax.ShapeDtypeStruct((n_one, 2 * width), jnp.bfloat16),
        scratch_shapes=[
            pltpu.VMEM((groups, 2, inner, 2 * points), jnp.bfloat16),
            pltpu.VMEM((n_one, width), jnp.bfloat16),
        ],
        compiler_params=params(),
        cost_estimate=cost(4 * n_one * n_one * width, 21 * MIB),
        name="middle_pass",
    )(values, grid_one, turned, potential, across)


def applied_step(own_ref, mate_ref, ham_ref, out_ref, sent_ref, rows_ref):
    @pl.when(pl.program_id(0) == 0)
    def _():
        side_by_side((own_ref, mate_ref), rows_ref)

    vals = dot_f32(rows_ref[...], flatten(ham_ref), NT)
    height = out_ref.shape[0]
    out_ref[...] = vals[:height]
    sent_ref[...] = vals[height:].astype(sent_ref.dtype)


def applied_pass(own, mate, gathered, steps=4):
    n_narrow, height, width = own.shape
    shards, depth, cols = gathered.shape
    depth = depth // 2
    points = shards * depth
    resident = pl.BlockSpec(own.shape, lambda s: (0, 0, 0))
    block = pl.BlockSpec((height, points // steps), lambda s: (0, s))
    return pl.pallas_call(
        applied_step,
        grid=(steps,),
        in_specs=[
            resident,
            resident,
            pl.BlockSpec((shards // steps, depth, cols), lambda s: (s, 1, 0)),
        ],
        out_specs=[block, block],
        out_shape=[
            jax.ShapeDtypeStruct((height, points), jnp.float32),
            jax.ShapeDtypeStruct((height, points), jnp.bfloat16),
        ],
        scratch_shapes=[pltpu.VMEM((2 * height, cols), jnp.bfloat16)],
        compiler_params=params(),
        cost_estimate=cost(4 * height * cols * points, 8 * MIB),
        name="applied_pass",
    )(own, mate, gathered)


def final_step(
    half_ref, near_ref, far_ref, near_a, near_b, far_a, far_b, across_ref, kept_ref, moved_ref,
    own_ref, energy_ref, swap_ref, out_ref, acc_ref,
):
    step = pl.program_id(0)
    states, _, rows, _ = near_ref.shape
    height = states * rows
    lefts = [ref[:, block].reshape(height, -1) for ref in (near_ref, far_ref) for block in range(2)]
    rights = [flatten(ref) for ref in (near_a, near_b, far_a, far_b)]
    total = dot_f32(jnp.concatenate(lefts, 1), jnp.concatenate(rights, 0), NN)

    @pl.when(step == 0)
    def _():
        acc_ref[...] = total

    @pl.when(step > 0)
    def _():
        acc_ref[...] += total

    @pl.when(step == pl.num_programs(0) - 1)
    def _():
        even = half_ref[0] == 0
        blocks, _, width = own_ref.shape
        part = width // 2
        for block in range(blocks):
            cols = slice(block * width, (block + 1) * width)
            kept = kept_ref[:, block * part : (block + 1) * part]
            moved = moved_ref[:, block * part : (block + 1) * part].astype(jnp.float32)
            applied = [jnp.where(even, kept, moved), jnp.where(even, moved, kept)]
            value = acc_ref[:, cols] + jnp.concatenate(applied, 1)
            value += across_ref[:, block].reshape(height, width).astype(jnp.float32)
            value += energy_ref[...] * own_ref[block].astype(jnp.float32)
            swapped = dot_f32(swap_ref[...], value.astype(jnp.bfloat16), NN)
            out_ref[:, :, cols] = swapped.astype(out_ref.dtype).reshape(rows, states, width)


def final_pass(half, received, near, far, kept, moved, own, energy, swap, piece):
    states, blocks, rows, double = received.shape
    width = double // 2
    height = states * rows
    shards, _, cols = near.shape
    points = shards * piece
    weights = [
        pl.BlockSpec((shards, piece, cols), lambda s, h: (0, 2 * s, 0)),
        pl.BlockSpec((shards, piece, cols), lambda s, h: (0, 2 * s + 1, 0)),
    ]
    whole = lambda array: pl.BlockSpec(array.shape, lambda s, h: (0,) * array.ndim)
    return pl.pallas_call(
        final_step,
        grid_spec=pltpu.PrefetchScalarGridSpec(
            num_scalar_prefetch=1,
            grid=(blocks // 2,),
            in_specs=[
                pl.BlockSpec((states, 2, rows, points), lambda s, h: (0, s, 0, h[0])),
                pl.BlockSpec((states, 2, rows, points), lambda s, h: (0, s, 0, 1 - h[0])),
                *weights,
                *weights,
                pl.BlockSpec((states, blocks, rows, width), lambda s, h: (0, 0, 0, 1)),
                whole(kept),
                whole(moved),
                whole(own),
                whole(energy),
                whole(swap),
            ],
            out_specs=pl.BlockSpec((rows, states, cols), lambda s, h: (0, 0, 0)),
            scratch_shapes=[pltpu.VMEM((height, cols), jnp.float32)],
        ),
        out_shape=jax.ShapeDtypeStruct((rows, states, cols), jnp.bfloat16),
        compiler_params=params(),
        cost_estimate=cost(2 * height * cols * (cols + height), 14 * MIB),
        name="final_pass",
    )(
        half, received, received, near, near, far, far, received, kept, moved, own, energy, swap
    )


def on_device(coeffs, ham_one, grid_one, ham_two, grid_two, pair_potential, third_energy):
    n_wide = lax.axis_size("wide")
    n_narrow = lax.axis_size("narrow")
    both = ("wide", "narrow")
    half = lax.axis_index("narrow") % 2
    core = lax.axis_index("wide") % 2
    narrow_pairs = [(n, n ^ 1) for n in range(n_narrow)]
    wide_pairs = [(w, w ^ 1) for w in range(n_wide)]

    local = coeffs[0]
    rows, states, width = local.shape
    n_one, count = pair_potential.shape
    cols = grid_two.shape[1]
    inner = rows // n_narrow
    height = inner * states
    piece = count // 2
    share = rows // 2
    assert states == n_wide and inner == count and n_wide * count == width

    pieces = grid_two.reshape(n_narrow, 2, piece, cols)
    near = lax.dynamic_index_in_dim(pieces, half, 1, False).reshape(share, cols)
    far = lax.dynamic_index_in_dim(pieces, 1 - half, 1, False).reshape(share, cols)
    slim = pair_potential.T.astype(jnp.bfloat16)
    near = lax.all_gather(jnp.concatenate([near, slim], 0), "wide", axis=0, tiled=False)

    away = lax.dynamic_slice_in_dim(ham_two, (1 - core) * share, share, 0)
    stay = lax.dynamic_slice_in_dim(ham_two, core * share, share, 0)
    stay = jnp.where(core == half, stay, lax.ppermute(away, "wide", wide_pairs))
    far = lax.all_gather(jnp.concatenate([far, stay], 0), "wide", axis=0, tiled=False)

    own = local.reshape(n_narrow, inner, states, width).swapaxes(1, 2)
    own = lax.all_to_all(own.reshape(n_narrow, height, width), "narrow", 0, 0, tiled=True)
    mate = lax.ppermute(own, "narrow", narrow_pairs)
    by_state = lax.all_to_all(jnp.swapaxes(local, 0, 1), "wide", 0, 0, tiled=True)
    across = dot_f32(ham_one, by_state.reshape(n_one, width), NN).astype(jnp.bfloat16)
    turned = lax.optimization_barrier(grid_one.T)
    own, mate, across, turned = lax.optimization_barrier((own, mate, across, turned))

    values = forward_pass(own, mate, near, states, piece)
    values = lax.all_to_all(
        values.reshape(n_wide * n_narrow, 2 * inner, width // 2), both, 0, 0, tiled=True
    )
    values = values.reshape(n_wide * n_narrow // 2, 2, 2, inner, width // 2)
    potential = near[:, share:].reshape(n_wide, 2, piece, n_one).swapaxes(0, 1)
    potential = potential.reshape(width, n_one).T
    pair = middle_pass(values, grid_one, turned, potential, across)
    pair = lax.all_to_all(
        pair.reshape(n_wide * n_narrow, inner, 2 * width), both, 0, 0, tiled=True
    )

    kept, moved = applied_pass(own, mate, far)
    moved = lax.ppermute(moved, "narrow", narrow_pairs)
    energy = jnp.repeat(third_energy, inner)[:, None]
    target = jnp.arange(height)
    source = target % states * inner + target // states
    swap = (source[:, None] == jnp.arange(height)[None, :]).astype(jnp.bfloat16)
    out = final_pass(
        half[None],
        pair.reshape(n_wide, n_narrow, inner, 2 * width),
        near, far, kept, moved, own, energy, swap, piece,
    )
    return out[None]


def solution(mesh):
    return jax.shard_map(
        on_device,
        mesh=mesh,
        in_specs=(
            P(None, "wide", None, "narrow"),
            P(),
            P(),
            P("wide", None),
            P("wide", None),
            P(None, ("wide", "narrow")),
            P(),
        ),
        out_specs=P(None, ("wide", "narrow"), None, None),
        check_vma=False,
    )
```

```python
import jax
import jax.numpy as jnp
from jax import lax
from jax.experimental import pallas as pl
from jax.experimental.pallas import tpu as pltpu
from jax.sharding import PartitionSpec as P

MIB = 1 << 20
NN = ((1,), (0,))
NT = ((1,), (1,))


def dot_f32(left, right, contract):
    return lax.dot_general(
        left, right, (contract, ((), ())), preferred_element_type=jnp.float32
    )


def params():
    return pltpu.CompilerParams(vmem_limit_bytes=56 * MIB)


def cost(flops, moved):
    return pl.CostEstimate(flops=flops, bytes_accessed=moved, transcendentals=0)


def flatten(ref):
    return ref[...].reshape(-1, ref.shape[-1])


def side_by_side(refs, out_ref):
    height, width = refs[0].shape[1:]
    for slot, ref in enumerate(refs):
        for part in range(ref.shape[0]):
            rows = slice(slot * height, (slot + 1) * height)
            out_ref[rows, part * width : (part + 1) * width] = ref[part]


def forward_step(own_ref, mate_ref, first_ref, second_ref, out_ref, rows_ref):
    @pl.when(pl.program_id(0) == 0)
    def _():
        side_by_side((own_ref, mate_ref), rows_ref)

    right = jnp.concatenate([flatten(first_ref), flatten(second_ref)], 0)
    vals = dot_f32(rows_ref[...], right, NT).astype(out_ref.dtype)
    states, _, _, inner, points = out_ref.shape
    vals = vals.reshape(2, states, inner, 2 * points)
    for block in range(2):
        for slot in range(2):
            out_ref[:, block, slot] = vals[slot, :, :, block * points : (block + 1) * points]


def forward_pass(own, mate, gathered, states, piece):
    n_narrow, height, width = own.shape
    shards, _, cols = gathered.shape
    inner = height // states
    points = shards * piece
    resident = pl.BlockSpec(own.shape, lambda s: (0, 0, 0))
    return pl.pallas_call(
        forward_step,
        grid=(n_narrow // 2,),
        in_specs=[
            resident,
            resident,
            pl.BlockSpec((shards, piece, cols), lambda s: (0, 2 * s, 0)),
            pl.BlockSpec((shards, piece, cols), lambda s: (0, 2 * s + 1, 0)),
        ],
        out_specs=pl.BlockSpec((states, 2, 2, inner, points), lambda s: (0, s, 0, 0, 0)),
        out_shape=jax.ShapeDtypeStruct((states, n_narrow, 2, inner, points), jnp.bfloat16),
        scratch_shapes=[pltpu.VMEM((2 * height, cols), jnp.bfloat16)],
        compiler_params=params(),
        cost_estimate=cost(4 * height * cols * points * n_narrow, 8 * MIB),
        name="forward_pass",
    )(own, mate, gathered, gathered)


def middle_step(
    values_ref, grid_ref, turned_ref, potential_ref, across_ref, out_ref, rows_ref, kept_ref
):
    step = pl.program_id(0)
    half = pl.num_programs(0) // 2
    tile = grid_ref.shape[0]
    points = values_ref.shape[-1]
    width = 2 * points

    @pl.when(step == 0)
    def _():
        rows_ref[:, :, :, :points] = values_ref[:, 0]
        for slot in range(2):
            rows_ref[:, slot, :, points:] = values_ref[:, 1, 1 - slot]

    @pl.when(step < half)
    def _():
        vals = dot_f32(grid_ref[...], rows_ref[...].reshape(-1, width), NN)
        weighted = vals * potential_ref[...].astype(jnp.float32)
        kept_ref[pl.ds(pl.multiple_of(step * tile, tile), tile)] = weighted.astype(jnp.bfloat16)

    @pl.when(step >= half)
    def _():
        out_ref[:, :width] = dot_f32(turned_ref[...], kept_ref[...], NN).astype(out_ref.dtype)
        out_ref[:, width:] = across_ref[...]


def middle_pass(values, grid_one, turned, potential, across, tile=1024):
    n_one, width = across.shape
    half = n_one // tile
    early = lambda s: (jnp.minimum(s, half - 1), 0)
    late = lambda s: (jnp.maximum(s - half, 0), 0)
    groups, _, _, inner, points = values.shape
    return pl.pallas_call(
        middle_step,
        grid=(2 * half,),
        in_specs=[
            pl.BlockSpec(values.shape, lambda s: (0, 0, 0, 0, 0)),
            pl.BlockSpec((tile, n_one), early),
            pl.BlockSpec((tile, n_one), late),
            pl.BlockSpec((tile, width), early),
            pl.BlockSpec((tile, width), late),
        ],
        out_specs=pl.BlockSpec((tile, 2 * width), late),
        out_shape=jax.ShapeDtypeStruct((n_one, 2 * width), jnp.bfloat16),
        scratch_shapes=[
            pltpu.VMEM((groups, 2, inner, 2 * points), jnp.bfloat16),
            pltpu.VMEM((n_one, width), jnp.bfloat16),
        ],
        compiler_params=params(),
        cost_estimate=cost(4 * n_one * n_one * width, 21 * MIB),
        name="middle_pass",
    )(values, grid_one, turned, potential, across)


def applied_step(own_ref, mate_ref, ham_ref, out_ref, sent_ref, rows_ref):
    @pl.when(pl.program_id(0) == 0)
    def _():
        side_by_side((own_ref, mate_ref), rows_ref)

    vals = dot_f32(rows_ref[...], flatten(ham_ref), NT)
    height = out_ref.shape[0]
    out_ref[...] = vals[:height]
    sent_ref[...] = vals[height:].astype(sent_ref.dtype)


def applied_pass(own, mate, gathered, steps=4):
    n_narrow, height, width = own.shape
    shards, depth, cols = gathered.shape
    points = shards * depth
    resident = pl.BlockSpec(own.shape, lambda s: (0, 0, 0))
    block = pl.BlockSpec((height, points // steps), lambda s: (0, s))
    return pl.pallas_call(
        applied_step,
        grid=(steps,),
        in_specs=[
            resident,
            resident,
            pl.BlockSpec((shards // steps, depth, cols), lambda s: (s, 0, 0)),
        ],
        out_specs=[block, block],
        out_shape=[
            jax.ShapeDtypeStruct((height, points), jnp.float32),
            jax.ShapeDtypeStruct((height, points), jnp.bfloat16),
        ],
        scratch_shapes=[pltpu.VMEM((2 * height, cols), jnp.bfloat16)],
        compiler_params=params(),
        cost_estimate=cost(4 * height * cols * points, 8 * MIB),
        name="applied_pass",
    )(own, mate, gathered)


def final_step(
    half_ref, near_ref, far_ref, near_a, near_b, far_a, far_b, across_ref, kept_ref, moved_ref,
    own_ref, energy_ref, swap_ref, out_ref, acc_ref,
):
    step = pl.program_id(0)
    states, _, rows, _ = near_ref.shape
    height = states * rows
    lefts = [ref[:, block].reshape(height, -1) for ref in (near_ref, far_ref) for block in range(2)]
    rights = [flatten(ref) for ref in (near_a, near_b, far_a, far_b)]
    total = dot_f32(jnp.concatenate(lefts, 1), jnp.concatenate(rights, 0), NN)

    @pl.when(step == 0)
    def _():
        acc_ref[...] = total

    @pl.when(step > 0)
    def _():
        acc_ref[...] += total

    @pl.when(step == pl.num_programs(0) - 1)
    def _():
        even = half_ref[0] == 0
        blocks, _, width = own_ref.shape
        part = width // 2
        for block in range(blocks):
            cols = slice(block * width, (block + 1) * width)
            kept = kept_ref[:, block * part : (block + 1) * part]
            moved = moved_ref[:, block * part : (block + 1) * part].astype(jnp.float32)
            applied = [jnp.where(even, kept, moved), jnp.where(even, moved, kept)]
            value = acc_ref[:, cols] + jnp.concatenate(applied, 1)
            value += across_ref[:, block].reshape(height, width).astype(jnp.float32)
            value += energy_ref[...] * own_ref[block].astype(jnp.float32)
            swapped = dot_f32(swap_ref[...], value.astype(jnp.bfloat16), NN)
            out_ref[:, :, cols] = swapped.astype(out_ref.dtype).reshape(rows, states, width)


def final_pass(half, received, near, far, kept, moved, own, energy, swap, piece):
    states, blocks, rows, double = received.shape
    width = double // 2
    height = states * rows
    shards, _, cols = near.shape
    points = shards * piece
    weights = [
        pl.BlockSpec((shards, piece, cols), lambda s, h: (0, 2 * s, 0)),
        pl.BlockSpec((shards, piece, cols), lambda s, h: (0, 2 * s + 1, 0)),
    ]
    whole = lambda array: pl.BlockSpec(array.shape, lambda s, h: (0,) * array.ndim)
    return pl.pallas_call(
        final_step,
        grid_spec=pltpu.PrefetchScalarGridSpec(
            num_scalar_prefetch=1,
            grid=(blocks // 2,),
            in_specs=[
                pl.BlockSpec((states, 2, rows, points), lambda s, h: (0, s, 0, h[0])),
                pl.BlockSpec((states, 2, rows, points), lambda s, h: (0, s, 0, 1 - h[0])),
                *weights,
                *weights,
                pl.BlockSpec((states, blocks, rows, width), lambda s, h: (0, 0, 0, 1)),
                whole(kept),
                whole(moved),
                whole(own),
                whole(energy),
                whole(swap),
            ],
            out_specs=pl.BlockSpec((rows, states, cols), lambda s, h: (0, 0, 0)),
            scratch_shapes=[pltpu.VMEM((height, cols), jnp.float32)],
        ),
        out_shape=jax.ShapeDtypeStruct((rows, states, cols), jnp.bfloat16),
        compiler_params=params(),
        cost_estimate=cost(2 * height * cols * (cols + height), 14 * MIB),
        name="final_pass",
    )(
        half, received, received, near, near, far, far, received, kept, moved, own, energy, swap
    )


def fetch_other_half(near, after, core, share):
    n_narrow = lax.axis_size("narrow")
    shards = near.shape[0]
    quarter = shards // 4
    ring = 4
    near, _ = lax.optimization_barrier((near, after))
    got = []
    for side in (0, 1):
        step = 1 - 2 * side
        pairs = [(n, n // ring * ring + (n + step) % ring) for n in range(n_narrow)]
        first = 2 * quarter * core + quarter * side
        part = lax.dynamic_slice(near, (first, 0, 0), (quarter, share, near.shape[2]))
        got.append(lax.ppermute(part, "narrow", pairs))
    mine = jnp.concatenate(got, 0)
    pairs = [(w, w ^ 1) for w in range(lax.axis_size("wide"))]
    theirs = lax.ppermute(mine, "wide", pairs)
    return jnp.where(
        core == 0, jnp.concatenate([mine, theirs], 0), jnp.concatenate([theirs, mine], 0)
    )


def on_device(coeffs, ham_one, grid_one, ham_two, grid_two, pair_potential, third_energy):
    n_wide = lax.axis_size("wide")
    n_narrow = lax.axis_size("narrow")
    both = ("wide", "narrow")
    half = lax.axis_index("narrow") % 2
    core = lax.axis_index("wide") % 2
    narrow_pairs = [(n, n ^ 1) for n in range(n_narrow)]
    wide_pairs = [(w, w ^ 1) for w in range(n_wide)]

    local = coeffs[0]
    rows, states, width = local.shape
    n_one, count = pair_potential.shape
    cols = grid_two.shape[1]
    inner = rows // n_narrow
    height = inner * states
    piece = count // 2
    share = rows // 2
    assert states == n_wide and inner == count and n_wide * count == width

    pieces = grid_two.reshape(n_narrow, 2, piece, cols)
    near = lax.dynamic_index_in_dim(pieces, half, 1, False).reshape(share, cols)
    slim = pair_potential.T.astype(jnp.bfloat16)
    near = lax.all_gather(jnp.concatenate([near, slim], 0), "wide", axis=0, tiled=False)

    away = lax.dynamic_slice_in_dim(ham_two, (1 - core) * share, share, 0)
    stay = lax.dynamic_slice_in_dim(ham_two, core * share, share, 0)
    stay = jnp.where(core == half, stay, lax.ppermute(away, "wide", wide_pairs))
    half_ham = lax.all_gather(stay, "wide", axis=0, tiled=False)

    own = local.reshape(n_narrow, inner, states, width).swapaxes(1, 2)
    own = lax.all_to_all(own.reshape(n_narrow, height, width), "narrow", 0, 0, tiled=True)
    mate = lax.ppermute(own, "narrow", narrow_pairs)
    by_state = lax.all_to_all(jnp.swapaxes(local, 0, 1), "wide", 0, 0, tiled=True)
    turned = lax.optimization_barrier(grid_one.T)
    own, mate, by_state, turned = lax.optimization_barrier((own, mate, by_state, turned))

    values = forward_pass(own, mate, near, states, piece)
    across = dot_f32(ham_one, by_state.reshape(n_one, width), NN).astype(jnp.bfloat16)
    far = fetch_other_half(near, values, core, share)
    values = lax.all_to_all(
        values.reshape(n_wide * n_narrow, 2 * inner, width // 2), both, 0, 0, tiled=True
    )
    values = values.reshape(n_wide * n_narrow // 2, 2, 2, inner, width // 2)
    potential = near[:, share:].reshape(n_wide, 2, piece, n_one).swapaxes(0, 1)
    potential = potential.reshape(width, n_one).T
    pair = middle_pass(values, grid_one, turned, potential, across)
    pair = lax.all_to_all(
        pair.reshape(n_wide * n_narrow, inner, 2 * width), both, 0, 0, tiled=True
    )

    kept, moved = applied_pass(own, mate, half_ham)
    moved = lax.ppermute(moved, "narrow", narrow_pairs)
    energy = jnp.repeat(third_energy, inner)[:, None]
    target = jnp.arange(height)
    source = target % states * inner + target // states
    swap = (source[:, None] == jnp.arange(height)[None, :]).astype(jnp.bfloat16)
    out = final_pass(
        half[None],
        pair.reshape(n_wide, n_narrow, inner, 2 * width),
        near, far, kept, moved, own, energy, swap, piece,
    )
    return out[None]


def solution(mesh):
    return jax.shard_map(
        on_device,
        mesh=mesh,
        in_specs=(
            P(None, "wide", None, "narrow"),
            P(),
            P(),
            P("wide", None),
            P("wide", None),
            P(None, ("wide", "narrow")),
            P(),
        ),
        out_specs=P(None, ("wide", "narrow"), None, None),
        check_vma=False,
    )
```

```python
import jax
import jax.numpy as jnp
from jax import lax
from jax.experimental import pallas as pl
from jax.experimental.pallas import tpu as pltpu
from jax.sharding import PartitionSpec as P

MIB = 1 << 20
NN = ((1,), (0,))
NT = ((1,), (1,))


def dot_f32(left, right, contract):
    return lax.dot_general(
        left, right, (contract, ((), ())), preferred_element_type=jnp.float32
    )


def params():
    return pltpu.CompilerParams(vmem_limit_bytes=56 * MIB)


def cost(flops, moved):
    return pl.CostEstimate(flops=flops, bytes_accessed=moved, transcendentals=0)


def flatten(ref):
    return ref[...].reshape(-1, ref.shape[-1])


def side_by_side(refs, out_ref):
    height, width = refs[0].shape[1:]
    for slot, ref in enumerate(refs):
        for part in range(ref.shape[0]):
            rows = slice(slot * height, (slot + 1) * height)
            out_ref[rows, part * width : (part + 1) * width] = ref[part]


def forward_step(own_ref, mate_ref, first_ref, second_ref, out_ref, rows_ref):
    @pl.when(pl.program_id(0) == 0)
    def _():
        side_by_side((own_ref, mate_ref), rows_ref)

    right = jnp.concatenate([flatten(first_ref), flatten(second_ref)], 0)
    vals = dot_f32(rows_ref[...], right, NT).astype(out_ref.dtype)
    states, _, _, inner, points = out_ref.shape
    vals = vals.reshape(2, states, inner, 2 * points)
    for block in range(2):
        for slot in range(2):
            out_ref[:, block, slot] = vals[slot, :, :, block * points : (block + 1) * points]


def forward_pass(own, mate, gathered, states, piece):
    n_narrow, height, width = own.shape
    shards, _, cols = gathered.shape
    inner = height // states
    points = shards * piece
    resident = pl.BlockSpec(own.shape, lambda s: (0, 0, 0))
    return pl.pallas_call(
        forward_step,
        grid=(n_narrow // 2,),
        in_specs=[
            resident,
            resident,
            pl.BlockSpec((shards, piece, cols), lambda s: (0, 2 * s, 0)),
            pl.BlockSpec((shards, piece, cols), lambda s: (0, 2 * s + 1, 0)),
        ],
        out_specs=pl.BlockSpec((states, 2, 2, inner, points), lambda s: (0, s, 0, 0, 0)),
        out_shape=jax.ShapeDtypeStruct((states, n_narrow, 2, inner, points), jnp.bfloat16),
        scratch_shapes=[pltpu.VMEM((2 * height, cols), jnp.bfloat16)],
        compiler_params=params(),
        cost_estimate=cost(4 * height * cols * points * n_narrow, 8 * MIB),
        name="forward_pass",
    )(own, mate, gathered, gathered)


def middle_step(
    values_ref, grid_ref, turned_ref, potential_ref, across_ref, out_ref, rows_ref, kept_ref
):
    step = pl.program_id(0)
    half = pl.num_programs(0) // 2
    tile = grid_ref.shape[0]
    points = values_ref.shape[-1]
    width = 2 * points

    @pl.when(step == 0)
    def _():
        rows_ref[:, :, :, :points] = values_ref[:, 0]
        for slot in range(2):
            rows_ref[:, slot, :, points:] = values_ref[:, 1, 1 - slot]

    @pl.when(step < half)
    def _():
        vals = dot_f32(grid_ref[...], rows_ref[...].reshape(-1, width), NN)
        weighted = vals * potential_ref[...].astype(jnp.float32)
        kept_ref[pl.ds(pl.multiple_of(step * tile, tile), tile)] = weighted.astype(jnp.bfloat16)

    @pl.when(step >= half)
    def _():
        out_ref[:, :width] = dot_f32(turned_ref[...], kept_ref[...], NN).astype(out_ref.dtype)
        out_ref[:, width:] = across_ref[...]


def middle_pass(values, grid_one, turned, potential, across, tile=1024):
    n_one, width = across.shape
    half = n_one // tile
    early = lambda s: (jnp.minimum(s, half - 1), 0)
    late = lambda s: (jnp.maximum(s - half, 0), 0)
    groups, _, _, inner, points = values.shape
    return pl.pallas_call(
        middle_step,
        grid=(2 * half,),
        in_specs=[
            pl.BlockSpec(values.shape, lambda s: (0, 0, 0, 0, 0)),
            pl.BlockSpec((tile, n_one), early),
            pl.BlockSpec((tile, n_one), late),
            pl.BlockSpec((tile, width), early),
            pl.BlockSpec((tile, width), late),
        ],
        out_specs=pl.BlockSpec((tile, 2 * width), late),
        out_shape=jax.ShapeDtypeStruct((n_one, 2 * width), jnp.bfloat16),
        scratch_shapes=[
            pltpu.VMEM((groups, 2, inner, 2 * points), jnp.bfloat16),
            pltpu.VMEM((n_one, width), jnp.bfloat16),
        ],
        compiler_params=params(),
        cost_estimate=cost(4 * n_one * n_one * width, 21 * MIB),
        name="middle_pass",
    )(values, grid_one, turned, potential, across)


def applied_step(own_ref, mate_ref, ham_ref, out_ref, sent_ref, rows_ref):
    @pl.when(pl.program_id(0) == 0)
    def _():
        side_by_side((own_ref, mate_ref), rows_ref)

    vals = dot_f32(rows_ref[...], flatten(ham_ref), NT)
    height = out_ref.shape[0]
    out_ref[...] = vals[:height]
    sent_ref[...] = vals[height:].astype(sent_ref.dtype)


def applied_pass(own, mate, gathered, steps=4):
    n_narrow, height, width = own.shape
    shards, depth, cols = gathered.shape
    points = shards * depth
    resident = pl.BlockSpec(own.shape, lambda s: (0, 0, 0))
    block = pl.BlockSpec((height, points // steps), lambda s: (0, s))
    return pl.pallas_call(
        applied_step,
        grid=(steps,),
        in_specs=[
            resident,
            resident,
            pl.BlockSpec((shards // steps, depth, cols), lambda s: (s, 0, 0)),
        ],
        out_specs=[block, block],
        out_shape=[
            jax.ShapeDtypeStruct((height, points), jnp.float32),
            jax.ShapeDtypeStruct((height, points), jnp.bfloat16),
        ],
        scratch_shapes=[pltpu.VMEM((2 * height, cols), jnp.bfloat16)],
        compiler_params=params(),
        cost_estimate=cost(4 * height * cols * points, 8 * MIB),
        name="applied_pass",
    )(own, mate, gathered)


def final_step(
    half_ref, near_ref, far_ref, near_a, near_b, far_a, far_b, across_ref, kept_ref, moved_ref,
    own_ref, energy_ref, swap_ref, out_ref, acc_ref,
):
    step = pl.program_id(0)
    states, _, rows, _ = near_ref.shape
    height = states * rows
    lefts = [ref[:, block].reshape(height, -1) for ref in (near_ref, far_ref) for block in range(2)]
    rights = [flatten(ref) for ref in (near_a, near_b, far_a, far_b)]
    total = dot_f32(jnp.concatenate(lefts, 1), jnp.concatenate(rights, 0), NN)

    @pl.when(step == 0)
    def _():
        acc_ref[...] = total

    @pl.when(step > 0)
    def _():
        acc_ref[...] += total

    @pl.when(step == pl.num_programs(0) - 1)
    def _():
        even = half_ref[0] == 0
        blocks, _, width = own_ref.shape
        part = width // 2
        for block in range(blocks):
            cols = slice(block * width, (block + 1) * width)
            kept = kept_ref[:, block * part : (block + 1) * part]
            moved = moved_ref[:, block * part : (block + 1) * part].astype(jnp.float32)
            applied = [jnp.where(even, kept, moved), jnp.where(even, moved, kept)]
            value = acc_ref[:, cols] + jnp.concatenate(applied, 1)
            value += across_ref[:, block].reshape(height, width).astype(jnp.float32)
            value += energy_ref[...] * own_ref[block].astype(jnp.float32)
            swapped = dot_f32(swap_ref[...], value.astype(jnp.bfloat16), NN)
            out_ref[:, :, cols] = swapped.astype(out_ref.dtype).reshape(rows, states, width)


def final_pass(half, received, near, far, kept, moved, own, energy, swap, piece):
    states, blocks, rows, double = received.shape
    width = double // 2
    height = states * rows
    shards, _, cols = near.shape
    points = shards * piece
    weights = [
        pl.BlockSpec((shards, piece, cols), lambda s, h: (0, 2 * s, 0)),
        pl.BlockSpec((shards, piece, cols), lambda s, h: (0, 2 * s + 1, 0)),
    ]
    whole = lambda array: pl.BlockSpec(array.shape, lambda s, h: (0,) * array.ndim)
    return pl.pallas_call(
        final_step,
        grid_spec=pltpu.PrefetchScalarGridSpec(
            num_scalar_prefetch=1,
            grid=(blocks // 2,),
            in_specs=[
                pl.BlockSpec((states, 2, rows, points), lambda s, h: (0, s, 0, h[0])),
                pl.BlockSpec((states, 2, rows, points), lambda s, h: (0, s, 0, 1 - h[0])),
                *weights,
                *weights,
                pl.BlockSpec((states, blocks, rows, width), lambda s, h: (0, 0, 0, 1)),
                whole(kept),
                whole(moved),
                whole(own),
                whole(energy),
                whole(swap),
            ],
            out_specs=pl.BlockSpec((rows, states, cols), lambda s, h: (0, 0, 0)),
            scratch_shapes=[pltpu.VMEM((height, cols), jnp.float32)],
        ),
        out_shape=jax.ShapeDtypeStruct((rows, states, cols), jnp.bfloat16),
        compiler_params=params(),
        cost_estimate=cost(2 * height * cols * (cols + height), 14 * MIB),
        name="final_pass",
    )(
        half, received, received, near, near, far, far, received, kept, moved, own, energy, swap
    )


def on_device(coeffs, ham_one, grid_one, ham_two, grid_two, pair_potential, third_energy):
    n_wide = lax.axis_size("wide")
    n_narrow = lax.axis_size("narrow")
    both = ("wide", "narrow")
    half = lax.axis_index("narrow") % 2
    core = lax.axis_index("wide") % 2
    narrow_pairs = [(n, n ^ 1) for n in range(n_narrow)]
    wide_pairs = [(w, w ^ 1) for w in range(n_wide)]

    local = coeffs[0]
    rows, states, width = local.shape
    n_one, count = pair_potential.shape
    cols = grid_two.shape[1]
    inner = rows // n_narrow
    height = inner * states
    piece = count // 2
    share = rows // 2
    assert states == n_wide and inner == count and n_wide * count == width

    pieces = grid_two.reshape(n_narrow, 2, piece, cols)
    near = lax.dynamic_index_in_dim(pieces, half, 1, False).reshape(share, cols)
    far = lax.dynamic_index_in_dim(pieces, 1 - half, 1, False).reshape(share, cols)
    slim = pair_potential.T.astype(jnp.bfloat16)
    near = lax.all_gather(jnp.concatenate([near, slim], 0), "wide", axis=0, tiled=False)

    away = lax.dynamic_slice_in_dim(ham_two, (1 - core) * share, share, 0)
    stay = lax.dynamic_slice_in_dim(ham_two, core * share, share, 0)
    stay = jnp.where(core == half, stay, lax.ppermute(away, "wide", wide_pairs))
    half_ham = lax.all_gather(stay, "wide", axis=0, tiled=False)

    own = local.reshape(n_narrow, inner, states, width).swapaxes(1, 2)
    own = lax.all_to_all(own.reshape(n_narrow, height, width), "narrow", 0, 0, tiled=True)
    own, far = lax.optimization_barrier((own, far))
    far = lax.all_gather(far, "wide", axis=0, tiled=False)
    mate = lax.ppermute(own, "narrow", narrow_pairs)
    by_state = lax.all_to_all(jnp.swapaxes(local, 0, 1), "wide", 0, 0, tiled=True)
    turned = lax.optimization_barrier(grid_one.T)
    own, mate, by_state, turned = lax.optimization_barrier((own, mate, by_state, turned))

    values = forward_pass(own, mate, near, states, piece)
    across = dot_f32(ham_one, by_state.reshape(n_one, width), NN).astype(jnp.bfloat16)
    values = lax.all_to_all(
        values.reshape(n_wide * n_narrow, 2 * inner, width // 2), both, 0, 0, tiled=True
    )
    values = values.reshape(n_wide * n_narrow // 2, 2, 2, inner, width // 2)
    potential = near[:, share:].reshape(n_wide, 2, piece, n_one).swapaxes(0, 1)
    potential = potential.reshape(width, n_one).T
    pair = middle_pass(values, grid_one, turned, potential, across)
    pair = lax.all_to_all(
        pair.reshape(n_wide * n_narrow, inner, 2 * width), both, 0, 0, tiled=True
    )

    kept, moved = applied_pass(own, mate, half_ham)
    moved = lax.ppermute(moved, "narrow", narrow_pairs)
    energy = jnp.repeat(third_energy, inner)[:, None]
    target = jnp.arange(height)
    source = target % states * inner + target // states
    swap = (source[:, None] == jnp.arange(height)[None, :]).astype(jnp.bfloat16)
    out = final_pass(
        half[None],
        pair.reshape(n_wide, n_narrow, inner, 2 * width),
        near, far, kept, moved, own, energy, swap, piece,
    )
    return out[None]


def solution(mesh):
    return jax.shard_map(
        on_device,
        mesh=mesh,
        in_specs=(
            P(None, "wide", None, "narrow"),
            P(),
            P(),
            P("wide", None),
            P("wide", None),
            P(None, ("wide", "narrow")),
            P(),
        ),
        out_specs=P(None, ("wide", "narrow"), None, None),
        check_vma=False,
    )
```

```python
import jax
import jax.numpy as jnp
from jax import lax
from jax.experimental import pallas as pl
from jax.experimental.pallas import tpu as pltpu
from jax.sharding import PartitionSpec as P

MIB = 1 << 20
NN = ((1,), (0,))
NT = ((1,), (1,))


def dot_f32(left, right, contract):
    return lax.dot_general(
        left, right, (contract, ((), ())), preferred_element_type=jnp.float32
    )


def params():
    return pltpu.CompilerParams(vmem_limit_bytes=56 * MIB)


def cost(flops, moved):
    return pl.CostEstimate(flops=flops, bytes_accessed=moved, transcendentals=0)


def flatten(ref):
    return ref[...].reshape(-1, ref.shape[-1])


def side_by_side(refs, out_ref):
    height, width = refs[0].shape[1:]
    for slot, ref in enumerate(refs):
        for part in range(ref.shape[0]):
            rows = slice(slot * height, (slot + 1) * height)
            out_ref[rows, part * width : (part + 1) * width] = ref[part]


def forward_step(own_ref, mate_ref, first_ref, second_ref, out_ref, rows_ref):
    @pl.when(pl.program_id(0) == 0)
    def _():
        side_by_side((own_ref, mate_ref), rows_ref)

    right = jnp.concatenate([flatten(first_ref), flatten(second_ref)], 0)
    vals = dot_f32(rows_ref[...], right, NT).astype(out_ref.dtype)
    states, _, _, inner, points = out_ref.shape
    vals = vals.reshape(2, states, inner, 2 * points)
    for block in range(2):
        for slot in range(2):
            out_ref[:, block, slot] = vals[slot, :, :, block * points : (block + 1) * points]


def forward_pass(own, mate, gathered, states, piece):
    n_narrow, height, width = own.shape
    shards, _, cols = gathered.shape
    inner = height // states
    points = shards * piece
    resident = pl.BlockSpec(own.shape, lambda s: (0, 0, 0))
    return pl.pallas_call(
        forward_step,
        grid=(n_narrow // 2,),
        in_specs=[
            resident,
            resident,
            pl.BlockSpec((shards, piece, cols), lambda s: (0, 2 * s, 0)),
            pl.BlockSpec((shards, piece, cols), lambda s: (0, 2 * s + 1, 0)),
        ],
        out_specs=pl.BlockSpec((states, 2, 2, inner, points), lambda s: (0, s, 0, 0, 0)),
        out_shape=jax.ShapeDtypeStruct((states, n_narrow, 2, inner, points), jnp.bfloat16),
        scratch_shapes=[pltpu.VMEM((2 * height, cols), jnp.bfloat16)],
        compiler_params=params(),
        cost_estimate=cost(4 * height * cols * points * n_narrow, 8 * MIB),
        name="forward_pass",
    )(own, mate, gathered, gathered)


def middle_step(
    values_ref, grid_ref, turned_ref, potential_ref, across_ref, out_ref, rows_ref, kept_ref
):
    step = pl.program_id(0)
    half = pl.num_programs(0) // 2
    tile = grid_ref.shape[0]
    points = values_ref.shape[-1]
    width = 2 * points

    @pl.when(step == 0)
    def _():
        rows_ref[:, :, :, :points] = values_ref[:, 0]
        for slot in range(2):
            rows_ref[:, slot, :, points:] = values_ref[:, 1, 1 - slot]

    @pl.when(step < half)
    def _():
        vals = dot_f32(grid_ref[...], rows_ref[...].reshape(-1, width), NN)
        weighted = vals * potential_ref[...].astype(jnp.float32)
        kept_ref[pl.ds(pl.multiple_of(step * tile, tile), tile)] = weighted.astype(jnp.bfloat16)

    @pl.when(step >= half)
    def _():
        out_ref[:, :width] = dot_f32(turned_ref[...], kept_ref[...], NN).astype(out_ref.dtype)
        out_ref[:, width:] = across_ref[...]


def middle_pass(values, grid_one, turned, potential, across, tile=1024):
    n_one, width = across.shape
    half = n_one // tile
    early = lambda s: (jnp.minimum(s, half - 1), 0)
    late = lambda s: (jnp.maximum(s - half, 0), 0)
    groups, _, _, inner, points = values.shape
    return pl.pallas_call(
        middle_step,
        grid=(2 * half,),
        in_specs=[
            pl.BlockSpec(values.shape, lambda s: (0, 0, 0, 0, 0)),
            pl.BlockSpec((tile, n_one), early),
            pl.BlockSpec((tile, n_one), late),
            pl.BlockSpec((tile, width), early),
            pl.BlockSpec((tile, width), late),
        ],
        out_specs=pl.BlockSpec((tile, 2 * width), late),
        out_shape=jax.ShapeDtypeStruct((n_one, 2 * width), jnp.bfloat16),
        scratch_shapes=[
            pltpu.VMEM((groups, 2, inner, 2 * points), jnp.bfloat16),
            pltpu.VMEM((n_one, width), jnp.bfloat16),
        ],
        compiler_params=params(),
        cost_estimate=cost(4 * n_one * n_one * width, 21 * MIB),
        name="middle_pass",
    )(values, grid_one, turned, potential, across)


def applied_step(own_ref, mate_ref, ham_ref, out_ref, sent_ref, rows_ref):
    @pl.when(pl.program_id(0) == 0)
    def _():
        side_by_side((own_ref, mate_ref), rows_ref)

    vals = dot_f32(rows_ref[...], flatten(ham_ref), NT)
    height = out_ref.shape[0]
    out_ref[...] = vals[:height]
    sent_ref[...] = vals[height:].astype(sent_ref.dtype)


def applied_pass(own, mate, gathered, steps=4):
    n_narrow, height, width = own.shape
    shards, sides, depth, cols = gathered.shape
    points = shards * sides * depth
    parts = steps // sides
    resident = pl.BlockSpec(own.shape, lambda s: (0, 0, 0))
    block = pl.BlockSpec((height, points // steps), lambda s: (0, s))
    return pl.pallas_call(
        applied_step,
        grid=(steps,),
        in_specs=[
            resident,
            resident,
            pl.BlockSpec((shards // parts, 1, depth, cols), lambda s: (s % parts, s // parts, 0, 0)),
        ],
        out_specs=[block, block],
        out_shape=[
            jax.ShapeDtypeStruct((height, points), jnp.float32),
            jax.ShapeDtypeStruct((height, points), jnp.bfloat16),
        ],
        scratch_shapes=[pltpu.VMEM((2 * height, cols), jnp.bfloat16)],
        compiler_params=params(),
        cost_estimate=cost(4 * height * cols * points, 8 * MIB),
        name="applied_pass",
    )(own, mate, gathered)


def final_step(
    half_ref, near_ref, far_ref, near_a, near_b, far_a0, far_a1, far_b0, far_b1, across_ref,
    kept_ref, moved_ref, own_ref, energy_ref, swap_ref, out_ref, acc_ref,
):
    step = pl.program_id(0)
    states, _, rows, _ = near_ref.shape
    height = states * rows
    lefts = [ref[:, block].reshape(height, -1) for ref in (near_ref, far_ref) for block in range(2)]
    rights = [flatten(ref) for ref in (near_a, near_b, far_a0, far_a1, far_b0, far_b1)]
    total = dot_f32(jnp.concatenate(lefts, 1), jnp.concatenate(rights, 0), NN)

    @pl.when(step == 0)
    def _():
        acc_ref[...] = total

    @pl.when(step > 0)
    def _():
        acc_ref[...] += total

    @pl.when(step == pl.num_programs(0) - 1)
    def _():
        even = half_ref[0] == 0
        blocks, _, width = own_ref.shape
        part = width // 2
        for block in range(blocks):
            cols = slice(block * width, (block + 1) * width)
            kept = kept_ref[:, block * part : (block + 1) * part]
            moved = moved_ref[:, block * part : (block + 1) * part].astype(jnp.float32)
            applied = [jnp.where(even, kept, moved), jnp.where(even, moved, kept)]
            value = acc_ref[:, cols] + jnp.concatenate(applied, 1)
            value += across_ref[:, block].reshape(height, width).astype(jnp.float32)
            value += energy_ref[...] * own_ref[block].astype(jnp.float32)
            swapped = dot_f32(swap_ref[...], value.astype(jnp.bfloat16), NN)
            out_ref[:, :, cols] = swapped.astype(out_ref.dtype).reshape(rows, states, width)


def final_pass(half, received, near, far, kept, moved, own, energy, swap, piece):
    states, blocks, rows, double = received.shape
    width = double // 2
    height = states * rows
    shards, _, cols = near.shape
    points = shards * piece
    weights = [
        pl.BlockSpec((shards, piece, cols), lambda s, h: (0, 2 * s, 0)),
        pl.BlockSpec((shards, piece, cols), lambda s, h: (0, 2 * s + 1, 0)),
    ]
    part = (far.shape[0], 1, piece, cols)
    others = [
        pl.BlockSpec(part, lambda s, h: (0, 0, 2 * s, 0)),
        pl.BlockSpec(part, lambda s, h: (0, 1, 2 * s, 0)),
        pl.BlockSpec(part, lambda s, h: (0, 0, 2 * s + 1, 0)),
        pl.BlockSpec(part, lambda s, h: (0, 1, 2 * s + 1, 0)),
    ]
    whole = lambda array: pl.BlockSpec(array.shape, lambda s, h: (0,) * array.ndim)
    return pl.pallas_call(
        final_step,
        grid_spec=pltpu.PrefetchScalarGridSpec(
            num_scalar_prefetch=1,
            grid=(blocks // 2,),
            in_specs=[
                pl.BlockSpec((states, 2, rows, points), lambda s, h: (0, s, 0, h[0])),
                pl.BlockSpec((states, 2, rows, points), lambda s, h: (0, s, 0, 1 - h[0])),
                *weights,
                *others,
                pl.BlockSpec((states, blocks, rows, width), lambda s, h: (0, 0, 0, 1)),
                whole(kept),
                whole(moved),
                whole(own),
                whole(energy),
                whole(swap),
            ],
            out_specs=pl.BlockSpec((rows, states, cols), lambda s, h: (0, 0, 0)),
            scratch_shapes=[pltpu.VMEM((height, cols), jnp.float32)],
        ),
        out_shape=jax.ShapeDtypeStruct((rows, states, cols), jnp.bfloat16),
        compiler_params=params(),
        cost_estimate=cost(2 * height * cols * (cols + height), 14 * MIB),
        name="final_pass",
    )(
        half, received, received, near, near, far, far, far, far, received, kept, moved, own, energy, swap
    )


def on_device(coeffs, ham_one, grid_one, ham_two, grid_two, pair_potential, third_energy):
    n_wide = lax.axis_size("wide")
    n_narrow = lax.axis_size("narrow")
    both = ("wide", "narrow")
    half = lax.axis_index("narrow") % 2
    core = lax.axis_index("wide") % 2
    narrow_pairs = [(n, n ^ 1) for n in range(n_narrow)]
    wide_pairs = [(w, w ^ 1) for w in range(n_wide)]

    local = coeffs[0]
    rows, states, width = local.shape
    n_one, count = pair_potential.shape
    cols = grid_two.shape[1]
    inner = rows // n_narrow
    height = inner * states
    piece = count // 2
    share = rows // 2
    assert states == n_wide and inner == count and n_wide * count == width

    pieces = grid_two.reshape(n_narrow, 2, piece, cols)
    near = lax.dynamic_index_in_dim(pieces, half, 1, False).reshape(share, cols)
    far = lax.dynamic_index_in_dim(pieces, 1 - half, 1, False).reshape(share, cols)
    groups = n_wide // 2
    side = lax.axis_index("wide") // groups
    across_y = [(w, (w + groups) % n_wide) for w in range(n_wide)]
    members = [list(range(groups)), list(range(groups, n_wide))]
    slim = pair_potential.T.astype(jnp.bfloat16)
    near = lax.all_gather(jnp.concatenate([near, slim], 0), "wide", axis=0, tiled=False)

    away = lax.dynamic_slice_in_dim(ham_two, (1 - core) * share, share, 0)
    stay = lax.dynamic_slice_in_dim(ham_two, core * share, share, 0)
    stay = jnp.where(core == half, stay, lax.ppermute(away, "wide", wide_pairs))

    own = local.reshape(n_narrow, inner, states, width).swapaxes(1, 2)
    own = lax.all_to_all(own.reshape(n_narrow, height, width), "narrow", 0, 0, tiled=True)
    mine = jnp.stack([stay, far])
    theirs = lax.ppermute(mine, "wide", across_y)
    own, theirs, mine = lax.optimization_barrier((own, theirs, mine))
    joined = jnp.where(side == 0, jnp.stack([mine, theirs]), jnp.stack([theirs, mine]))
    stay, far = joined[:, 0], joined[:, 1]
    half_ham = lax.all_gather(stay, "wide", axis=0, tiled=False, axis_index_groups=members)
    far = lax.all_gather(far, "wide", axis=0, tiled=False, axis_index_groups=members)
    mate = lax.ppermute(own, "narrow", narrow_pairs)
    by_state = lax.all_to_all(jnp.swapaxes(local, 0, 1), "wide", 0, 0, tiled=True)
    turned = lax.optimization_barrier(grid_one.T)
    own, mate, by_state, turned = lax.optimization_barrier((own, mate, by_state, turned))

    values = forward_pass(own, mate, near, states, piece)
    across = dot_f32(ham_one, by_state.reshape(n_one, width), NN).astype(jnp.bfloat16)
    values = lax.all_to_all(
        values.reshape(n_wide * n_narrow, 2 * inner, width // 2), both, 0, 0, tiled=True
    )
    values = values.reshape(n_wide * n_narrow // 2, 2, 2, inner, width // 2)
    potential = near[:, share:].reshape(n_wide, 2, piece, n_one).swapaxes(0, 1)
    potential = potential.reshape(width, n_one).T
    pair = middle_pass(values, grid_one, turned, potential, across)
    pair = lax.all_to_all(
        pair.reshape(n_wide * n_narrow, inner, 2 * width), both, 0, 0, tiled=True
    )

    kept, moved = applied_pass(own, mate, half_ham)
    moved = lax.ppermute(moved, "narrow", narrow_pairs)
    energy = jnp.repeat(third_energy, inner)[:, None]
    target = jnp.arange(height)
    source = target % states * inner + target // states
    swap = (source[:, None] == jnp.arange(height)[None, :]).astype(jnp.bfloat16)
    out = final_pass(
        half[None],
        pair.reshape(n_wide, n_narrow, inner, 2 * width),
        near, far, kept, moved, own, energy, swap, piece,
    )
    return out[None]


def solution(mesh):
    return jax.shard_map(
        on_device,
        mesh=mesh,
        in_specs=(
            P(None, "wide", None, "narrow"),
            P(),
            P(),
            P("wide", None),
            P("wide", None),
            P(None, ("wide", "narrow")),
            P(),
        ),
        out_specs=P(None, ("wide", "narrow"), None, None),
        check_vma=False,
    )
```

```python
import jax
import jax.numpy as jnp
from jax import lax
from jax.experimental import pallas as pl
from jax.experimental.pallas import tpu as pltpu
from jax.sharding import PartitionSpec as P

MIB = 1 << 20
NN = ((1,), (0,))
NT = ((1,), (1,))


def dot_f32(left, right, contract):
    return lax.dot_general(
        left, right, (contract, ((), ())), preferred_element_type=jnp.float32
    )


def params():
    return pltpu.CompilerParams(vmem_limit_bytes=56 * MIB)


def cost(flops, moved):
    return pl.CostEstimate(flops=flops, bytes_accessed=moved, transcendentals=0)


def flatten(ref):
    return ref[...].reshape(-1, ref.shape[-1])


def side_by_side(refs, out_ref):
    height, width = refs[0].shape[1:]
    for slot, ref in enumerate(refs):
        for part in range(ref.shape[0]):
            rows = slice(slot * height, (slot + 1) * height)
            out_ref[rows, part * width : (part + 1) * width] = ref[part]


def forward_step(own_ref, mate_ref, a0_ref, a1_ref, b0_ref, b1_ref, out_ref, rows_ref):
    @pl.when(pl.program_id(0) == 0)
    def _():
        side_by_side((own_ref, mate_ref), rows_ref)

    right = jnp.concatenate([flatten(ref) for ref in (a0_ref, a1_ref, b0_ref, b1_ref)], 0)
    vals = dot_f32(rows_ref[...], right, NT).astype(out_ref.dtype)
    states, _, _, inner, points = out_ref.shape
    vals = vals.reshape(2, states, inner, 2 * points)
    for block in range(2):
        for slot in range(2):
            out_ref[:, block, slot] = vals[slot, :, :, block * points : (block + 1) * points]


def piece_specs(gathered, piece):
    shards, _, _, cols = gathered.shape
    block = (shards, 1, piece, cols)
    return [
        pl.BlockSpec(block, lambda s, *_: (0, 0, 2 * s, 0)),
        pl.BlockSpec(block, lambda s, *_: (0, 1, 2 * s, 0)),
        pl.BlockSpec(block, lambda s, *_: (0, 0, 2 * s + 1, 0)),
        pl.BlockSpec(block, lambda s, *_: (0, 1, 2 * s + 1, 0)),
    ]


def forward_pass(own, mate, gathered, states, piece):
    n_narrow, height, width = own.shape
    shards, sides, _, cols = gathered.shape
    shards = shards * sides
    inner = height // states
    points = shards * piece
    resident = pl.BlockSpec(own.shape, lambda s: (0, 0, 0))
    return pl.pallas_call(
        forward_step,
        grid=(n_narrow // 2,),
        in_specs=[
            resident,
            resident,
            *piece_specs(gathered, piece),
        ],
        out_specs=pl.BlockSpec((states, 2, 2, inner, points), lambda s: (0, s, 0, 0, 0)),
        out_shape=jax.ShapeDtypeStruct((states, n_narrow, 2, inner, points), jnp.bfloat16),
        scratch_shapes=[pltpu.VMEM((2 * height, cols), jnp.bfloat16)],
        compiler_params=params(),
        cost_estimate=cost(4 * height * cols * points * n_narrow, 8 * MIB),
        name="forward_pass",
    )(own, mate, gathered, gathered, gathered, gathered)


def middle_step(
    values_ref, grid_ref, turned_ref, potential_ref, across_ref, out_ref, rows_ref, kept_ref
):
    step = pl.program_id(0)
    half = pl.num_programs(0) // 2
    tile = grid_ref.shape[0]
    points = values_ref.shape[-1]
    width = 2 * points

    @pl.when(step == 0)
    def _():
        rows_ref[:, :, :, :points] = values_ref[:, 0]
        for slot in range(2):
            rows_ref[:, slot, :, points:] = values_ref[:, 1, 1 - slot]

    @pl.when(step < half)
    def _():
        vals = dot_f32(grid_ref[...], rows_ref[...].reshape(-1, width), NN)
        weighted = vals * potential_ref[...].astype(jnp.float32)
        kept_ref[pl.ds(pl.multiple_of(step * tile, tile), tile)] = weighted.astype(jnp.bfloat16)

    @pl.when(step >= half)
    def _():
        out_ref[:, :width] = dot_f32(turned_ref[...], kept_ref[...], NN).astype(out_ref.dtype)
        out_ref[:, width:] = across_ref[...]


def middle_pass(values, grid_one, turned, potential, across, tile=1024):
    n_one, width = across.shape
    half = n_one // tile
    early = lambda s: (jnp.minimum(s, half - 1), 0)
    late = lambda s: (jnp.maximum(s - half, 0), 0)
    groups, _, _, inner, points = values.shape
    return pl.pallas_call(
        middle_step,
        grid=(2 * half,),
        in_specs=[
            pl.BlockSpec(values.shape, lambda s: (0, 0, 0, 0, 0)),
            pl.BlockSpec((tile, n_one), early),
            pl.BlockSpec((tile, n_one), late),
            pl.BlockSpec((tile, width), early),
            pl.BlockSpec((tile, width), late),
        ],
        out_specs=pl.BlockSpec((tile, 2 * width), late),
        out_shape=jax.ShapeDtypeStruct((n_one, 2 * width), jnp.bfloat16),
        scratch_shapes=[
            pltpu.VMEM((groups, 2, inner, 2 * points), jnp.bfloat16),
            pltpu.VMEM((n_one, width), jnp.bfloat16),
        ],
        compiler_params=params(),
        cost_estimate=cost(4 * n_one * n_one * width, 21 * MIB),
        name="middle_pass",
    )(values, grid_one, turned, potential, across)


def applied_step(own_ref, mate_ref, ham_ref, out_ref, sent_ref, rows_ref):
    @pl.when(pl.program_id(0) == 0)
    def _():
        side_by_side((own_ref, mate_ref), rows_ref)

    vals = dot_f32(rows_ref[...], flatten(ham_ref), NT)
    height = out_ref.shape[0]
    out_ref[...] = vals[:height]
    sent_ref[...] = vals[height:].astype(sent_ref.dtype)


def applied_pass(own, mate, gathered, steps=4):
    n_narrow, height, width = own.shape
    shards, sides, depth, cols = gathered.shape
    points = shards * sides * depth
    parts = steps // sides
    resident = pl.BlockSpec(own.shape, lambda s: (0, 0, 0))
    block = pl.BlockSpec((height, points // steps), lambda s: (0, s))
    return pl.pallas_call(
        applied_step,
        grid=(steps,),
        in_specs=[
            resident,
            resident,
            pl.BlockSpec((shards // parts, 1, depth, cols), lambda s: (s % parts, s // parts, 0, 0)),
        ],
        out_specs=[block, block],
        out_shape=[
            jax.ShapeDtypeStruct((height, points), jnp.float32),
            jax.ShapeDtypeStruct((height, points), jnp.bfloat16),
        ],
        scratch_shapes=[pltpu.VMEM((2 * height, cols), jnp.bfloat16)],
        compiler_params=params(),
        cost_estimate=cost(4 * height * cols * points, 8 * MIB),
        name="applied_pass",
    )(own, mate, gathered)


def final_step(
    half_ref, near_ref, far_ref, near_a0, near_a1, near_b0, near_b1, far_a0, far_a1, far_b0,
    far_b1, across_ref, kept_ref, moved_ref, own_ref, energy_ref, swap_ref, out_ref, acc_ref,
):
    step = pl.program_id(0)
    states, _, rows, _ = near_ref.shape
    height = states * rows
    lefts = [ref[:, block].reshape(height, -1) for ref in (near_ref, far_ref) for block in range(2)]
    rights = (near_a0, near_a1, near_b0, near_b1, far_a0, far_a1, far_b0, far_b1)
    rights = [flatten(ref) for ref in rights]
    total = dot_f32(jnp.concatenate(lefts, 1), jnp.concatenate(rights, 0), NN)

    @pl.when(step == 0)
    def _():
        acc_ref[...] = total

    @pl.when(step > 0)
    def _():
        acc_ref[...] += total

    @pl.when(step == pl.num_programs(0) - 1)
    def _():
        even = half_ref[0] == 0
        blocks, _, width = own_ref.shape
        part = width // 2
        for block in range(blocks):
            cols = slice(block * width, (block + 1) * width)
            kept = kept_ref[:, block * part : (block + 1) * part]
            moved = moved_ref[:, block * part : (block + 1) * part].astype(jnp.float32)
            applied = [jnp.where(even, kept, moved), jnp.where(even, moved, kept)]
            value = acc_ref[:, cols] + jnp.concatenate(applied, 1)
            value += across_ref[:, block].reshape(height, width).astype(jnp.float32)
            value += energy_ref[...] * own_ref[block].astype(jnp.float32)
            swapped = dot_f32(swap_ref[...], value.astype(jnp.bfloat16), NN)
            out_ref[:, :, cols] = swapped.astype(out_ref.dtype).reshape(rows, states, width)


def final_pass(half, received, near, far, kept, moved, own, energy, swap, piece):
    states, blocks, rows, double = received.shape
    width = double // 2
    height = states * rows
    shards, sides, _, cols = near.shape
    points = shards * sides * piece
    whole = lambda array: pl.BlockSpec(array.shape, lambda s, h: (0,) * array.ndim)
    return pl.pallas_call(
        final_step,
        grid_spec=pltpu.PrefetchScalarGridSpec(
            num_scalar_prefetch=1,
            grid=(blocks // 2,),
            in_specs=[
                pl.BlockSpec((states, 2, rows, points), lambda s, h: (0, s, 0, h[0])),
                pl.BlockSpec((states, 2, rows, points), lambda s, h: (0, s, 0, 1 - h[0])),
                *piece_specs(near, piece),
                *piece_specs(far, piece),
                pl.BlockSpec((states, blocks, rows, width), lambda s, h: (0, 0, 0, 1)),
                whole(kept),
                whole(moved),
                whole(own),
                whole(energy),
                whole(swap),
            ],
            out_specs=pl.BlockSpec((rows, states, cols), lambda s, h: (0, 0, 0)),
            scratch_shapes=[pltpu.VMEM((height, cols), jnp.float32)],
        ),
        out_shape=jax.ShapeDtypeStruct((rows, states, cols), jnp.bfloat16),
        compiler_params=params(),
        cost_estimate=cost(2 * height * cols * (cols + height), 14 * MIB),
        name="final_pass",
    )(
        half, received, received, *[near] * 4, *[far] * 4, received, kept, moved, own, energy, swap
    )


def on_device(coeffs, ham_one, grid_one, ham_two, grid_two, pair_potential, third_energy):
    n_wide = lax.axis_size("wide")
    n_narrow = lax.axis_size("narrow")
    both = ("wide", "narrow")
    half = lax.axis_index("narrow") % 2
    core = lax.axis_index("wide") % 2
    narrow_pairs = [(n, n ^ 1) for n in range(n_narrow)]
    wide_pairs = [(w, w ^ 1) for w in range(n_wide)]

    local = coeffs[0]
    rows, states, width = local.shape
    n_one, count = pair_potential.shape
    cols = grid_two.shape[1]
    inner = rows // n_narrow
    height = inner * states
    piece = count // 2
    share = rows // 2
    assert states == n_wide and inner == count and n_wide * count == width

    groups = n_wide // 2
    side = lax.axis_index("wide") // groups
    across_y = [(w, (w + groups) % n_wide) for w in range(n_wide)]
    members = [list(range(groups)), list(range(groups, n_wide))]

    def both_sides(mine, theirs):
        return jnp.where(side == 0, jnp.stack([mine, theirs]), jnp.stack([theirs, mine]))

    def gather(value):
        return lax.all_gather(value, "wide", axis=0, tiled=False, axis_index_groups=members)

    pieces = grid_two.reshape(n_narrow, 2, piece, cols)
    near = lax.dynamic_index_in_dim(pieces, half, 1, False).reshape(share, cols)
    near = jnp.concatenate([near, pair_potential.T.astype(jnp.bfloat16)], 0)
    near = gather(both_sides(near, lax.ppermute(near, "wide", across_y)))

    far = lax.dynamic_index_in_dim(pieces, 1 - half, 1, False).reshape(share, cols)
    away = lax.dynamic_slice_in_dim(ham_two, (1 - core) * share, share, 0)
    stay = lax.dynamic_slice_in_dim(ham_two, core * share, share, 0)
    stay = jnp.where(core == half, stay, lax.ppermute(away, "wide", wide_pairs))

    own = local.reshape(n_narrow, inner, states, width).swapaxes(1, 2)
    own = lax.all_to_all(own.reshape(n_narrow, height, width), "narrow", 0, 0, tiled=True)
    mine = jnp.stack([stay, far])
    theirs = lax.ppermute(mine, "wide", across_y)
    own, theirs, mine = lax.optimization_barrier((own, theirs, mine))
    joined = both_sides(mine, theirs)
    stay, far = joined[:, 0], joined[:, 1]
    half_ham = gather(stay)
    far = gather(far)
    mate = lax.ppermute(own, "narrow", narrow_pairs)
    by_state = lax.all_to_all(jnp.swapaxes(local, 0, 1), "wide", 0, 0, tiled=True)
    turned = lax.optimization_barrier(grid_one.T)
    own, mate, by_state, turned = lax.optimization_barrier((own, mate, by_state, turned))

    values = forward_pass(own, mate, near, states, piece)
    across = dot_f32(ham_one, by_state.reshape(n_one, width), NN).astype(jnp.bfloat16)
    values = lax.all_to_all(
        values.reshape(n_wide * n_narrow, 2 * inner, width // 2), both, 0, 0, tiled=True
    )
    values = values.reshape(n_wide * n_narrow // 2, 2, 2, inner, width // 2)
    potential = near[:, :, share:].reshape(groups, 2, 2, piece, n_one).transpose(2, 1, 0, 3, 4)
    potential = potential.reshape(width, n_one).T
    pair = middle_pass(values, grid_one, turned, potential, across)
    pair = lax.all_to_all(
        pair.reshape(n_wide * n_narrow, inner, 2 * width), both, 0, 0, tiled=True
    )

    kept, moved = applied_pass(own, mate, half_ham)
    moved = lax.ppermute(moved, "narrow", narrow_pairs)
    energy = jnp.repeat(third_energy, inner)[:, None]
    target = jnp.arange(height)
    source = target % states * inner + target // states
    swap = (source[:, None] == jnp.arange(height)[None, :]).astype(jnp.bfloat16)
    out = final_pass(
        half[None],
        pair.reshape(n_wide, n_narrow, inner, 2 * width),
        near, far, kept, moved, own, energy, swap, piece,
    )
    return out[None]


def solution(mesh):
    return jax.shard_map(
        on_device,
        mesh=mesh,
        in_specs=(
            P(None, "wide", None, "narrow"),
            P(),
            P(),
            P("wide", None),
            P("wide", None),
            P(None, ("wide", "narrow")),
            P(),
        ),
        out_specs=P(None, ("wide", "narrow"), None, None),
        check_vma=False,
    )
```

```python
import jax
import jax.numpy as jnp
from jax import lax
from jax.experimental import pallas as pl
from jax.experimental.pallas import tpu as pltpu
from jax.sharding import PartitionSpec as P

MIB = 1 << 20
NN = ((1,), (0,))
NT = ((1,), (1,))


def dot_f32(left, right, contract):
    return lax.dot_general(
        left, right, (contract, ((), ())), preferred_element_type=jnp.float32
    )


def params():
    return pltpu.CompilerParams(vmem_limit_bytes=56 * MIB)


def cost(flops, moved):
    return pl.CostEstimate(flops=flops, bytes_accessed=moved, transcendentals=0)


def flatten(ref):
    return ref[...].reshape(-1, ref.shape[-1])


def side_by_side(refs, out_ref):
    height, width = refs[0].shape[1:]
    for slot, ref in enumerate(refs):
        for part in range(ref.shape[0]):
            rows = slice(slot * height, (slot + 1) * height)
            out_ref[rows, part * width : (part + 1) * width] = ref[part]


def forward_step(own_ref, mate_ref, a0_ref, a1_ref, b0_ref, b1_ref, out_ref, rows_ref):
    @pl.when(pl.program_id(0) == 0)
    def _():
        side_by_side((own_ref, mate_ref), rows_ref)

    right = jnp.concatenate([flatten(ref) for ref in (a0_ref, a1_ref, b0_ref, b1_ref)], 0)
    vals = dot_f32(rows_ref[...], right, NT).astype(out_ref.dtype)
    states, _, _, inner, points = out_ref.shape
    vals = vals.reshape(2, states, inner, 2 * points)
    for block in range(2):
        for slot in range(2):
            out_ref[:, block, slot] = vals[slot, :, :, block * points : (block + 1) * points]


def piece_specs(gathered, piece):
    shards, _, _, cols = gathered.shape
    block = (shards, 1, piece, cols)
    return [
        pl.BlockSpec(block, lambda s, *_: (0, 0, 2 * s, 0)),
        pl.BlockSpec(block, lambda s, *_: (0, 1, 2 * s, 0)),
        pl.BlockSpec(block, lambda s, *_: (0, 0, 2 * s + 1, 0)),
        pl.BlockSpec(block, lambda s, *_: (0, 1, 2 * s + 1, 0)),
    ]


def forward_pass(own, mate, gathered, states, piece):
    n_narrow, height, width = own.shape
    shards, sides, _, cols = gathered.shape
    shards = shards * sides
    inner = height // states
    points = shards * piece
    resident = pl.BlockSpec(own.shape, lambda s: (0, 0, 0))
    return pl.pallas_call(
        forward_step,
        grid=(n_narrow // 2,),
        in_specs=[
            resident,
            resident,
            *piece_specs(gathered, piece),
        ],
        out_specs=pl.BlockSpec((states, 2, 2, inner, points), lambda s: (0, s, 0, 0, 0)),
        out_shape=jax.ShapeDtypeStruct((states, n_narrow, 2, inner, points), jnp.bfloat16),
        scratch_shapes=[pltpu.VMEM((2 * height, cols), jnp.bfloat16)],
        compiler_params=params(),
        cost_estimate=cost(4 * height * cols * points * n_narrow, 8 * MIB),
        name="forward_pass",
    )(own, mate, gathered, gathered, gathered, gathered)


def middle_step(
    values_ref, grid_ref, turned_ref, potential_ref, across_ref, out_ref, rows_ref, kept_ref
):
    step = pl.program_id(0)
    half = pl.num_programs(0) // 2
    tile = grid_ref.shape[0]
    points = values_ref.shape[-1]
    width = 2 * points

    @pl.when(step == 0)
    def _():
        rows_ref[:, :, :, :points] = values_ref[:, 0]
        for slot in range(2):
            rows_ref[:, slot, :, points:] = values_ref[:, 1, 1 - slot]

    @pl.when(step < half)
    def _():
        vals = dot_f32(grid_ref[...], rows_ref[...].reshape(-1, width), NN)
        weighted = vals * potential_ref[...].astype(jnp.float32)
        kept_ref[pl.ds(pl.multiple_of(step * tile, tile), tile)] = weighted.astype(jnp.bfloat16)

    @pl.when(step >= half)
    def _():
        out_ref[:, :width] = dot_f32(turned_ref[...], kept_ref[...], NN).astype(out_ref.dtype)
        out_ref[:, width:] = across_ref[...]


def middle_pass(values, grid_one, turned, potential, across, tile=1024):
    n_one, width = across.shape
    half = n_one // tile
    early = lambda s: (jnp.minimum(s, half - 1), 0)
    late = lambda s: (jnp.maximum(s - half, 0), 0)
    groups, _, _, inner, points = values.shape
    return pl.pallas_call(
        middle_step,
        grid=(2 * half,),
        in_specs=[
            pl.BlockSpec(values.shape, lambda s: (0, 0, 0, 0, 0)),
            pl.BlockSpec((tile, n_one), early),
            pl.BlockSpec((tile, n_one), late),
            pl.BlockSpec((tile, width), early),
            pl.BlockSpec((tile, width), late),
        ],
        out_specs=pl.BlockSpec((tile, 2 * width), late),
        out_shape=jax.ShapeDtypeStruct((n_one, 2 * width), jnp.bfloat16),
        scratch_shapes=[
            pltpu.VMEM((groups, 2, inner, 2 * points), jnp.bfloat16),
            pltpu.VMEM((n_one, width), jnp.bfloat16),
        ],
        compiler_params=params(),
        cost_estimate=cost(4 * n_one * n_one * width, 21 * MIB),
        name="middle_pass",
    )(values, grid_one, turned, potential, across)


def applied_step(own_ref, mate_ref, ham_ref, out_ref, sent_ref, rows_ref):
    @pl.when(pl.program_id(0) == 0)
    def _():
        side_by_side((own_ref, mate_ref), rows_ref)

    vals = dot_f32(rows_ref[...], flatten(ham_ref), NT)
    height = out_ref.shape[0]
    out_ref[...] = vals[:height]
    sent_ref[...] = vals[height:].astype(sent_ref.dtype)


def applied_pass(own, mate, gathered, steps=4):
    n_narrow, height, width = own.shape
    shards, sides, depth, cols = gathered.shape
    points = shards * sides * depth
    parts = steps // sides
    resident = pl.BlockSpec(own.shape, lambda s: (0, 0, 0))
    block = pl.BlockSpec((height, points // steps), lambda s: (0, s))
    return pl.pallas_call(
        applied_step,
        grid=(steps,),
        in_specs=[
            resident,
            resident,
            pl.BlockSpec((shards // parts, 1, depth, cols), lambda s: (s % parts, s // parts, 0, 0)),
        ],
        out_specs=[block, block],
        out_shape=[
            jax.ShapeDtypeStruct((height, points), jnp.float32),
            jax.ShapeDtypeStruct((height, points), jnp.bfloat16),
        ],
        scratch_shapes=[pltpu.VMEM((2 * height, cols), jnp.bfloat16)],
        compiler_params=params(),
        cost_estimate=cost(4 * height * cols * points, 8 * MIB),
        name="applied_pass",
    )(own, mate, gathered)


def final_step(
    half_ref, near_ref, far_ref, near_a0, near_a1, near_b0, near_b1, far_a0, far_a1, far_b0,
    far_b1, across_ref, kept_ref, moved_ref, own_ref, energy_ref, swap_ref, out_ref, acc_ref,
):
    step = pl.program_id(0)
    states, _, rows, _ = near_ref.shape
    height = states * rows
    lefts = [ref[:, block].reshape(height, -1) for ref in (near_ref, far_ref) for block in range(2)]
    rights = (near_a0, near_a1, near_b0, near_b1, far_a0, far_a1, far_b0, far_b1)
    rights = [flatten(ref) for ref in rights]
    total = dot_f32(jnp.concatenate(lefts, 1), jnp.concatenate(rights, 0), NN)

    @pl.when(step == 0)
    def _():
        acc_ref[...] = total

    @pl.when(step > 0)
    def _():
        acc_ref[...] += total

    @pl.when(step == pl.num_programs(0) - 1)
    def _():
        even = half_ref[0] == 0
        blocks, _, width = own_ref.shape
        part = width // 2
        for block in range(blocks):
            cols = slice(block * width, (block + 1) * width)
            kept = kept_ref[:, block * part : (block + 1) * part]
            moved = moved_ref[:, block * part : (block + 1) * part].astype(jnp.float32)
            applied = [jnp.where(even, kept, moved), jnp.where(even, moved, kept)]
            value = acc_ref[:, cols] + jnp.concatenate(applied, 1)
            value += across_ref[:, block].reshape(height, width).astype(jnp.float32)
            value += energy_ref[...] * own_ref[block].astype(jnp.float32)
            swapped = dot_f32(swap_ref[...], value.astype(jnp.bfloat16), NN)
            out_ref[:, :, cols] = swapped.astype(out_ref.dtype).reshape(rows, states, width)


def final_pass(half, received, near, far, kept, moved, own, energy, swap, piece):
    states, blocks, rows, double = received.shape
    width = double // 2
    height = states * rows
    shards, sides, _, cols = near.shape
    points = shards * sides * piece
    whole = lambda array: pl.BlockSpec(array.shape, lambda s, h: (0,) * array.ndim)
    return pl.pallas_call(
        final_step,
        grid_spec=pltpu.PrefetchScalarGridSpec(
            num_scalar_prefetch=1,
            grid=(blocks // 2,),
            in_specs=[
                pl.BlockSpec((states, 2, rows, points), lambda s, h: (0, s, 0, h[0])),
                pl.BlockSpec((states, 2, rows, points), lambda s, h: (0, s, 0, 1 - h[0])),
                *piece_specs(near, piece),
                *piece_specs(far, piece),
                pl.BlockSpec((states, blocks, rows, width), lambda s, h: (0, 0, 0, 1)),
                whole(kept),
                whole(moved),
                whole(own),
                whole(energy),
                whole(swap),
            ],
            out_specs=pl.BlockSpec((rows, states, cols), lambda s, h: (0, 0, 0)),
            scratch_shapes=[pltpu.VMEM((height, cols), jnp.float32)],
        ),
        out_shape=jax.ShapeDtypeStruct((rows, states, cols), jnp.bfloat16),
        compiler_params=params(),
        cost_estimate=cost(2 * height * cols * (cols + height), 14 * MIB),
        name="final_pass",
    )(
        half, received, received, *[near] * 4, *[far] * 4, received, kept, moved, own, energy, swap
    )


def on_device(coeffs, ham_one, grid_one, ham_two, grid_two, pair_potential, third_energy):
    n_wide = lax.axis_size("wide")
    n_narrow = lax.axis_size("narrow")
    both = ("wide", "narrow")
    half = lax.axis_index("narrow") % 2
    core = lax.axis_index("wide") % 2
    narrow_pairs = [(n, n ^ 1) for n in range(n_narrow)]
    wide_pairs = [(w, w ^ 1) for w in range(n_wide)]

    local = coeffs[0]
    rows, states, width = local.shape
    n_one, count = pair_potential.shape
    cols = grid_two.shape[1]
    inner = rows // n_narrow
    height = inner * states
    piece = count // 2
    share = rows // 2
    assert states == n_wide and inner == count and n_wide * count == width

    groups = n_wide // 2
    side = lax.axis_index("wide") // groups
    across_y = [(w, (w + groups) % n_wide) for w in range(n_wide)]
    members = [list(range(groups)), list(range(groups, n_wide))]

    def both_sides(mine, theirs):
        return jnp.where(side == 0, jnp.stack([mine, theirs]), jnp.stack([theirs, mine]))

    def gather(value):
        return lax.all_gather(value, "wide", axis=0, tiled=False, axis_index_groups=members)

    pieces = grid_two.reshape(n_narrow, 2, piece, cols)
    near = lax.dynamic_index_in_dim(pieces, half, 1, False).reshape(share, cols)
    near = jnp.concatenate([near, pair_potential.T.astype(jnp.bfloat16)], 0)
    near = gather(both_sides(near, lax.ppermute(near, "wide", across_y)))

    far = lax.dynamic_index_in_dim(pieces, 1 - half, 1, False).reshape(share, cols)
    away = lax.dynamic_slice_in_dim(ham_two, (1 - core) * share, share, 0)
    stay = lax.dynamic_slice_in_dim(ham_two, core * share, share, 0)
    stay = jnp.where(core == half, stay, lax.ppermute(away, "wide", wide_pairs))

    own = local.reshape(n_narrow, inner, states, width).swapaxes(1, 2)
    own = lax.all_to_all(own.reshape(n_narrow, height, width), "narrow", 0, 0, tiled=True)
    mine = jnp.stack([stay, far])
    theirs = lax.ppermute(mine, "wide", across_y)
    mate = lax.ppermute(own, "narrow", narrow_pairs)
    by_state = lax.all_to_all(jnp.swapaxes(local, 0, 1), "wide", 0, 0, tiled=True)

    turned = lax.optimization_barrier(grid_one.T)
    values = forward_pass(own, mate, near, states, piece)
    values, by_state, turned = lax.optimization_barrier((values, by_state, turned))
    by_state, theirs, mine = lax.optimization_barrier((by_state, theirs, mine))
    joined = both_sides(mine, theirs)
    stay, far = joined[:, 0], joined[:, 1]
    half_ham = gather(stay)
    far = gather(far)
    across = dot_f32(ham_one, by_state.reshape(n_one, width), NN).astype(jnp.bfloat16)
    values = lax.all_to_all(
        values.reshape(n_wide * n_narrow, 2 * inner, width // 2), both, 0, 0, tiled=True
    )
    values = values.reshape(n_wide * n_narrow // 2, 2, 2, inner, width // 2)
    potential = near[:, :, share:].reshape(groups, 2, 2, piece, n_one).transpose(2, 1, 0, 3, 4)
    potential = potential.reshape(width, n_one).T
    pair = middle_pass(values, grid_one, turned, potential, across)
    pair = lax.all_to_all(
        pair.reshape(n_wide * n_narrow, inner, 2 * width), both, 0, 0, tiled=True
    )

    kept, moved = applied_pass(own, mate, half_ham)
    moved = lax.ppermute(moved, "narrow", narrow_pairs)
    energy = jnp.repeat(third_energy, inner)[:, None]
    target = jnp.arange(height)
    source = target % states * inner + target // states
    swap = (source[:, None] == jnp.arange(height)[None, :]).astype(jnp.bfloat16)
    out = final_pass(
        half[None],
        pair.reshape(n_wide, n_narrow, inner, 2 * width),
        near, far, kept, moved, own, energy, swap, piece,
    )
    return out[None]


def solution(mesh):
    return jax.shard_map(
        on_device,
        mesh=mesh,
        in_specs=(
            P(None, "wide", None, "narrow"),
            P(),
            P(),
            P("wide", None),
            P("wide", None),
            P(None, ("wide", "narrow")),
            P(),
        ),
        out_specs=P(None, ("wide", "narrow"), None, None),
        check_vma=False,
    )
```

```python
import jax
import jax.numpy as jnp
from jax import lax
from jax.experimental import pallas as pl
from jax.experimental.pallas import tpu as pltpu
from jax.sharding import PartitionSpec as P

MIB = 1 << 20
NN = ((1,), (0,))
NT = ((1,), (1,))


def dot_f32(left, right, contract):
    return lax.dot_general(
        left, right, (contract, ((), ())), preferred_element_type=jnp.float32
    )


def params():
    return pltpu.CompilerParams(vmem_limit_bytes=56 * MIB)


def cost(flops, moved):
    return pl.CostEstimate(flops=flops, bytes_accessed=moved, transcendentals=0)


def flatten(ref):
    return ref[...].reshape(-1, ref.shape[-1])


def side_by_side(refs, out_ref):
    height, width = refs[0].shape[1:]
    for slot, ref in enumerate(refs):
        for part in range(ref.shape[0]):
            rows = slice(slot * height, (slot + 1) * height)
            out_ref[rows, part * width : (part + 1) * width] = ref[part]


def forward_step(own_ref, mate_ref, a0_ref, a1_ref, b0_ref, b1_ref, out_ref, rows_ref):
    @pl.when(pl.program_id(0) == 0)
    def _():
        side_by_side((own_ref, mate_ref), rows_ref)

    right = jnp.concatenate([flatten(ref) for ref in (a0_ref, a1_ref, b0_ref, b1_ref)], 0)
    vals = dot_f32(rows_ref[...], right, NT).astype(out_ref.dtype)
    states, _, _, inner, points = out_ref.shape
    vals = vals.reshape(2, states, inner, 2 * points)
    for block in range(2):
        for slot in range(2):
            out_ref[:, block, slot] = vals[slot, :, :, block * points : (block + 1) * points]


def piece_specs(gathered, piece):
    shards, _, _, cols = gathered.shape
    block = (shards, 1, piece, cols)
    return [
        pl.BlockSpec(block, lambda s, *_: (0, 0, 2 * s, 0)),
        pl.BlockSpec(block, lambda s, *_: (0, 1, 2 * s, 0)),
        pl.BlockSpec(block, lambda s, *_: (0, 0, 2 * s + 1, 0)),
        pl.BlockSpec(block, lambda s, *_: (0, 1, 2 * s + 1, 0)),
    ]


def forward_pass(own, mate, gathered, states, piece):
    n_narrow, height, width = own.shape
    shards, sides, _, cols = gathered.shape
    shards = shards * sides
    inner = height // states
    points = shards * piece
    resident = pl.BlockSpec(own.shape, lambda s: (0, 0, 0))
    return pl.pallas_call(
        forward_step,
        grid=(n_narrow // 2,),
        in_specs=[
            resident,
            resident,
            *piece_specs(gathered, piece),
        ],
        out_specs=pl.BlockSpec((states, 2, 2, inner, points), lambda s: (0, s, 0, 0, 0)),
        out_shape=jax.ShapeDtypeStruct((states, n_narrow, 2, inner, points), jnp.bfloat16),
        scratch_shapes=[pltpu.VMEM((2 * height, cols), jnp.bfloat16)],
        compiler_params=params(),
        cost_estimate=cost(4 * height * cols * points * n_narrow, 8 * MIB),
        name="forward_pass",
    )(own, mate, gathered, gathered, gathered, gathered)


def middle_step(
    values_ref, grid_ref, turned_ref, potential_ref, across_ref, out_ref, rows_ref, kept_ref
):
    step = pl.program_id(0)
    half = pl.num_programs(0) // 2
    tile = grid_ref.shape[0]
    points = values_ref.shape[-1]
    width = 2 * points

    @pl.when(step == 0)
    def _():
        rows_ref[:, :, :, :points] = values_ref[:, 0]
        for slot in range(2):
            rows_ref[:, slot, :, points:] = values_ref[:, 1, 1 - slot]

    @pl.when(step < half)
    def _():
        vals = dot_f32(grid_ref[...], rows_ref[...].reshape(-1, width), NN)
        weighted = vals * potential_ref[...].astype(jnp.float32)
        kept_ref[pl.ds(pl.multiple_of(step * tile, tile), tile)] = weighted.astype(jnp.bfloat16)

    @pl.when(step >= half)
    def _():
        out_ref[:, :width] = dot_f32(turned_ref[...], kept_ref[...], NN).astype(out_ref.dtype)
        out_ref[:, width:] = across_ref[...]


def middle_pass(values, grid_one, turned, potential, across, tile=1024):
    n_one, width = across.shape
    half = n_one // tile
    early = lambda s: (jnp.minimum(s, half - 1), 0)
    late = lambda s: (jnp.maximum(s - half, 0), 0)
    groups, _, _, inner, points = values.shape
    return pl.pallas_call(
        middle_step,
        grid=(2 * half,),
        in_specs=[
            pl.BlockSpec(values.shape, lambda s: (0, 0, 0, 0, 0)),
            pl.BlockSpec((tile, n_one), early),
            pl.BlockSpec((tile, n_one), late),
            pl.BlockSpec((tile, width), early),
            pl.BlockSpec((tile, width), late),
        ],
        out_specs=pl.BlockSpec((tile, 2 * width), late),
        out_shape=jax.ShapeDtypeStruct((n_one, 2 * width), jnp.bfloat16),
        scratch_shapes=[
            pltpu.VMEM((groups, 2, inner, 2 * points), jnp.bfloat16),
            pltpu.VMEM((n_one, width), jnp.bfloat16),
        ],
        compiler_params=params(),
        cost_estimate=cost(4 * n_one * n_one * width, 21 * MIB),
        name="middle_pass",
    )(values, grid_one, turned, potential, across)


def applied_step(own_ref, mate_ref, ham_ref, out_ref, sent_ref, rows_ref):
    @pl.when(pl.program_id(0) == 0)
    def _():
        side_by_side((own_ref, mate_ref), rows_ref)

    vals = dot_f32(rows_ref[...], flatten(ham_ref), NT)
    height = out_ref.shape[0]
    out_ref[...] = vals[:height]
    sent_ref[...] = vals[height:].astype(sent_ref.dtype)


def applied_pass(own, mate, gathered, steps=4):
    n_narrow, height, width = own.shape
    shards, sides, depth, cols = gathered.shape
    points = shards * sides * depth
    parts = steps // sides
    resident = pl.BlockSpec(own.shape, lambda s: (0, 0, 0))
    block = pl.BlockSpec((height, points // steps), lambda s: (0, s))
    return pl.pallas_call(
        applied_step,
        grid=(steps,),
        in_specs=[
            resident,
            resident,
            pl.BlockSpec((shards // parts, 1, depth, cols), lambda s: (s % parts, s // parts, 0, 0)),
        ],
        out_specs=[block, block],
        out_shape=[
            jax.ShapeDtypeStruct((height, points), jnp.float32),
            jax.ShapeDtypeStruct((height, points), jnp.bfloat16),
        ],
        scratch_shapes=[pltpu.VMEM((2 * height, cols), jnp.bfloat16)],
        compiler_params=params(),
        cost_estimate=cost(4 * height * cols * points, 8 * MIB),
        name="applied_pass",
    )(own, mate, gathered)


def final_step(
    half_ref, near_ref, far_ref, near_a0, near_a1, near_b0, near_b1, far_a0, far_a1, far_b0,
    far_b1, across_ref, kept_ref, moved_ref, own_ref, energy_ref, swap_ref, out_ref, acc_ref,
):
    step = pl.program_id(0)
    states, _, rows, _ = near_ref.shape
    height = states * rows
    lefts = [ref[:, block].reshape(height, -1) for ref in (near_ref, far_ref) for block in range(2)]
    rights = (near_a0, near_a1, near_b0, near_b1, far_a0, far_a1, far_b0, far_b1)
    rights = [flatten(ref) for ref in rights]
    total = dot_f32(jnp.concatenate(lefts, 1), jnp.concatenate(rights, 0), NN)

    @pl.when(step == 0)
    def _():
        acc_ref[...] = total

    @pl.when(step > 0)
    def _():
        acc_ref[...] += total

    @pl.when(step == pl.num_programs(0) - 1)
    def _():
        even = half_ref[0] == 0
        blocks, _, width = own_ref.shape
        part = width // 2
        for block in range(blocks):
            cols = slice(block * width, (block + 1) * width)
            kept = kept_ref[:, block * part : (block + 1) * part]
            moved = moved_ref[:, block * part : (block + 1) * part].astype(jnp.float32)
            applied = [jnp.where(even, kept, moved), jnp.where(even, moved, kept)]
            value = acc_ref[:, cols] + jnp.concatenate(applied, 1)
            value += across_ref[:, block].reshape(height, width).astype(jnp.float32)
            value += energy_ref[...] * own_ref[block].astype(jnp.float32)
            swapped = dot_f32(swap_ref[...], value.astype(jnp.bfloat16), NN)
            out_ref[:, :, cols] = swapped.astype(out_ref.dtype).reshape(rows, states, width)


def final_pass(half, received, near, far, kept, moved, own, energy, swap, piece):
    states, blocks, rows, double = received.shape
    width = double // 2
    height = states * rows
    shards, sides, _, cols = near.shape
    points = shards * sides * piece
    whole = lambda array: pl.BlockSpec(array.shape, lambda s, h: (0,) * array.ndim)
    return pl.pallas_call(
        final_step,
        grid_spec=pltpu.PrefetchScalarGridSpec(
            num_scalar_prefetch=1,
            grid=(blocks // 2,),
            in_specs=[
                pl.BlockSpec((states, 2, rows, points), lambda s, h: (0, s, 0, h[0])),
                pl.BlockSpec((states, 2, rows, points), lambda s, h: (0, s, 0, 1 - h[0])),
                *piece_specs(near, piece),
                *piece_specs(far, piece),
                pl.BlockSpec((states, blocks, rows, width), lambda s, h: (0, 0, 0, 1)),
                whole(kept),
                whole(moved),
                whole(own),
                whole(energy),
                whole(swap),
            ],
            out_specs=pl.BlockSpec((rows, states, cols), lambda s, h: (0, 0, 0)),
            scratch_shapes=[pltpu.VMEM((height, cols), jnp.float32)],
        ),
        out_shape=jax.ShapeDtypeStruct((rows, states, cols), jnp.bfloat16),
        compiler_params=params(),
        cost_estimate=cost(2 * height * cols * (cols + height), 14 * MIB),
        name="final_pass",
    )(
        half, received, received, *[near] * 4, *[far] * 4, received, kept, moved, own, energy, swap
    )


def on_device(coeffs, ham_one, grid_one, ham_two, grid_two, pair_potential, third_energy):
    n_wide = lax.axis_size("wide")
    n_narrow = lax.axis_size("narrow")
    both = ("wide", "narrow")
    half = lax.axis_index("narrow") % 2
    core = lax.axis_index("wide") % 2
    narrow_pairs = [(n, n ^ 1) for n in range(n_narrow)]
    wide_pairs = [(w, w ^ 1) for w in range(n_wide)]

    local = coeffs[0]
    rows, states, width = local.shape
    n_one, count = pair_potential.shape
    cols = grid_two.shape[1]
    inner = rows // n_narrow
    height = inner * states
    piece = count // 2
    share = rows // 2
    assert states == n_wide and inner == count and n_wide * count == width

    groups = n_wide // 2
    side = lax.axis_index("wide") // groups
    across_y = [(w, (w + groups) % n_wide) for w in range(n_wide)]
    members = [list(range(groups)), list(range(groups, n_wide))]

    def both_sides(mine, theirs):
        return jnp.where(side == 0, jnp.stack([mine, theirs]), jnp.stack([theirs, mine]))

    def gather(value):
        return lax.all_gather(value, "wide", axis=0, tiled=False, axis_index_groups=members)

    pieces = grid_two.reshape(n_narrow, 2, piece, cols)
    near = lax.dynamic_index_in_dim(pieces, half, 1, False).reshape(share, cols)
    near = jnp.concatenate([near, pair_potential.T.astype(jnp.bfloat16)], 0)
    near = gather(both_sides(near, lax.ppermute(near, "wide", across_y)))

    far = lax.dynamic_index_in_dim(pieces, 1 - half, 1, False).reshape(share, cols)
    away = lax.dynamic_slice_in_dim(ham_two, (1 - core) * share, share, 0)
    stay = lax.dynamic_slice_in_dim(ham_two, core * share, share, 0)
    stay = jnp.where(core == half, stay, lax.ppermute(away, "wide", wide_pairs))

    own = local.reshape(n_narrow, inner, states, width).swapaxes(1, 2)
    own = lax.all_to_all(own.reshape(n_narrow, height, width), "narrow", 0, 0, tiled=True)
    own, stay = lax.optimization_barrier((own, stay))
    half_ham = lax.all_gather(stay, "wide", axis=0, tiled=False)[:, None]
    theirs = lax.ppermute(far, "wide", across_y)
    mate = lax.ppermute(own, "narrow", narrow_pairs)
    by_state = lax.all_to_all(jnp.swapaxes(local, 0, 1), "wide", 0, 0, tiled=True)

    turned = lax.optimization_barrier(grid_one.T)
    values = forward_pass(own, mate, near, states, piece)
    values, by_state, turned = lax.optimization_barrier((values, by_state, turned))
    by_state, theirs = lax.optimization_barrier((by_state, theirs))
    far = gather(both_sides(far, theirs))
    across = dot_f32(ham_one, by_state.reshape(n_one, width), NN).astype(jnp.bfloat16)
    values = lax.all_to_all(
        values.reshape(n_wide * n_narrow, 2 * inner, width // 2), both, 0, 0, tiled=True
    )
    values = values.reshape(n_wide * n_narrow // 2, 2, 2, inner, width // 2)
    potential = near[:, :, share:].reshape(groups, 2, 2, piece, n_one).transpose(2, 1, 0, 3, 4)
    potential = potential.reshape(width, n_one).T
    pair = middle_pass(values, grid_one, turned, potential, across)
    pair = lax.all_to_all(
        pair.reshape(n_wide * n_narrow, inner, 2 * width), both, 0, 0, tiled=True
    )

    kept, moved = applied_pass(own, mate, half_ham)
    moved = lax.ppermute(moved, "narrow", narrow_pairs)
    energy = jnp.repeat(third_energy, inner)[:, None]
    target = jnp.arange(height)
    source = target % states * inner + target // states
    swap = (source[:, None] == jnp.arange(height)[None, :]).astype(jnp.bfloat16)
    out = final_pass(
        half[None],
        pair.reshape(n_wide, n_narrow, inner, 2 * width),
        near, far, kept, moved, own, energy, swap, piece,
    )
    return out[None]


def solution(mesh):
    return jax.shard_map(
        on_device,
        mesh=mesh,
        in_specs=(
            P(None, "wide", None, "narrow"),
            P(),
            P(),
            P("wide", None),
            P("wide", None),
            P(None, ("wide", "narrow")),
            P(),
        ),
        out_specs=P(None, ("wide", "narrow"), None, None),
        check_vma=False,
    )
```

```python
import jax
import jax.numpy as jnp
from jax import lax
from jax.experimental import pallas as pl
from jax.experimental.pallas import tpu as pltpu
from jax.sharding import PartitionSpec as P

MIB = 1 << 20
NN = ((1,), (0,))
NT = ((1,), (1,))


def dot_f32(left, right, contract):
    return lax.dot_general(
        left, right, (contract, ((), ())), preferred_element_type=jnp.float32
    )


def params(mib):
    return pltpu.CompilerParams(vmem_limit_bytes=mib * MIB)


def cost(flops, moved):
    return pl.CostEstimate(flops=flops, bytes_accessed=moved, transcendentals=0)


def flatten(ref):
    return ref[...].reshape(-1, ref.shape[-1])


def side_by_side(refs, out_ref):
    height, width = refs[0].shape[1:]
    for slot, ref in enumerate(refs):
        for part in range(ref.shape[0]):
            rows = slice(slot * height, (slot + 1) * height)
            out_ref[rows, part * width : (part + 1) * width] = ref[part]


def forward_step(own_ref, mate_ref, a0_ref, a1_ref, b0_ref, b1_ref, out_ref, rows_ref):
    @pl.when(pl.program_id(0) == 0)
    def _():
        side_by_side((own_ref, mate_ref), rows_ref)

    right = jnp.concatenate([flatten(ref) for ref in (a0_ref, a1_ref, b0_ref, b1_ref)], 0)
    vals = dot_f32(rows_ref[...], right, NT).astype(out_ref.dtype)
    states, _, _, inner, points = out_ref.shape
    vals = vals.reshape(2, states, inner, 2 * points)
    for block in range(2):
        for slot in range(2):
            out_ref[:, block, slot] = vals[slot, :, :, block * points : (block + 1) * points]


def piece_specs(gathered, piece):
    shards, _, _, cols = gathered.shape
    block = (shards, 1, piece, cols)
    return [
        pl.BlockSpec(block, lambda s, *_: (0, 0, 2 * s, 0)),
        pl.BlockSpec(block, lambda s, *_: (0, 1, 2 * s, 0)),
        pl.BlockSpec(block, lambda s, *_: (0, 0, 2 * s + 1, 0)),
        pl.BlockSpec(block, lambda s, *_: (0, 1, 2 * s + 1, 0)),
    ]


def forward_pass(own, mate, gathered, states, piece):
    n_narrow, height, width = own.shape
    shards, sides, _, cols = gathered.shape
    shards = shards * sides
    inner = height // states
    points = shards * piece
    resident = pl.BlockSpec(own.shape, lambda s: (0, 0, 0))
    return pl.pallas_call(
        forward_step,
        grid=(n_narrow // 2,),
        in_specs=[
            resident,
            resident,
            *piece_specs(gathered, piece),
        ],
        out_specs=pl.BlockSpec((states, 2, 2, inner, points), lambda s: (0, s, 0, 0, 0)),
        out_shape=jax.ShapeDtypeStruct((states, n_narrow, 2, inner, points), jnp.bfloat16),
        scratch_shapes=[pltpu.VMEM((2 * height, cols), jnp.bfloat16)],
        compiler_params=params(50),
        cost_estimate=cost(4 * height * cols * points * n_narrow, 8 * MIB),
        name="forward_pass",
    )(own, mate, gathered, gathered, gathered, gathered)


def middle_step(
    values_ref, grid_ref, turned_ref, potential_ref, across_ref, out_ref, rows_ref, kept_ref
):
    step = pl.program_id(0)
    half = pl.num_programs(0) // 2
    tile = grid_ref.shape[0]
    points = values_ref.shape[-1]
    width = 2 * points

    @pl.when(step == 0)
    def _():
        rows_ref[:, :, :, :points] = values_ref[:, 0]
        for slot in range(2):
            rows_ref[:, slot, :, points:] = values_ref[:, 1, 1 - slot]

    @pl.when(step < half)
    def _():
        vals = dot_f32(grid_ref[...], rows_ref[...].reshape(-1, width), NN)
        weighted = vals * potential_ref[...].astype(jnp.float32)
        kept_ref[pl.ds(pl.multiple_of(step * tile, tile), tile)] = weighted.astype(jnp.bfloat16)

    @pl.when(step >= half)
    def _():
        out_ref[:, :width] = dot_f32(turned_ref[...], kept_ref[...], NN).astype(out_ref.dtype)
        out_ref[:, width:] = across_ref[...]


def middle_pass(values, grid_one, turned, potential, across, tile=1024):
    n_one, width = across.shape
    half = n_one // tile
    early = lambda s: (jnp.minimum(s, half - 1), 0)
    late = lambda s: (jnp.maximum(s - half, 0), 0)
    groups, _, _, inner, points = values.shape
    return pl.pallas_call(
        middle_step,
        grid=(2 * half,),
        in_specs=[
            pl.BlockSpec(values.shape, lambda s: (0, 0, 0, 0, 0)),
            pl.BlockSpec((tile, n_one), early),
            pl.BlockSpec((tile, n_one), late),
            pl.BlockSpec((tile, width), early),
            pl.BlockSpec((tile, width), late),
        ],
        out_specs=pl.BlockSpec((tile, 2 * width), late),
        out_shape=jax.ShapeDtypeStruct((n_one, 2 * width), jnp.bfloat16),
        scratch_shapes=[
            pltpu.VMEM((groups, 2, inner, 2 * points), jnp.bfloat16),
            pltpu.VMEM((n_one, width), jnp.bfloat16),
        ],
        compiler_params=params(52),
        cost_estimate=cost(4 * n_one * n_one * width, 21 * MIB),
        name="middle_pass",
    )(values, grid_one, turned, potential, across)


def applied_step(own_ref, mate_ref, ham_ref, out_ref, sent_ref, rows_ref):
    @pl.when(pl.program_id(0) == 0)
    def _():
        side_by_side((own_ref, mate_ref), rows_ref)

    vals = dot_f32(rows_ref[...], flatten(ham_ref), NT)
    height = out_ref.shape[0]
    out_ref[...] = vals[:height]
    sent_ref[...] = vals[height:].astype(sent_ref.dtype)


def applied_pass(own, mate, gathered, steps=4):
    n_narrow, height, width = own.shape
    shards, sides, depth, cols = gathered.shape
    points = shards * sides * depth
    parts = steps // sides
    resident = pl.BlockSpec(own.shape, lambda s: (0, 0, 0))
    block = pl.BlockSpec((height, points // steps), lambda s: (0, s))
    return pl.pallas_call(
        applied_step,
        grid=(steps,),
        in_specs=[
            resident,
            resident,
            pl.BlockSpec((shards // parts, 1, depth, cols), lambda s: (s % parts, s // parts, 0, 0)),
        ],
        out_specs=[block, block],
        out_shape=[
            jax.ShapeDtypeStruct((height, points), jnp.float32),
            jax.ShapeDtypeStruct((height, points), jnp.bfloat16),
        ],
        scratch_shapes=[pltpu.VMEM((2 * height, cols), jnp.bfloat16)],
        compiler_params=params(50),
        cost_estimate=cost(4 * height * cols * points, 8 * MIB),
        name="applied_pass",
    )(own, mate, gathered)


def final_step(
    half_ref, near_ref, far_ref, near_a0, near_a1, near_b0, near_b1, far_a0, far_a1, far_b0,
    far_b1, across_ref, kept_ref, moved_ref, own_ref, energy_ref, swap_ref, out_ref, acc_ref,
):
    step = pl.program_id(0)
    states, _, rows, _ = near_ref.shape
    height = states * rows
    lefts = [ref[:, block].reshape(height, -1) for ref in (near_ref, far_ref) for block in range(2)]
    rights = (near_a0, near_a1, near_b0, near_b1, far_a0, far_a1, far_b0, far_b1)
    rights = [flatten(ref) for ref in rights]
    total = dot_f32(jnp.concatenate(lefts, 1), jnp.concatenate(rights, 0), NN)

    @pl.when(step == 0)
    def _():
        acc_ref[...] = total

    @pl.when(step > 0)
    def _():
        acc_ref[...] += total

    @pl.when(step == pl.num_programs(0) - 1)
    def _():
        even = half_ref[0] == 0
        blocks, _, width = own_ref.shape
        part = width // 2
        for block in range(blocks):
            cols = slice(block * width, (block + 1) * width)
            kept = kept_ref[:, block * part : (block + 1) * part]
            moved = moved_ref[:, block * part : (block + 1) * part].astype(jnp.float32)
            low = jnp.where(even, kept, moved)
            high = jnp.where(even, moved, kept)
            left = lax.broadcasted_iota(jnp.int32, low.shape, 1) < part // 2
            applied = [
                jnp.where(left, low, pltpu.roll(high, part // 2, 1)),
                jnp.where(left, pltpu.roll(low, part // 2, 1), high),
            ]
            value = acc_ref[:, cols] + jnp.concatenate(applied, 1)
            value += across_ref[:, block].reshape(height, width).astype(jnp.float32)
            value += energy_ref[...] * own_ref[block].astype(jnp.float32)
            swapped = dot_f32(swap_ref[...], value.astype(jnp.bfloat16), NN)
            out_ref[:, :, cols] = swapped.astype(out_ref.dtype).reshape(rows, states, width)


def final_pass(half, received, near, far, kept, moved, own, energy, swap, piece):
    states, blocks, rows, double = received.shape
    width = double // 2
    height = states * rows
    shards, sides, _, cols = near.shape
    points = shards * sides * piece
    whole = lambda array: pl.BlockSpec(array.shape, lambda s, h: (0,) * array.ndim)
    return pl.pallas_call(
        final_step,
        grid_spec=pltpu.PrefetchScalarGridSpec(
            num_scalar_prefetch=1,
            grid=(blocks // 2,),
            in_specs=[
                pl.BlockSpec((states, 2, rows, points), lambda s, h: (0, s, 0, h[0])),
                pl.BlockSpec((states, 2, rows, points), lambda s, h: (0, s, 0, 1 - h[0])),
                *piece_specs(near, piece),
                *piece_specs(far, piece),
                pl.BlockSpec((states, blocks, rows, width), lambda s, h: (0, 0, 0, 1)),
                whole(kept),
                whole(moved),
                whole(own),
                whole(energy),
                whole(swap),
            ],
            out_specs=pl.BlockSpec((rows, states, cols), lambda s, h: (0, 0, 0)),
            scratch_shapes=[pltpu.VMEM((height, cols), jnp.float32)],
        ),
        out_shape=jax.ShapeDtypeStruct((rows, states, cols), jnp.bfloat16),
        compiler_params=params(50),
        cost_estimate=cost(2 * height * cols * (cols + height), 14 * MIB),
        name="final_pass",
    )(
        half, received, received, *[near] * 4, *[far] * 4, received, kept, moved, own, energy, swap
    )


def on_device(coeffs, ham_one, grid_one, ham_two, grid_two, pair_potential, third_energy):
    n_wide = lax.axis_size("wide")
    n_narrow = lax.axis_size("narrow")
    both = ("wide", "narrow")
    half = lax.axis_index("narrow") % 2
    narrow_pairs = [(n, n ^ 1) for n in range(n_narrow)]

    local = coeffs[0]
    rows, states, width = local.shape
    n_one, count = pair_potential.shape
    cols = grid_two.shape[1]
    inner = rows // n_narrow
    height = inner * states
    piece = count // 2
    share = rows // 2
    assert states == n_wide and inner == count and n_wide * count == width

    groups = n_wide // 2
    side = lax.axis_index("wide") // groups
    across_y = [(w, (w + groups) % n_wide) for w in range(n_wide)]
    members = [list(range(groups)), list(range(groups, n_wide))]

    def both_sides(mine, theirs):
        return jnp.where(side == 0, jnp.stack([mine, theirs]), jnp.stack([theirs, mine]))

    def gather(value):
        return lax.all_gather(value, "wide", axis=0, tiled=False, axis_index_groups=members)

    pieces = grid_two.reshape(n_narrow, 2, piece, cols)
    near = lax.dynamic_index_in_dim(pieces, half, 1, False).reshape(share, cols)
    near = jnp.concatenate([near, pair_potential.T.astype(jnp.bfloat16)], 0)
    near = gather(both_sides(near, lax.ppermute(near, "wide", across_y)))

    far = lax.dynamic_index_in_dim(pieces, 1 - half, 1, False).reshape(share, cols)
    stay = lax.dynamic_slice_in_dim(ham_two, half * share, share, 0)

    own = local.reshape(n_narrow, inner, states, width).swapaxes(1, 2)
    own = lax.all_to_all(own.reshape(n_narrow, height, width), "narrow", 0, 0, tiled=True)
    mine = jnp.stack([stay, far])
    theirs = lax.ppermute(mine, "wide", across_y)
    own, theirs, mine = lax.optimization_barrier((own, theirs, mine))
    joined = both_sides(mine, theirs)
    stay, far = joined[:, 0], joined[:, 1]
    half_ham = gather(stay)
    far = gather(far)
    mate = lax.ppermute(own, "narrow", narrow_pairs)
    by_state = lax.all_to_all(jnp.swapaxes(local, 0, 1), "wide", 0, 0, tiled=True)

    turned = lax.optimization_barrier(grid_one.T)
    values = forward_pass(own, mate, near, states, piece)
    values, by_state, turned = lax.optimization_barrier((values, by_state, turned))
    across = dot_f32(ham_one, by_state.reshape(n_one, width), NN).astype(jnp.bfloat16)
    values = lax.all_to_all(
        values.reshape(n_wide * n_narrow, 2 * inner, width // 2), both, 0, 0, tiled=True
    )
    values = values.reshape(n_wide * n_narrow // 2, 2, 2, inner, width // 2)
    potential = near[:, :, share:].reshape(groups, 2, 2, piece, n_one).transpose(2, 1, 0, 3, 4)
    potential = potential.reshape(width, n_one).T
    pair = middle_pass(values, grid_one, turned, potential, across)
    pair = lax.all_to_all(
        pair.reshape(n_wide * n_narrow, inner, 2 * width), both, 0, 0, tiled=True
    )

    kept, moved = applied_pass(own, mate, half_ham)
    moved = lax.ppermute(moved, "narrow", narrow_pairs)
    energy = jnp.repeat(third_energy, inner)[:, None]
    target = jnp.arange(height)
    source = target % states * inner + target // states
    swap = (source[:, None] == jnp.arange(height)[None, :]).astype(jnp.bfloat16)
    out = final_pass(
        half[None],
        pair.reshape(n_wide, n_narrow, inner, 2 * width),
        near, far, kept, moved, own, energy, swap, piece,
    )
    return out[None]


def solution(mesh):
    return jax.shard_map(
        on_device,
        mesh=mesh,
        in_specs=(
            P(None, "wide", None, "narrow"),
            P(),
            P(),
            P("wide", None),
            P("wide", None),
            P(None, ("wide", "narrow")),
            P(),
        ),
        out_specs=P(None, ("wide", "narrow"), None, None),
        check_vma=False,
    )
```

```python
import jax
import jax.numpy as jnp
from jax import lax
from jax.experimental import pallas as pl
from jax.experimental.pallas import tpu as pltpu
from jax.sharding import PartitionSpec as P

MIB = 1 << 20
NN = ((1,), (0,))
NT = ((1,), (1,))


def dot_f32(left, right, contract):
    return lax.dot_general(
        left, right, (contract, ((), ())), preferred_element_type=jnp.float32
    )


def params(mib):
    return pltpu.CompilerParams(vmem_limit_bytes=mib * MIB)


def cost(flops, moved):
    return pl.CostEstimate(flops=flops, bytes_accessed=moved, transcendentals=0)


def flatten(ref):
    return ref[...].reshape(-1, ref.shape[-1])


def side_by_side(refs, out_ref):
    height, width = refs[0].shape[1:]
    for slot, ref in enumerate(refs):
        for part in range(ref.shape[0]):
            rows = slice(slot * height, (slot + 1) * height)
            out_ref[rows, part * width : (part + 1) * width] = ref[part]


def forward_step(own_ref, mate_ref, a0_ref, a1_ref, b0_ref, b1_ref, out_ref, rows_ref):
    @pl.when(pl.program_id(0) == 0)
    def _():
        side_by_side((own_ref, mate_ref), rows_ref)

    right = jnp.concatenate([flatten(ref) for ref in (a0_ref, a1_ref, b0_ref, b1_ref)], 0)
    vals = dot_f32(rows_ref[...], right, NT).astype(out_ref.dtype)
    states, _, _, inner, points = out_ref.shape
    vals = vals.reshape(2, states, inner, 2 * points)
    for block in range(2):
        for slot in range(2):
            out_ref[:, block, slot] = vals[slot, :, :, block * points : (block + 1) * points]


def piece_specs(gathered, piece, first=0):
    shards, _, _, cols = gathered.shape
    block = (shards, 1, piece, cols)
    return [
        pl.BlockSpec(block, lambda s, *_: (0, 0, first + 2 * s, 0)),
        pl.BlockSpec(block, lambda s, *_: (0, 1, first + 2 * s, 0)),
        pl.BlockSpec(block, lambda s, *_: (0, 0, first + 2 * s + 1, 0)),
        pl.BlockSpec(block, lambda s, *_: (0, 1, first + 2 * s + 1, 0)),
    ]


def forward_pass(own, mate, gathered, states, piece):
    n_narrow, height, width = own.shape
    shards, sides, _, cols = gathered.shape
    shards = shards * sides
    inner = height // states
    points = shards * piece
    resident = pl.BlockSpec(own.shape, lambda s: (0, 0, 0))
    return pl.pallas_call(
        forward_step,
        grid=(n_narrow // 2,),
        in_specs=[
            resident,
            resident,
            *piece_specs(gathered, piece),
        ],
        out_specs=pl.BlockSpec((states, 2, 2, inner, points), lambda s: (0, s, 0, 0, 0)),
        out_shape=jax.ShapeDtypeStruct((states, n_narrow, 2, inner, points), jnp.bfloat16),
        scratch_shapes=[pltpu.VMEM((2 * height, cols), jnp.bfloat16)],
        compiler_params=params(50),
        cost_estimate=cost(4 * height * cols * points * n_narrow, 8 * MIB),
        name="forward_pass",
    )(own, mate, gathered, gathered, gathered, gathered)


def middle_step(
    values_ref, grid_ref, turned_ref, potential_ref, across_ref, out_ref, rows_ref, kept_ref
):
    step = pl.program_id(0)
    half = pl.num_programs(0) // 2
    tile = grid_ref.shape[0]
    points = values_ref.shape[-1]
    width = 2 * points

    @pl.when(step == 0)
    def _():
        rows_ref[:, :, :, :points] = values_ref[:, 0]
        for slot in range(2):
            rows_ref[:, slot, :, points:] = values_ref[:, 1, 1 - slot]

    @pl.when(step < half)
    def _():
        vals = dot_f32(grid_ref[...], rows_ref[...].reshape(-1, width), NN)
        weighted = vals * potential_ref[...].astype(jnp.float32)
        kept_ref[pl.ds(pl.multiple_of(step * tile, tile), tile)] = weighted.astype(jnp.bfloat16)

    @pl.when(step >= half)
    def _():
        out_ref[:, :width] = dot_f32(turned_ref[...], kept_ref[...], NN).astype(out_ref.dtype)
        out_ref[:, width:] = across_ref[...]


def middle_pass(values, grid_one, turned, potential, across, tile=1024):
    n_one, width = across.shape
    half = n_one // tile
    early = lambda s: (jnp.minimum(s, half - 1), 0)
    late = lambda s: (jnp.maximum(s - half, 0), 0)
    groups, _, _, inner, points = values.shape
    return pl.pallas_call(
        middle_step,
        grid=(2 * half,),
        in_specs=[
            pl.BlockSpec(values.shape, lambda s: (0, 0, 0, 0, 0)),
            pl.BlockSpec((tile, n_one), early),
            pl.BlockSpec((tile, n_one), late),
            pl.BlockSpec((tile, width), early),
            pl.BlockSpec((tile, width), late),
        ],
        out_specs=pl.BlockSpec((tile, 2 * width), late),
        out_shape=jax.ShapeDtypeStruct((n_one, 2 * width), jnp.bfloat16),
        scratch_shapes=[
            pltpu.VMEM((groups, 2, inner, 2 * points), jnp.bfloat16),
            pltpu.VMEM((n_one, width), jnp.bfloat16),
        ],
        compiler_params=params(52),
        cost_estimate=cost(4 * n_one * n_one * width, 21 * MIB),
        name="middle_pass",
    )(values, grid_one, turned, potential, across)


def applied_step(own_ref, mate_ref, ham_ref, out_ref, sent_ref, rows_ref):
    @pl.when(pl.program_id(0) == 0)
    def _():
        side_by_side((own_ref, mate_ref), rows_ref)

    vals = dot_f32(rows_ref[...], flatten(ham_ref), NT)
    height = out_ref.shape[0]
    out_ref[...] = vals[:height]
    sent_ref[...] = vals[height:].astype(sent_ref.dtype)


def applied_pass(own, mate, gathered, steps=4):
    n_narrow, height, width = own.shape
    shards, sides, depth, cols = gathered.shape
    depth = depth // 2
    points = shards * sides * depth
    parts = steps // sides
    resident = pl.BlockSpec(own.shape, lambda s: (0, 0, 0))
    block = pl.BlockSpec((height, points // steps), lambda s: (0, s))
    return pl.pallas_call(
        applied_step,
        grid=(steps,),
        in_specs=[
            resident,
            resident,
            pl.BlockSpec((shards // parts, 1, depth, cols), lambda s: (s % parts, s // parts, 0, 0)),
        ],
        out_specs=[block, block],
        out_shape=[
            jax.ShapeDtypeStruct((height, points), jnp.float32),
            jax.ShapeDtypeStruct((height, points), jnp.bfloat16),
        ],
        scratch_shapes=[pltpu.VMEM((2 * height, cols), jnp.bfloat16)],
        compiler_params=params(50),
        cost_estimate=cost(4 * height * cols * points, 8 * MIB),
        name="applied_pass",
    )(own, mate, gathered)


def final_step(
    half_ref, near_ref, far_ref, near_a0, near_a1, near_b0, near_b1, far_a0, far_a1, far_b0,
    far_b1, across_ref, kept_ref, moved_ref, own_ref, energy_ref, swap_ref, out_ref, acc_ref,
):
    step = pl.program_id(0)
    states, _, rows, _ = near_ref.shape
    height = states * rows
    lefts = [ref[:, block].reshape(height, -1) for ref in (near_ref, far_ref) for block in range(2)]
    rights = (near_a0, near_a1, near_b0, near_b1, far_a0, far_a1, far_b0, far_b1)
    rights = [flatten(ref) for ref in rights]
    total = dot_f32(jnp.concatenate(lefts, 1), jnp.concatenate(rights, 0), NN)

    @pl.when(step == 0)
    def _():
        acc_ref[...] = total

    @pl.when(step > 0)
    def _():
        acc_ref[...] += total

    @pl.when(step == pl.num_programs(0) - 1)
    def _():
        even = half_ref[0] == 0
        blocks, _, width = own_ref.shape
        part = width // 2
        for block in range(blocks):
            cols = slice(block * width, (block + 1) * width)
            kept = kept_ref[:, block * part : (block + 1) * part]
            moved = moved_ref[:, block * part : (block + 1) * part].astype(jnp.float32)
            low = jnp.where(even, kept, moved)
            high = jnp.where(even, moved, kept)
            left = lax.broadcasted_iota(jnp.int32, low.shape, 1) < part // 2
            applied = [
                jnp.where(left, low, pltpu.roll(high, part // 2, 1)),
                jnp.where(left, pltpu.roll(low, part // 2, 1), high),
            ]
            value = acc_ref[:, cols] + jnp.concatenate(applied, 1)
            value += across_ref[:, block].reshape(height, width).astype(jnp.float32)
            value += energy_ref[...] * own_ref[block].astype(jnp.float32)
            swapped = dot_f32(swap_ref[...], value.astype(jnp.bfloat16), NN)
            out_ref[:, :, cols] = swapped.astype(out_ref.dtype).reshape(rows, states, width)


def final_pass(half, received, near, far, kept, moved, own, energy, swap, piece):
    states, blocks, rows, double = received.shape
    width = double // 2
    height = states * rows
    shards, sides, _, cols = near.shape
    points = shards * sides * piece
    whole = lambda array: pl.BlockSpec(array.shape, lambda s, h: (0,) * array.ndim)
    return pl.pallas_call(
        final_step,
        grid_spec=pltpu.PrefetchScalarGridSpec(
            num_scalar_prefetch=1,
            grid=(blocks // 2,),
            in_specs=[
                pl.BlockSpec((states, 2, rows, points), lambda s, h: (0, s, 0, h[0])),
                pl.BlockSpec((states, 2, rows, points), lambda s, h: (0, s, 0, 1 - h[0])),
                *piece_specs(near, piece),
                *piece_specs(far, piece, blocks),
                pl.BlockSpec((states, blocks, rows, width), lambda s, h: (0, 0, 0, 1)),
                whole(kept),
                whole(moved),
                whole(own),
                whole(energy),
                whole(swap),
            ],
            out_specs=pl.BlockSpec((rows, states, cols), lambda s, h: (0, 0, 0)),
            scratch_shapes=[pltpu.VMEM((height, cols), jnp.float32)],
        ),
        out_shape=jax.ShapeDtypeStruct((rows, states, cols), jnp.bfloat16),
        compiler_params=params(50),
        cost_estimate=cost(2 * height * cols * (cols + height), 14 * MIB),
        name="final_pass",
    )(
        half, received, received, *[near] * 4, *[far] * 4, received, kept, moved, own, energy, swap
    )


def on_device(coeffs, ham_one, grid_one, ham_two, grid_two, pair_potential, third_energy):
    n_wide = lax.axis_size("wide")
    n_narrow = lax.axis_size("narrow")
    both = ("wide", "narrow")
    half = lax.axis_index("narrow") % 2
    narrow_pairs = [(n, n ^ 1) for n in range(n_narrow)]

    local = coeffs[0]
    rows, states, width = local.shape
    n_one, count = pair_potential.shape
    cols = grid_two.shape[1]
    inner = rows // n_narrow
    height = inner * states
    piece = count // 2
    share = rows // 2
    assert states == n_wide and inner == count and n_wide * count == width

    groups = n_wide // 2
    side = lax.axis_index("wide") // groups
    across_y = [(w, (w + groups) % n_wide) for w in range(n_wide)]
    members = [list(range(groups)), list(range(groups, n_wide))]

    def both_sides(mine, theirs):
        return jnp.where(side == 0, jnp.stack([mine, theirs]), jnp.stack([theirs, mine]))

    def gather(value):
        return lax.all_gather(value, "wide", axis=0, tiled=False, axis_index_groups=members)

    pieces = grid_two.reshape(n_narrow, 2, piece, cols)
    near = lax.dynamic_index_in_dim(pieces, half, 1, False).reshape(share, cols)
    near = jnp.concatenate([near, pair_potential.T.astype(jnp.bfloat16)], 0)
    near = gather(both_sides(near, lax.ppermute(near, "wide", across_y)))

    far = lax.dynamic_index_in_dim(pieces, 1 - half, 1, False).reshape(share, cols)
    stay = lax.dynamic_slice_in_dim(ham_two, half * share, share, 0)

    own = local.reshape(n_narrow, inner, states, width).swapaxes(1, 2)
    own = lax.all_to_all(own.reshape(n_narrow, height, width), "narrow", 0, 0, tiled=True)
    mine = jnp.concatenate([stay, far], 0)
    theirs = lax.ppermute(mine, "wide", across_y)
    mate = lax.ppermute(own, "narrow", narrow_pairs)
    by_state = lax.all_to_all(jnp.swapaxes(local, 0, 1), "wide", 0, 0, tiled=True)

    turned = lax.optimization_barrier(grid_one.T)
    values = forward_pass(own, mate, near, states, piece)
    values, by_state, turned = lax.optimization_barrier((values, by_state, turned))
    by_state, theirs, mine = lax.optimization_barrier((by_state, theirs, mine))
    far = gather(both_sides(mine, theirs))
    across = dot_f32(ham_one, by_state.reshape(n_one, width), NN).astype(jnp.bfloat16)
    values = lax.all_to_all(
        values.reshape(n_wide * n_narrow, 2 * inner, width // 2), both, 0, 0, tiled=True
    )
    values = values.reshape(n_wide * n_narrow // 2, 2, 2, inner, width // 2)
    potential = near[:, :, share:].reshape(groups, 2, 2, piece, n_one).transpose(2, 1, 0, 3, 4)
    potential = potential.reshape(width, n_one).T
    pair = middle_pass(values, grid_one, turned, potential, across)
    pair = lax.all_to_all(
        pair.reshape(n_wide * n_narrow, inner, 2 * width), both, 0, 0, tiled=True
    )

    kept, moved = applied_pass(own, mate, far)
    moved = lax.ppermute(moved, "narrow", narrow_pairs)
    energy = jnp.repeat(third_energy, inner)[:, None]
    target = jnp.arange(height)
    source = target % states * inner + target // states
    swap = (source[:, None] == jnp.arange(height)[None, :]).astype(jnp.bfloat16)
    out = final_pass(
        half[None],
        pair.reshape(n_wide, n_narrow, inner, 2 * width),
        near, far, kept, moved, own, energy, swap, piece,
    )
    return out[None]


def solution(mesh):
    return jax.shard_map(
        on_device,
        mesh=mesh,
        in_specs=(
            P(None, "wide", None, "narrow"),
            P(),
            P(),
            P("wide", None),
            P("wide", None),
            P(None, ("wide", "narrow")),
            P(),
        ),
        out_specs=P(None, ("wide", "narrow"), None, None),
        check_vma=False,
    )
```

```python
import jax
import jax.numpy as jnp
from jax import lax
from jax.experimental import pallas as pl
from jax.experimental.pallas import tpu as pltpu
from jax.sharding import PartitionSpec as P

MIB = 1 << 20
NN = ((1,), (0,))
NT = ((1,), (1,))


def dot_f32(left, right, contract):
    return lax.dot_general(
        left, right, (contract, ((), ())), preferred_element_type=jnp.float32
    )


def params(mib):
    return pltpu.CompilerParams(vmem_limit_bytes=mib * MIB)


def cost(flops, moved):
    return pl.CostEstimate(flops=flops, bytes_accessed=moved, transcendentals=0)


def flatten(ref):
    return ref[...].reshape(-1, ref.shape[-1])


def side_by_side(refs, out_ref):
    height, width = refs[0].shape[1:]
    for slot, ref in enumerate(refs):
        for part in range(ref.shape[0]):
            rows = slice(slot * height, (slot + 1) * height)
            out_ref[rows, part * width : (part + 1) * width] = ref[part]


def forward_step(own_ref, mate_ref, a0_ref, a1_ref, b0_ref, b1_ref, out_ref, rows_ref):
    @pl.when(pl.program_id(0) == 0)
    def _():
        side_by_side((own_ref, mate_ref), rows_ref)

    right = jnp.concatenate([flatten(ref) for ref in (a0_ref, a1_ref, b0_ref, b1_ref)], 0)
    vals = dot_f32(rows_ref[...], right, NT).astype(out_ref.dtype)
    states, _, _, inner, points = out_ref.shape
    vals = vals.reshape(2, states, inner, 2 * points)
    for block in range(2):
        for slot in range(2):
            out_ref[:, block, slot] = vals[slot, :, :, block * points : (block + 1) * points]


def piece_specs(gathered, piece):
    shards, _, _, cols = gathered.shape
    block = (shards, 1, piece, cols)
    return [
        pl.BlockSpec(block, lambda s, *_: (0, 0, 2 * s, 0)),
        pl.BlockSpec(block, lambda s, *_: (0, 1, 2 * s, 0)),
        pl.BlockSpec(block, lambda s, *_: (0, 0, 2 * s + 1, 0)),
        pl.BlockSpec(block, lambda s, *_: (0, 1, 2 * s + 1, 0)),
    ]


def forward_pass(own, mate, gathered, states, piece):
    n_narrow, height, width = own.shape
    shards, sides, _, cols = gathered.shape
    shards = shards * sides
    inner = height // states
    points = shards * piece
    resident = pl.BlockSpec(own.shape, lambda s: (0, 0, 0))
    return pl.pallas_call(
        forward_step,
        grid=(n_narrow // 2,),
        in_specs=[
            resident,
            resident,
            *piece_specs(gathered, piece),
        ],
        out_specs=pl.BlockSpec((states, 2, 2, inner, points), lambda s: (0, s, 0, 0, 0)),
        out_shape=jax.ShapeDtypeStruct((states, n_narrow, 2, inner, points), jnp.bfloat16),
        scratch_shapes=[pltpu.VMEM((2 * height, cols), jnp.bfloat16)],
        compiler_params=params(50),
        cost_estimate=cost(4 * height * cols * points * n_narrow, 8 * MIB),
        name="forward_pass",
    )(own, mate, gathered, gathered, gathered, gathered)


def middle_step(
    values_ref, grid_ref, turned_ref, potential_ref, across_ref, out_ref, rows_ref, kept_ref
):
    step = pl.program_id(0)
    half = pl.num_programs(0) // 2
    tile = grid_ref.shape[0]
    points = values_ref.shape[-1]
    width = 2 * points

    @pl.when(step == 0)
    def _():
        rows_ref[:, :, :, :points] = values_ref[:, 0]
        for slot in range(2):
            rows_ref[:, slot, :, points:] = values_ref[:, 1, 1 - slot]

    @pl.when(step < half)
    def _():
        vals = dot_f32(grid_ref[...], rows_ref[...].reshape(-1, width), NN)
        weighted = vals * potential_ref[...].astype(jnp.float32)
        kept_ref[pl.ds(pl.multiple_of(step * tile, tile), tile)] = weighted.astype(jnp.bfloat16)

    @pl.when(step >= half)
    def _():
        out_ref[:, :width] = dot_f32(turned_ref[...], kept_ref[...], NN).astype(out_ref.dtype)
        out_ref[:, width:] = across_ref[...]


def middle_pass(values, grid_one, turned, potential, across, tile=1024):
    n_one, width = across.shape
    half = n_one // tile
    early = lambda s: (jnp.minimum(s, half - 1), 0)
    late = lambda s: (jnp.maximum(s - half, 0), 0)
    groups, _, _, inner, points = values.shape
    return pl.pallas_call(
        middle_step,
        grid=(2 * half,),
        in_specs=[
            pl.BlockSpec(values.shape, lambda s: (0, 0, 0, 0, 0)),
            pl.BlockSpec((tile, n_one), early),
            pl.BlockSpec((tile, n_one), late),
            pl.BlockSpec((tile, width), early),
            pl.BlockSpec((tile, width), late),
        ],
        out_specs=pl.BlockSpec((tile, 2 * width), late),
        out_shape=jax.ShapeDtypeStruct((n_one, 2 * width), jnp.bfloat16),
        scratch_shapes=[
            pltpu.VMEM((groups, 2, inner, 2 * points), jnp.bfloat16),
            pltpu.VMEM((n_one, width), jnp.bfloat16),
        ],
        compiler_params=params(52),
        cost_estimate=cost(4 * n_one * n_one * width, 21 * MIB),
        name="middle_pass",
    )(values, grid_one, turned, potential, across)


def applied_step(own_ref, mate_ref, ham_ref, out_ref, sent_ref, rows_ref):
    @pl.when(pl.program_id(0) == 0)
    def _():
        side_by_side((own_ref, mate_ref), rows_ref)

    vals = dot_f32(rows_ref[...], flatten(ham_ref), NT)
    height = out_ref.shape[0]
    out_ref[...] = vals[:height]
    sent_ref[...] = vals[height:].astype(sent_ref.dtype)


def applied_pass(own, mate, gathered, steps=4):
    n_narrow, height, width = own.shape
    shards, sides, depth, cols = gathered.shape
    points = shards * sides * depth
    parts = steps // sides
    resident = pl.BlockSpec(own.shape, lambda s: (0, 0, 0))
    block = pl.BlockSpec((height, points // steps), lambda s: (0, s))
    return pl.pallas_call(
        applied_step,
        grid=(steps,),
        in_specs=[
            resident,
            resident,
            pl.BlockSpec((shards // parts, 1, depth, cols), lambda s: (s % parts, s // parts, 0, 0)),
        ],
        out_specs=[block, block],
        out_shape=[
            jax.ShapeDtypeStruct((height, points), jnp.float32),
            jax.ShapeDtypeStruct((height, points), jnp.bfloat16),
        ],
        scratch_shapes=[pltpu.VMEM((2 * height, cols), jnp.bfloat16)],
        compiler_params=params(50),
        cost_estimate=cost(4 * height * cols * points, 8 * MIB),
        name="applied_pass",
    )(own, mate, gathered)


def final_step(
    half_ref, near_ref, far_ref, near_a0, near_a1, near_b0, near_b1, far_a0, far_a1, far_b0,
    far_b1, across_ref, kept_ref, moved_ref, own_ref, energy_ref, swap_ref, out_ref, acc_ref,
):
    step = pl.program_id(0)
    states, _, rows, _ = near_ref.shape
    height = states * rows
    lefts = [ref[:, block].reshape(height, -1) for ref in (near_ref, far_ref) for block in range(2)]
    rights = (near_a0, near_a1, near_b0, near_b1, far_a0, far_a1, far_b0, far_b1)
    rights = [flatten(ref) for ref in rights]
    total = dot_f32(jnp.concatenate(lefts, 1), jnp.concatenate(rights, 0), NN)

    @pl.when(step == 0)
    def _():
        acc_ref[...] = total

    @pl.when(step > 0)
    def _():
        acc_ref[...] += total

    @pl.when(step == pl.num_programs(0) - 1)
    def _():
        even = half_ref[0] == 0
        blocks, _, width = own_ref.shape
        part = width // 2
        for block in range(blocks):
            cols = slice(block * width, (block + 1) * width)
            kept = kept_ref[:, block * part : (block + 1) * part]
            moved = moved_ref[:, block * part : (block + 1) * part].astype(jnp.float32)
            low = jnp.where(even, kept, moved)
            high = jnp.where(even, moved, kept)
            left = lax.broadcasted_iota(jnp.int32, low.shape, 1) < part // 2
            applied = [
                jnp.where(left, low, pltpu.roll(high, part // 2, 1)),
                jnp.where(left, pltpu.roll(low, part // 2, 1), high),
            ]
            value = acc_ref[:, cols] + jnp.concatenate(applied, 1)
            value += across_ref[:, block].reshape(height, width).astype(jnp.float32)
            value += energy_ref[...] * own_ref[block].astype(jnp.float32)
            swapped = dot_f32(swap_ref[...], value.astype(jnp.bfloat16), NN)
            out_ref[:, :, cols] = swapped.astype(out_ref.dtype).reshape(rows, states, width)


def final_pass(half, received, near, far, kept, moved, own, energy, swap, piece):
    states, blocks, rows, double = received.shape
    width = double // 2
    height = states * rows
    shards, sides, _, cols = near.shape
    points = shards * sides * piece
    whole = lambda array: pl.BlockSpec(array.shape, lambda s, h: (0,) * array.ndim)
    return pl.pallas_call(
        final_step,
        grid_spec=pltpu.PrefetchScalarGridSpec(
            num_scalar_prefetch=1,
            grid=(blocks // 2,),
            in_specs=[
                pl.BlockSpec((states, 2, rows, points), lambda s, h: (0, s, 0, h[0])),
                pl.BlockSpec((states, 2, rows, points), lambda s, h: (0, s, 0, 1 - h[0])),
                *piece_specs(near, piece),
                *piece_specs(far, piece),
                pl.BlockSpec((states, blocks, rows, width), lambda s, h: (0, 0, 0, 1)),
                whole(kept),
                whole(moved),
                whole(own),
                whole(energy),
                whole(swap),
            ],
            out_specs=pl.BlockSpec((rows, states, cols), lambda s, h: (0, 0, 0)),
            scratch_shapes=[pltpu.VMEM((height, cols), jnp.float32)],
        ),
        out_shape=jax.ShapeDtypeStruct((rows, states, cols), jnp.bfloat16),
        compiler_params=params(50),
        cost_estimate=cost(2 * height * cols * (cols + height), 14 * MIB),
        name="final_pass",
    )(
        half, received, received, *[near] * 4, *[far] * 4, received, kept, moved, own, energy, swap
    )


def on_device(coeffs, ham_one, grid_one, ham_two, grid_two, pair_potential, third_energy):
    n_wide = lax.axis_size("wide")
    n_narrow = lax.axis_size("narrow")
    both = ("wide", "narrow")
    half = lax.axis_index("narrow") % 2
    narrow_pairs = [(n, n ^ 1) for n in range(n_narrow)]

    local = coeffs[0]
    rows, states, width = local.shape
    n_one, count = pair_potential.shape
    cols = grid_two.shape[1]
    inner = rows // n_narrow
    height = inner * states
    piece = count // 2
    share = rows // 2
    assert states == n_wide and inner == count and n_wide * count == width

    groups = n_wide // 2
    side = lax.axis_index("wide") // groups
    across_y = [(w, (w + groups) % n_wide) for w in range(n_wide)]
    members = [list(range(groups)), list(range(groups, n_wide))]

    def both_sides(mine, theirs):
        return jnp.where(side == 0, jnp.stack([mine, theirs]), jnp.stack([theirs, mine]))

    def gather(value):
        return lax.all_gather(value, "wide", axis=0, tiled=False, axis_index_groups=members)

    pieces = grid_two.reshape(n_narrow, 2, piece, cols)
    near = lax.dynamic_index_in_dim(pieces, half, 1, False).reshape(share, cols)
    near = jnp.concatenate([near, pair_potential.T.astype(jnp.bfloat16)], 0)
    near = gather(both_sides(near, lax.ppermute(near, "wide", across_y)))

    far = lax.dynamic_index_in_dim(pieces, 1 - half, 1, False).reshape(share, cols)
    stay = lax.dynamic_slice_in_dim(ham_two, half * share, share, 0)

    own = local.reshape(n_narrow, inner, states, width).swapaxes(1, 2)
    own = lax.all_to_all(own.reshape(n_narrow, height, width), "narrow", 0, 0, tiled=True)
    other_stay = lax.ppermute(stay, "wide", across_y)
    own, other_stay = lax.optimization_barrier((own, other_stay))
    half_ham = gather(both_sides(stay, other_stay))
    other_far = lax.ppermute(far, "wide", across_y)
    mate = lax.ppermute(own, "narrow", narrow_pairs)
    by_state = lax.all_to_all(jnp.swapaxes(local, 0, 1), "wide", 0, 0, tiled=True)

    turned = lax.optimization_barrier(grid_one.T)
    values = forward_pass(own, mate, near, states, piece)
    values, by_state, turned = lax.optimization_barrier((values, by_state, turned))
    by_state, other_far = lax.optimization_barrier((by_state, other_far))
    far = gather(both_sides(far, other_far))
    across = dot_f32(ham_one, by_state.reshape(n_one, width), NN).astype(jnp.bfloat16)
    values = lax.all_to_all(
        values.reshape(n_wide * n_narrow, 2 * inner, width // 2), both, 0, 0, tiled=True
    )
    values = values.reshape(n_wide * n_narrow // 2, 2, 2, inner, width // 2)
    potential = near[:, :, share:].reshape(groups, 2, 2, piece, n_one).transpose(2, 1, 0, 3, 4)
    potential = potential.reshape(width, n_one).T
    pair = middle_pass(values, grid_one, turned, potential, across)
    pair = lax.all_to_all(
        pair.reshape(n_wide * n_narrow, inner, 2 * width), both, 0, 0, tiled=True
    )

    kept, moved = applied_pass(own, mate, half_ham)
    moved = lax.ppermute(moved, "narrow", narrow_pairs)
    energy = jnp.repeat(third_energy, inner)[:, None]
    target = jnp.arange(height)
    source = target % states * inner + target // states
    swap = (source[:, None] == jnp.arange(height)[None, :]).astype(jnp.bfloat16)
    out = final_pass(
        half[None],
        pair.reshape(n_wide, n_narrow, inner, 2 * width),
        near, far, kept, moved, own, energy, swap, piece,
    )
    return out[None]


def solution(mesh):
    return jax.shard_map(
        on_device,
        mesh=mesh,
        in_specs=(
            P(None, "wide", None, "narrow"),
            P(),
            P(),
            P("wide", None),
            P("wide", None),
            P(None, ("wide", "narrow")),
            P(),
        ),
        out_specs=P(None, ("wide", "narrow"), None, None),
        check_vma=False,
    )
```

```python
import jax
import jax.numpy as jnp
from jax import lax
from jax.experimental import pallas as pl
from jax.experimental.pallas import tpu as pltpu
from jax.sharding import PartitionSpec as P

MIB = 1 << 20
NN = ((1,), (0,))
NT = ((1,), (1,))


def dot_f32(left, right, contract):
    return lax.dot_general(
        left, right, (contract, ((), ())), preferred_element_type=jnp.float32
    )


def params(mib):
    return pltpu.CompilerParams(vmem_limit_bytes=mib * MIB)


def cost(flops, moved):
    return pl.CostEstimate(flops=flops, bytes_accessed=moved, transcendentals=0)


def flatten(ref):
    return ref[...].reshape(-1, ref.shape[-1])


def side_by_side(refs, out_ref):
    height, width = refs[0].shape[1:]
    for slot, ref in enumerate(refs):
        for part in range(ref.shape[0]):
            rows = slice(slot * height, (slot + 1) * height)
            out_ref[rows, part * width : (part + 1) * width] = ref[part]


def forward_step(own_ref, mate_ref, *refs):
    *grid_refs, out_ref, rows_ref = refs

    @pl.when(pl.program_id(0) == 0)
    def _():
        side_by_side((own_ref, mate_ref), rows_ref)

    right = jnp.concatenate([flatten(ref) for ref in grid_refs], 0)
    vals = dot_f32(rows_ref[...], right, NT).astype(out_ref.dtype)
    states, per, _, inner, points = out_ref.shape
    vals = vals.reshape(2, states, inner, per * points)
    for block in range(per):
        for slot in range(2):
            out_ref[:, block, slot] = vals[slot, :, :, block * points : (block + 1) * points]


def piece_specs(gathered, piece, per):
    shards, sides, _, cols = gathered.shape
    block = (shards, 1, piece, cols)

    def spec(block_of_step, side):
        return pl.BlockSpec(block, lambda s, *_: (0, side, per * s + block_of_step, 0))

    return [spec(which, side) for which in range(per) for side in range(sides)]


def forward_pass(own, mate, gathered, states, piece, per=4):
    n_narrow, height, width = own.shape
    shards, sides, _, cols = gathered.shape
    shards = shards * sides
    inner = height // states
    points = shards * piece
    resident = pl.BlockSpec(own.shape, lambda s: (0, 0, 0))
    return pl.pallas_call(
        forward_step,
        grid=(n_narrow // per,),
        in_specs=[
            resident,
            resident,
            *piece_specs(gathered, piece, per),
        ],
        out_specs=pl.BlockSpec((states, per, 2, inner, points), lambda s: (0, s, 0, 0, 0)),
        out_shape=jax.ShapeDtypeStruct((states, n_narrow, 2, inner, points), jnp.bfloat16),
        scratch_shapes=[pltpu.VMEM((2 * height, cols), jnp.bfloat16)],
        compiler_params=params(50),
        cost_estimate=cost(4 * height * cols * points * n_narrow, 8 * MIB),
        name="forward_pass",
    )(own, mate, *[gathered] * (sides * per))


def middle_step(
    values_ref, grid_ref, turned_ref, potential_ref, across_ref, out_ref, rows_ref, kept_ref
):
    step = pl.program_id(0)
    half = pl.num_programs(0) // 2
    tile = grid_ref.shape[0]
    points = values_ref.shape[-1]
    width = 2 * points

    @pl.when(step == 0)
    def _():
        rows_ref[:, :, :, :points] = values_ref[:, 0]
        for slot in range(2):
            rows_ref[:, slot, :, points:] = values_ref[:, 1, 1 - slot]

    @pl.when(step < half)
    def _():
        vals = dot_f32(grid_ref[...], rows_ref[...].reshape(-1, width), NN)
        weighted = vals * potential_ref[...].astype(jnp.float32)
        kept_ref[pl.ds(pl.multiple_of(step * tile, tile), tile)] = weighted.astype(jnp.bfloat16)

    @pl.when(step >= half)
    def _():
        out_ref[:, :width] = dot_f32(turned_ref[...], kept_ref[...], NN).astype(out_ref.dtype)
        out_ref[:, width:] = across_ref[...]


def middle_pass(values, grid_one, turned, potential, across, tile=1024):
    n_one, width = across.shape
    half = n_one // tile
    early = lambda s: (jnp.minimum(s, half - 1), 0)
    late = lambda s: (jnp.maximum(s - half, 0), 0)
    groups, _, _, inner, points = values.shape
    return pl.pallas_call(
        middle_step,
        grid=(2 * half,),
        in_specs=[
            pl.BlockSpec(values.shape, lambda s: (0, 0, 0, 0, 0)),
            pl.BlockSpec((tile, n_one), early),
            pl.BlockSpec((tile, n_one), late),
            pl.BlockSpec((tile, width), early),
            pl.BlockSpec((tile, width), late),
        ],
        out_specs=pl.BlockSpec((tile, 2 * width), late),
        out_shape=jax.ShapeDtypeStruct((n_one, 2 * width), jnp.bfloat16),
        scratch_shapes=[
            pltpu.VMEM((groups, 2, inner, 2 * points), jnp.bfloat16),
            pltpu.VMEM((n_one, width), jnp.bfloat16),
        ],
        compiler_params=params(52),
        cost_estimate=cost(4 * n_one * n_one * width, 21 * MIB),
        name="middle_pass",
    )(values, grid_one, turned, potential, across)


def applied_step(own_ref, mate_ref, ham_ref, out_ref, sent_ref, rows_ref):
    @pl.when(pl.program_id(0) == 0)
    def _():
        side_by_side((own_ref, mate_ref), rows_ref)

    vals = dot_f32(rows_ref[...], flatten(ham_ref), NT)
    height = out_ref.shape[0]
    out_ref[...] = vals[:height]
    sent_ref[...] = vals[height:].astype(sent_ref.dtype)


def applied_pass(own, mate, gathered, steps=4):
    n_narrow, height, width = own.shape
    shards, sides, depth, cols = gathered.shape
    points = shards * sides * depth
    parts = steps // sides
    resident = pl.BlockSpec(own.shape, lambda s: (0, 0, 0))
    block = pl.BlockSpec((height, points // steps), lambda s: (0, s))
    return pl.pallas_call(
        applied_step,
        grid=(steps,),
        in_specs=[
            resident,
            resident,
            pl.BlockSpec((shards // parts, 1, depth, cols), lambda s: (s % parts, s // parts, 0, 0)),
        ],
        out_specs=[block, block],
        out_shape=[
            jax.ShapeDtypeStruct((height, points), jnp.float32),
            jax.ShapeDtypeStruct((height, points), jnp.bfloat16),
        ],
        scratch_shapes=[pltpu.VMEM((2 * height, cols), jnp.bfloat16)],
        compiler_params=params(50),
        cost_estimate=cost(4 * height * cols * points, 8 * MIB),
        name="applied_pass",
    )(own, mate, gathered)


def final_step(half_ref, near_ref, far_ref, *refs):
    *grid_refs, across_ref, kept_ref, moved_ref, own_ref, energy_ref, swap_ref = refs[:-2]
    out_ref, acc_ref = refs[-2:]
    step = pl.program_id(0)
    states, per, rows, _ = near_ref.shape
    height = states * rows
    lefts = [
        ref[:, block].reshape(height, -1) for ref in (near_ref, far_ref) for block in range(per)
    ]
    rights = [flatten(ref) for ref in grid_refs]
    total = dot_f32(jnp.concatenate(lefts, 1), jnp.concatenate(rights, 0), NN)

    @pl.when(step == 0)
    def _():
        acc_ref[...] = total

    @pl.when(step > 0)
    def _():
        acc_ref[...] += total

    @pl.when(step == pl.num_programs(0) - 1)
    def _():
        even = half_ref[0] == 0
        blocks, _, width = own_ref.shape
        part = width // 2
        for block in range(blocks):
            cols = slice(block * width, (block + 1) * width)
            kept = kept_ref[:, block * part : (block + 1) * part]
            moved = moved_ref[:, block * part : (block + 1) * part].astype(jnp.float32)
            low = jnp.where(even, kept, moved)
            high = jnp.where(even, moved, kept)
            left = lax.broadcasted_iota(jnp.int32, low.shape, 1) < part // 2
            applied = [
                jnp.where(left, low, pltpu.roll(high, part // 2, 1)),
                jnp.where(left, pltpu.roll(low, part // 2, 1), high),
            ]
            value = acc_ref[:, cols] + jnp.concatenate(applied, 1)
            value += across_ref[:, block].reshape(height, width).astype(jnp.float32)
            value += energy_ref[...] * own_ref[block].astype(jnp.float32)
            swapped = dot_f32(swap_ref[...], value.astype(jnp.bfloat16), NN)
            out_ref[:, :, cols] = swapped.astype(out_ref.dtype).reshape(rows, states, width)


def final_pass(half, received, near, far, kept, moved, own, energy, swap, piece, per=4):
    states, blocks, rows, double = received.shape
    width = double // 2
    height = states * rows
    shards, sides, _, cols = near.shape
    points = shards * sides * piece
    whole = lambda array: pl.BlockSpec(array.shape, lambda s, h: (0,) * array.ndim)
    return pl.pallas_call(
        final_step,
        grid_spec=pltpu.PrefetchScalarGridSpec(
            num_scalar_prefetch=1,
            grid=(blocks // per,),
            in_specs=[
                pl.BlockSpec((states, per, rows, points), lambda s, h: (0, s, 0, h[0])),
                pl.BlockSpec((states, per, rows, points), lambda s, h: (0, s, 0, 1 - h[0])),
                *piece_specs(near, piece, per),
                *piece_specs(far, piece, per),
                pl.BlockSpec((states, blocks, rows, width), lambda s, h: (0, 0, 0, 1)),
                whole(kept),
                whole(moved),
                whole(own),
                whole(energy),
                whole(swap),
            ],
            out_specs=pl.BlockSpec((rows, states, cols), lambda s, h: (0, 0, 0)),
            scratch_shapes=[pltpu.VMEM((height, cols), jnp.float32)],
        ),
        out_shape=jax.ShapeDtypeStruct((rows, states, cols), jnp.bfloat16),
        compiler_params=params(50),
        cost_estimate=cost(2 * height * cols * (cols + height), 14 * MIB),
        name="final_pass",
    )(
        half, received, received, *[near] * (sides * per), *[far] * (sides * per), received, kept,
        moved, own, energy, swap,
    )


def on_device(coeffs, ham_one, grid_one, ham_two, grid_two, pair_potential, third_energy):
    n_wide = lax.axis_size("wide")
    n_narrow = lax.axis_size("narrow")
    both = ("wide", "narrow")
    half = lax.axis_index("narrow") % 2
    narrow_pairs = [(n, n ^ 1) for n in range(n_narrow)]

    local = coeffs[0]
    rows, states, width = local.shape
    n_one, count = pair_potential.shape
    cols = grid_two.shape[1]
    inner = rows // n_narrow
    height = inner * states
    piece = count // 2
    share = rows // 2
    assert states == n_wide and inner == count and n_wide * count == width

    groups = n_wide // 2
    side = lax.axis_index("wide") // groups
    across_y = [(w, (w + groups) % n_wide) for w in range(n_wide)]
    members = [list(range(groups)), list(range(groups, n_wide))]

    def both_sides(mine, theirs):
        return jnp.where(side == 0, jnp.stack([mine, theirs]), jnp.stack([theirs, mine]))

    def gather(value):
        return lax.all_gather(value, "wide", axis=0, tiled=False, axis_index_groups=members)

    pieces = grid_two.reshape(n_narrow, 2, piece, cols)
    near = lax.dynamic_index_in_dim(pieces, half, 1, False).reshape(share, cols)
    near = jnp.concatenate([near, pair_potential.T.astype(jnp.bfloat16)], 0)
    near = gather(both_sides(near, lax.ppermute(near, "wide", across_y)))

    far = lax.dynamic_index_in_dim(pieces, 1 - half, 1, False).reshape(share, cols)
    stay = lax.dynamic_slice_in_dim(ham_two, half * share, share, 0)

    own = local.reshape(n_narrow, inner, states, width).swapaxes(1, 2)
    own = lax.all_to_all(own.reshape(n_narrow, height, width), "narrow", 0, 0, tiled=True)
    other_stay = lax.ppermute(stay, "wide", across_y)
    own, other_stay = lax.optimization_barrier((own, other_stay))
    half_ham = gather(both_sides(stay, other_stay))
    other_far = lax.ppermute(far, "wide", across_y)
    mate = lax.ppermute(own, "narrow", narrow_pairs)
    by_state = lax.all_to_all(jnp.swapaxes(local, 0, 1), "wide", 0, 0, tiled=True)

    turned = lax.optimization_barrier(grid_one.T)
    values = forward_pass(own, mate, near, states, piece)
    values, by_state, turned = lax.optimization_barrier((values, by_state, turned))
    by_state, other_far = lax.optimization_barrier((by_state, other_far))
    far = gather(both_sides(far, other_far))
    across = dot_f32(ham_one, by_state.reshape(n_one, width), NN).astype(jnp.bfloat16)
    values = lax.all_to_all(
        values.reshape(n_wide * n_narrow, 2 * inner, width // 2), both, 0, 0, tiled=True
    )
    values = values.reshape(n_wide * n_narrow // 2, 2, 2, inner, width // 2)
    potential = near[:, :, share:].reshape(groups, 2, 2, piece, n_one).transpose(2, 1, 0, 3, 4)
    potential = potential.reshape(width, n_one).T
    pair = middle_pass(values, grid_one, turned, potential, across)
    pair = lax.all_to_all(
        pair.reshape(n_wide * n_narrow, inner, 2 * width), both, 0, 0, tiled=True
    )

    kept, moved = applied_pass(own, mate, half_ham)
    moved = lax.ppermute(moved, "narrow", narrow_pairs)
    energy = jnp.repeat(third_energy, inner)[:, None]
    target = jnp.arange(height)
    source = target % states * inner + target // states
    swap = (source[:, None] == jnp.arange(height)[None, :]).astype(jnp.bfloat16)
    out = final_pass(
        half[None],
        pair.reshape(n_wide, n_narrow, inner, 2 * width),
        near, far, kept, moved, own, energy, swap, piece,
    )
    return out[None]


def solution(mesh):
    return jax.shard_map(
        on_device,
        mesh=mesh,
        in_specs=(
            P(None, "wide", None, "narrow"),
            P(),
            P(),
            P("wide", None),
            P("wide", None),
            P(None, ("wide", "narrow")),
            P(),
        ),
        out_specs=P(None, ("wide", "narrow"), None, None),
        check_vma=False,
    )
```

```python
import jax
import jax.numpy as jnp
from jax import lax
from jax.experimental import pallas as pl
from jax.experimental.pallas import tpu as pltpu
from jax.sharding import PartitionSpec as P

MIB = 1 << 20
NN = ((1,), (0,))
NT = ((1,), (1,))


def dot_f32(left, right, contract):
    return lax.dot_general(
        left, right, (contract, ((), ())), preferred_element_type=jnp.float32
    )


def params(mib):
    return pltpu.CompilerParams(vmem_limit_bytes=mib * MIB)


def cost(flops, moved):
    return pl.CostEstimate(flops=flops, bytes_accessed=moved, transcendentals=0)


def flatten(ref):
    return ref[...].reshape(-1, ref.shape[-1])


def side_by_side(refs, out_ref):
    height, width = refs[0].shape[1:]
    for slot, ref in enumerate(refs):
        for part in range(ref.shape[0]):
            rows = slice(slot * height, (slot + 1) * height)
            out_ref[rows, part * width : (part + 1) * width] = ref[part]


def forward_step(own_ref, mate_ref, *refs):
    *grid_refs, out_ref, rows_ref = refs

    @pl.when(pl.program_id(0) == 0)
    def _():
        side_by_side((own_ref, mate_ref), rows_ref)

    right = jnp.concatenate([flatten(ref) for ref in grid_refs], 0)
    vals = dot_f32(rows_ref[...], right, NT).astype(out_ref.dtype)
    states, per, _, inner, points = out_ref.shape
    vals = vals.reshape(2, states, inner, per * points)
    for block in range(per):
        for slot in range(2):
            out_ref[:, block, slot] = vals[slot, :, :, block * points : (block + 1) * points]


def piece_specs(gathered, piece, per):
    shards, sides, _, cols = gathered.shape
    block = (shards, 1, piece, cols)

    def spec(block_of_step, side):
        return pl.BlockSpec(block, lambda s, *_: (0, side, per * s + block_of_step, 0))

    return [spec(which, side) for which in range(per) for side in range(sides)]


def forward_pass(own, mate, gathered, states, piece, per=4):
    n_narrow, height, width = own.shape
    shards, sides, _, cols = gathered.shape
    shards = shards * sides
    inner = height // states
    points = shards * piece
    resident = pl.BlockSpec(own.shape, lambda s: (0, 0, 0))
    return pl.pallas_call(
        forward_step,
        grid=(n_narrow // per,),
        in_specs=[
            resident,
            resident,
            *piece_specs(gathered, piece, per),
        ],
        out_specs=pl.BlockSpec((states, per, 2, inner, points), lambda s: (0, s, 0, 0, 0)),
        out_shape=jax.ShapeDtypeStruct((states, n_narrow, 2, inner, points), jnp.bfloat16),
        scratch_shapes=[pltpu.VMEM((2 * height, cols), jnp.bfloat16)],
        compiler_params=params(50),
        cost_estimate=cost(4 * height * cols * points * n_narrow, 8 * MIB),
        name="forward_pass",
    )(own, mate, *[gathered] * (sides * per))


def middle_step(
    values_ref, grid_ref, turned_ref, potential_ref, across_ref, out_ref, rows_ref, kept_ref
):
    step = pl.program_id(0)
    half = pl.num_programs(0) // 2
    tile = grid_ref.shape[0]
    points = values_ref.shape[-1]
    width = 2 * points

    @pl.when(step == 0)
    def _():
        rows_ref[:, :, :, :points] = values_ref[:, 0]
        for slot in range(2):
            rows_ref[:, slot, :, points:] = values_ref[:, 1, 1 - slot]

    @pl.when(step < half)
    def _():
        vals = dot_f32(grid_ref[...], rows_ref[...].reshape(-1, width), NN)
        weighted = vals * potential_ref[...].astype(jnp.float32)
        kept_ref[pl.ds(pl.multiple_of(step * tile, tile), tile)] = weighted.astype(jnp.bfloat16)

    @pl.when(step >= half)
    def _():
        out_ref[:, :width] = dot_f32(turned_ref[...], kept_ref[...], NN).astype(out_ref.dtype)
        out_ref[:, width:] = across_ref[...]


def middle_pass(values, grid_one, turned, potential, across, tile=1024):
    n_one, width = across.shape
    half = n_one // tile
    early = lambda s: (jnp.minimum(s, half - 1), 0)
    late = lambda s: (jnp.maximum(s - half, 0), 0)
    groups, _, _, inner, points = values.shape
    return pl.pallas_call(
        middle_step,
        grid=(2 * half,),
        in_specs=[
            pl.BlockSpec(values.shape, lambda s: (0, 0, 0, 0, 0)),
            pl.BlockSpec((tile, n_one), early),
            pl.BlockSpec((tile, n_one), late),
            pl.BlockSpec((tile, width), early),
            pl.BlockSpec((tile, width), late),
        ],
        out_specs=pl.BlockSpec((tile, 2 * width), late),
        out_shape=jax.ShapeDtypeStruct((n_one, 2 * width), jnp.bfloat16),
        scratch_shapes=[
            pltpu.VMEM((groups, 2, inner, 2 * points), jnp.bfloat16),
            pltpu.VMEM((n_one, width), jnp.bfloat16),
        ],
        compiler_params=params(52),
        cost_estimate=cost(4 * n_one * n_one * width, 21 * MIB),
        name="middle_pass",
    )(values, grid_one, turned, potential, across)


def applied_step(own_ref, mate_ref, ham_ref, out_ref, sent_ref, rows_ref):
    @pl.when(pl.program_id(0) == 0)
    def _():
        side_by_side((own_ref, mate_ref), rows_ref)

    vals = dot_f32(rows_ref[...], flatten(ham_ref), NT)
    height = out_ref.shape[0]
    out_ref[...] = vals[:height]
    sent_ref[...] = vals[height:].astype(sent_ref.dtype)


def applied_pass(own, mate, gathered, steps=4):
    n_narrow, height, width = own.shape
    shards, sides, depth, cols = gathered.shape
    points = shards * sides * depth
    parts = steps // sides
    resident = pl.BlockSpec(own.shape, lambda s: (0, 0, 0))
    block = pl.BlockSpec((height, points // steps), lambda s: (0, s))
    return pl.pallas_call(
        applied_step,
        grid=(steps,),
        in_specs=[
            resident,
            resident,
            pl.BlockSpec((shards // parts, 1, depth, cols), lambda s: (s % parts, s // parts, 0, 0)),
        ],
        out_specs=[block, block],
        out_shape=[
            jax.ShapeDtypeStruct((height, points), jnp.float32),
            jax.ShapeDtypeStruct((height, points), jnp.bfloat16),
        ],
        scratch_shapes=[pltpu.VMEM((2 * height, cols), jnp.bfloat16)],
        compiler_params=params(50),
        cost_estimate=cost(4 * height * cols * points, 8 * MIB),
        name="applied_pass",
    )(own, mate, gathered)


def final_step(half_ref, near_ref, far_ref, *refs):
    *grid_refs, across_ref, kept_ref, moved_ref, own_ref, energy_ref, swap_ref = refs[:-2]
    out_ref, acc_ref = refs[-2:]
    step = pl.program_id(0)
    states, per, rows, _ = near_ref.shape
    height = states * rows
    lefts = [
        ref[:, block].reshape(height, -1) for ref in (near_ref, far_ref) for block in range(per)
    ]
    rights = [flatten(ref) for ref in grid_refs]
    total = dot_f32(jnp.concatenate(lefts, 1), jnp.concatenate(rights, 0), NN)

    @pl.when(step == 0)
    def _():
        acc_ref[...] = total

    @pl.when(step > 0)
    def _():
        acc_ref[...] += total

    @pl.when(step == pl.num_programs(0) - 1)
    def _():
        even = half_ref[0] == 0
        blocks, _, width = own_ref.shape
        part = width // 2
        for block in range(blocks):
            cols = slice(block * width, (block + 1) * width)
            kept = kept_ref[:, block * part : (block + 1) * part]
            moved = moved_ref[:, block * part : (block + 1) * part].astype(jnp.float32)
            low = jnp.where(even, kept, moved)
            high = jnp.where(even, moved, kept)
            left = lax.broadcasted_iota(jnp.int32, low.shape, 1) < part // 2
            applied = [
                jnp.where(left, low, pltpu.roll(high, part // 2, 1)),
                jnp.where(left, pltpu.roll(low, part // 2, 1), high),
            ]
            value = acc_ref[:, cols] + jnp.concatenate(applied, 1)
            value += across_ref[:, block].reshape(height, width).astype(jnp.float32)
            value += energy_ref[...] * own_ref[block].astype(jnp.float32)
            swapped = dot_f32(swap_ref[...], value.astype(jnp.bfloat16), NN)
            out_ref[:, :, cols] = swapped.astype(out_ref.dtype).reshape(rows, states, width)


def final_pass(half, received, near, far, kept, moved, own, energy, swap, piece, per=4):
    states, blocks, rows, double = received.shape
    width = double // 2
    height = states * rows
    shards, sides, _, cols = near.shape
    points = shards * sides * piece
    whole = lambda array: pl.BlockSpec(array.shape, lambda s, h: (0,) * array.ndim)
    return pl.pallas_call(
        final_step,
        grid_spec=pltpu.PrefetchScalarGridSpec(
            num_scalar_prefetch=1,
            grid=(blocks // per,),
            in_specs=[
                pl.BlockSpec((states, per, rows, points), lambda s, h: (0, s, 0, h[0])),
                pl.BlockSpec((states, per, rows, points), lambda s, h: (0, s, 0, 1 - h[0])),
                *piece_specs(near, piece, per),
                *piece_specs(far, piece, per),
                pl.BlockSpec((states, blocks, rows, width), lambda s, h: (0, 0, 0, 1)),
                whole(kept),
                whole(moved),
                whole(own),
                whole(energy),
                whole(swap),
            ],
            out_specs=pl.BlockSpec((rows, states, cols), lambda s, h: (0, 0, 0)),
            scratch_shapes=[pltpu.VMEM((height, cols), jnp.float32)],
        ),
        out_shape=jax.ShapeDtypeStruct((rows, states, cols), jnp.bfloat16),
        compiler_params=params(50),
        cost_estimate=cost(2 * height * cols * (cols + height), 14 * MIB),
        name="final_pass",
    )(
        half, received, received, *[near] * (sides * per), *[far] * (sides * per), received, kept,
        moved, own, energy, swap,
    )


def on_device(coeffs, ham_one, grid_one, ham_two, grid_two, pair_potential, third_energy):
    n_wide = lax.axis_size("wide")
    n_narrow = lax.axis_size("narrow")
    both = ("wide", "narrow")
    half = lax.axis_index("narrow") % 2
    narrow_pairs = [(n, n ^ 1) for n in range(n_narrow)]

    local = coeffs[0]
    rows, states, width = local.shape
    n_one, count = pair_potential.shape
    cols = grid_two.shape[1]
    inner = rows // n_narrow
    height = inner * states
    piece = count // 2
    share = rows // 2
    assert states == n_wide and inner == count and n_wide * count == width

    groups = n_wide // 2
    side = lax.axis_index("wide") // groups
    across_y = [(w, (w + groups) % n_wide) for w in range(n_wide)]
    members = [list(range(groups)), list(range(groups, n_wide))]

    def both_sides(mine, theirs):
        return jnp.where(side == 0, jnp.stack([mine, theirs]), jnp.stack([theirs, mine]))

    def gather(value):
        return lax.all_gather(value, "wide", axis=0, tiled=False, axis_index_groups=members)

    pieces = grid_two.reshape(n_narrow, 2, piece, cols)
    near = lax.dynamic_index_in_dim(pieces, half, 1, False).reshape(share, cols)
    near = jnp.concatenate([near, pair_potential.T.astype(jnp.bfloat16)], 0)
    other_near = lax.ppermute(near, "wide", across_y)
    to_rows = local.reshape(n_narrow, inner, states, width).swapaxes(1, 2)
    to_rows = to_rows.reshape(n_narrow, height, width)
    to_states = jnp.swapaxes(local, 0, 1)
    other_near, to_rows, to_states = lax.optimization_barrier((other_near, to_rows, to_states))
    near = gather(both_sides(near, other_near))

    far = lax.dynamic_index_in_dim(pieces, 1 - half, 1, False).reshape(share, cols)
    stay = lax.dynamic_slice_in_dim(ham_two, half * share, share, 0)

    own = lax.all_to_all(to_rows, "narrow", 0, 0, tiled=True)
    other_stay = lax.ppermute(stay, "wide", across_y)
    own, other_stay = lax.optimization_barrier((own, other_stay))
    half_ham = gather(both_sides(stay, other_stay))
    other_far = lax.ppermute(far, "wide", across_y)
    mate = lax.ppermute(own, "narrow", narrow_pairs)
    by_state = lax.all_to_all(to_states, "wide", 0, 0, tiled=True)

    turned = lax.optimization_barrier(grid_one.T)
    values = forward_pass(own, mate, near, states, piece)
    values, by_state, turned = lax.optimization_barrier((values, by_state, turned))
    by_state, other_far = lax.optimization_barrier((by_state, other_far))
    far = gather(both_sides(far, other_far))
    across = dot_f32(ham_one, by_state.reshape(n_one, width), NN).astype(jnp.bfloat16)
    values = lax.all_to_all(
        values.reshape(n_wide * n_narrow, 2 * inner, width // 2), both, 0, 0, tiled=True
    )
    values = values.reshape(n_wide * n_narrow // 2, 2, 2, inner, width // 2)
    potential = near[:, :, share:].reshape(groups, 2, 2, piece, n_one).transpose(2, 1, 0, 3, 4)
    potential = potential.reshape(width, n_one).T
    pair = middle_pass(values, grid_one, turned, potential, across)
    pair = lax.all_to_all(
        pair.reshape(n_wide * n_narrow, inner, 2 * width), both, 0, 0, tiled=True
    )

    kept, moved = applied_pass(own, mate, half_ham)
    moved = lax.ppermute(moved, "narrow", narrow_pairs)
    energy = jnp.repeat(third_energy, inner)[:, None]
    target = jnp.arange(height)
    source = target % states * inner + target // states
    swap = (source[:, None] == jnp.arange(height)[None, :]).astype(jnp.bfloat16)
    out = final_pass(
        half[None],
        pair.reshape(n_wide, n_narrow, inner, 2 * width),
        near, far, kept, moved, own, energy, swap, piece,
    )
    return out[None]


def solution(mesh):
    return jax.shard_map(
        on_device,
        mesh=mesh,
        in_specs=(
            P(None, "wide", None, "narrow"),
            P(),
            P(),
            P("wide", None),
            P("wide", None),
            P(None, ("wide", "narrow")),
            P(),
        ),
        out_specs=P(None, ("wide", "narrow"), None, None),
        check_vma=False,
    )
```

```python
import jax
import jax.numpy as jnp
from jax import lax
from jax.experimental import pallas as pl
from jax.experimental.pallas import tpu as pltpu
from jax.sharding import PartitionSpec as P

MIB = 1 << 20
NN = ((1,), (0,))
NT = ((1,), (1,))


def dot_f32(left, right, contract):
    return lax.dot_general(
        left, right, (contract, ((), ())), preferred_element_type=jnp.float32
    )


def params(mib):
    return pltpu.CompilerParams(vmem_limit_bytes=mib * MIB)


def cost(flops, moved):
    return pl.CostEstimate(flops=flops, bytes_accessed=moved, transcendentals=0)


def flatten(ref):
    return ref[...].reshape(-1, ref.shape[-1])


def side_by_side(refs, out_ref):
    height, width = refs[0].shape[1:]
    for slot, ref in enumerate(refs):
        for part in range(ref.shape[0]):
            rows = slice(slot * height, (slot + 1) * height)
            out_ref[rows, part * width : (part + 1) * width] = ref[part]


def forward_step(own_ref, mate_ref, *refs):
    *grid_refs, out_ref, rows_ref = refs

    @pl.when(pl.program_id(0) == 0)
    def _():
        side_by_side((own_ref, mate_ref), rows_ref)

    right = jnp.concatenate([flatten(ref) for ref in grid_refs], 0)
    vals = dot_f32(rows_ref[...], right, NT).astype(out_ref.dtype)
    states, per, _, inner, points = out_ref.shape
    vals = vals.reshape(2, states, inner, per * points)
    for block in range(per):
        for slot in range(2):
            out_ref[:, block, slot] = vals[slot, :, :, block * points : (block + 1) * points]


def piece_specs(gathered, piece, per):
    shards, sides, _, cols = gathered.shape
    block = (shards, 1, piece, cols)

    def spec(block_of_step, side):
        return pl.BlockSpec(block, lambda s, *_: (0, side, per * s + block_of_step, 0))

    return [spec(which, side) for which in range(per) for side in range(sides)]


def forward_pass(own, mate, gathered, states, piece, per=4):
    n_narrow, height, width = own.shape
    shards, sides, _, cols = gathered.shape
    shards = shards * sides
    inner = height // states
    points = shards * piece
    resident = pl.BlockSpec(own.shape, lambda s: (0, 0, 0))
    return pl.pallas_call(
        forward_step,
        grid=(n_narrow // per,),
        in_specs=[
            resident,
            resident,
            *piece_specs(gathered, piece, per),
        ],
        out_specs=pl.BlockSpec((states, per, 2, inner, points), lambda s: (0, s, 0, 0, 0)),
        out_shape=jax.ShapeDtypeStruct((states, n_narrow, 2, inner, points), jnp.bfloat16),
        scratch_shapes=[pltpu.VMEM((2 * height, cols), jnp.bfloat16)],
        compiler_params=params(50),
        cost_estimate=cost(4 * height * cols * points * n_narrow, 8 * MIB),
        name="forward_pass",
    )(own, mate, *[gathered] * (sides * per))


def middle_step(
    values_ref, grid_ref, turned_ref, potential_ref, across_ref, out_ref, rows_ref, kept_ref
):
    step = pl.program_id(0)
    half = pl.num_programs(0) // 2
    tile = grid_ref.shape[0]
    points = values_ref.shape[-1]
    width = 2 * points

    @pl.when(step == 0)
    def _():
        rows_ref[:, :, :, :points] = values_ref[:, 0]
        for slot in range(2):
            rows_ref[:, slot, :, points:] = values_ref[:, 1, 1 - slot]

    @pl.when(step < half)
    def _():
        vals = dot_f32(grid_ref[...], rows_ref[...].reshape(-1, width), NN)
        weighted = vals * potential_ref[...].astype(jnp.float32)
        kept_ref[pl.ds(pl.multiple_of(step * tile, tile), tile)] = weighted.astype(jnp.bfloat16)

    @pl.when(step >= half)
    def _():
        out_ref[:, :width] = dot_f32(turned_ref[...], kept_ref[...], NN).astype(out_ref.dtype)
        out_ref[:, width:] = across_ref[...]


def middle_pass(values, grid_one, turned, potential, across, tile=1024):
    n_one, width = across.shape
    half = n_one // tile
    early = lambda s: (jnp.minimum(s, half - 1), 0)
    late = lambda s: (jnp.maximum(s - half, 0), 0)
    groups, _, _, inner, points = values.shape
    return pl.pallas_call(
        middle_step,
        grid=(2 * half,),
        in_specs=[
            pl.BlockSpec(values.shape, lambda s: (0, 0, 0, 0, 0)),
            pl.BlockSpec((tile, n_one), early),
            pl.BlockSpec((tile, n_one), late),
            pl.BlockSpec((tile, width), early),
            pl.BlockSpec((tile, width), late),
        ],
        out_specs=pl.BlockSpec((tile, 2 * width), late),
        out_shape=jax.ShapeDtypeStruct((n_one, 2 * width), jnp.bfloat16),
        scratch_shapes=[
            pltpu.VMEM((groups, 2, inner, 2 * points), jnp.bfloat16),
            pltpu.VMEM((n_one, width), jnp.bfloat16),
        ],
        compiler_params=params(52),
        cost_estimate=cost(4 * n_one * n_one * width, 21 * MIB),
        name="middle_pass",
    )(values, grid_one, turned, potential, across)


def applied_step(own_ref, mate_ref, ham_ref, out_ref, sent_ref, rows_ref):
    @pl.when(pl.program_id(0) == 0)
    def _():
        side_by_side((own_ref, mate_ref), rows_ref)

    vals = dot_f32(rows_ref[...], flatten(ham_ref), NT)
    height = out_ref.shape[0]
    out_ref[...] = vals[:height]
    sent_ref[...] = vals[height:].astype(sent_ref.dtype)


def applied_pass(own, mate, gathered, steps=4):
    n_narrow, height, width = own.shape
    shards, sides, depth, cols = gathered.shape
    points = shards * sides * depth
    parts = steps // sides
    resident = pl.BlockSpec(own.shape, lambda s: (0, 0, 0))
    block = pl.BlockSpec((height, points // steps), lambda s: (0, s))
    return pl.pallas_call(
        applied_step,
        grid=(steps,),
        in_specs=[
            resident,
            resident,
            pl.BlockSpec((shards // parts, 1, depth, cols), lambda s: (s % parts, s // parts, 0, 0)),
        ],
        out_specs=[block, block],
        out_shape=[
            jax.ShapeDtypeStruct((height, points), jnp.float32),
            jax.ShapeDtypeStruct((height, points), jnp.bfloat16),
        ],
        scratch_shapes=[pltpu.VMEM((2 * height, cols), jnp.bfloat16)],
        compiler_params=params(50),
        cost_estimate=cost(4 * height * cols * points, 8 * MIB),
        name="applied_pass",
    )(own, mate, gathered)


def final_step(half_ref, near_ref, far_ref, *refs):
    *grid_refs, across_ref, kept_ref, moved_ref, own_ref, energy_ref, swap_ref = refs[:-2]
    out_ref, acc_ref = refs[-2:]
    step = pl.program_id(0)
    states, per, rows, _ = near_ref.shape
    height = states * rows
    lefts = [
        ref[:, block].reshape(height, -1) for ref in (near_ref, far_ref) for block in range(per)
    ]
    rights = [flatten(ref) for ref in grid_refs]
    total = dot_f32(jnp.concatenate(lefts, 1), jnp.concatenate(rights, 0), NN)

    @pl.when(step == 0)
    def _():
        acc_ref[...] = total

    @pl.when(step > 0)
    def _():
        acc_ref[...] += total

    @pl.when(step == pl.num_programs(0) - 1)
    def _():
        even = half_ref[0] == 0
        blocks, _, width = own_ref.shape
        part = width // 2
        for block in range(blocks):
            cols = slice(block * width, (block + 1) * width)
            kept = kept_ref[:, block * part : (block + 1) * part]
            moved = moved_ref[:, block * part : (block + 1) * part].astype(jnp.float32)
            low = jnp.where(even, kept, moved)
            high = jnp.where(even, moved, kept)
            left = lax.broadcasted_iota(jnp.int32, low.shape, 1) < part // 2
            applied = [
                jnp.where(left, low, pltpu.roll(high, part // 2, 1)),
                jnp.where(left, pltpu.roll(low, part // 2, 1), high),
            ]
            value = acc_ref[:, cols] + jnp.concatenate(applied, 1)
            value += across_ref[:, block].reshape(height, width).astype(jnp.float32)
            value += energy_ref[...] * own_ref[block].astype(jnp.float32)
            swapped = dot_f32(swap_ref[...], value.astype(jnp.bfloat16), NN)
            out_ref[:, :, cols] = swapped.astype(out_ref.dtype).reshape(rows, states, width)


def final_pass(half, received, near, far, kept, moved, own, energy, swap, piece, per=4):
    states, blocks, rows, double = received.shape
    width = double // 2
    height = states * rows
    shards, sides, _, cols = near.shape
    points = shards * sides * piece
    whole = lambda array: pl.BlockSpec(array.shape, lambda s, h: (0,) * array.ndim)
    return pl.pallas_call(
        final_step,
        grid_spec=pltpu.PrefetchScalarGridSpec(
            num_scalar_prefetch=1,
            grid=(blocks // per,),
            in_specs=[
                pl.BlockSpec((states, per, rows, points), lambda s, h: (0, s, 0, h[0])),
                pl.BlockSpec((states, per, rows, points), lambda s, h: (0, s, 0, 1 - h[0])),
                *piece_specs(near, piece, per),
                *piece_specs(far, piece, per),
                pl.BlockSpec((states, blocks, rows, width), lambda s, h: (0, 0, 0, 1)),
                whole(kept),
                whole(moved),
                whole(own),
                whole(energy),
                whole(swap),
            ],
            out_specs=pl.BlockSpec((rows, states, cols), lambda s, h: (0, 0, 0)),
            scratch_shapes=[pltpu.VMEM((height, cols), jnp.float32)],
        ),
        out_shape=jax.ShapeDtypeStruct((rows, states, cols), jnp.bfloat16),
        compiler_params=params(50),
        cost_estimate=cost(2 * height * cols * (cols + height), 14 * MIB),
        name="final_pass",
    )(
        half, received, received, *[near] * (sides * per), *[far] * (sides * per), received, kept,
        moved, own, energy, swap,
    )


def on_device(coeffs, ham_one, grid_one, ham_two, grid_two, pair_potential, third_energy):
    n_wide = lax.axis_size("wide")
    n_narrow = lax.axis_size("narrow")
    both = ("wide", "narrow")
    half = lax.axis_index("narrow") % 2
    narrow_pairs = [(n, n ^ 1) for n in range(n_narrow)]

    local = coeffs[0]
    rows, states, width = local.shape
    n_one, count = pair_potential.shape
    cols = grid_two.shape[1]
    inner = rows // n_narrow
    height = inner * states
    piece = count // 2
    share = rows // 2
    assert states == n_wide and inner == count and n_wide * count == width

    groups = n_wide // 2
    side = lax.axis_index("wide") // groups
    across_y = [(w, (w + groups) % n_wide) for w in range(n_wide)]
    members = [list(range(groups)), list(range(groups, n_wide))]

    def both_sides(mine, theirs):
        return jnp.where(side == 0, jnp.stack([mine, theirs]), jnp.stack([theirs, mine]))

    def gather(value):
        return lax.all_gather(value, "wide", axis=0, tiled=False, axis_index_groups=members)

    pieces = grid_two.reshape(n_narrow, 2, piece, cols)
    near = lax.dynamic_index_in_dim(pieces, half, 1, False).reshape(share, cols)
    near = jnp.concatenate([near, pair_potential.T.astype(jnp.bfloat16)], 0)
    near = gather(both_sides(near, lax.ppermute(near, "wide", across_y)))

    far = lax.dynamic_index_in_dim(pieces, 1 - half, 1, False).reshape(share, cols)
    stay = lax.dynamic_slice_in_dim(ham_two, half * share, share, 0)

    own = local.reshape(n_narrow, inner, states, width).swapaxes(1, 2)
    own = lax.all_to_all(own.reshape(n_narrow, height, width), "narrow", 0, 0, tiled=True)
    other_stay = lax.ppermute(stay, "wide", across_y)
    to_states = jnp.swapaxes(local, 0, 1)
    own, other_stay, to_states = lax.optimization_barrier((own, other_stay, to_states))
    half_ham = gather(both_sides(stay, other_stay))
    other_far = lax.ppermute(far, "wide", across_y)
    mate = lax.ppermute(own, "narrow", narrow_pairs)
    by_state = lax.all_to_all(to_states, "wide", 0, 0, tiled=True)

    turned = lax.optimization_barrier(grid_one.T)
    values = forward_pass(own, mate, near, states, piece)
    values, by_state, turned = lax.optimization_barrier((values, by_state, turned))
    by_state, other_far = lax.optimization_barrier((by_state, other_far))
    far = gather(both_sides(far, other_far))
    across = dot_f32(ham_one, by_state.reshape(n_one, width), NN).astype(jnp.bfloat16)
    values = lax.all_to_all(
        values.reshape(n_wide * n_narrow, 2 * inner, width // 2), both, 0, 0, tiled=True
    )
    values = values.reshape(n_wide * n_narrow // 2, 2, 2, inner, width // 2)
    potential = near[:, :, share:].reshape(groups, 2, 2, piece, n_one).transpose(2, 1, 0, 3, 4)
    potential = potential.reshape(width, n_one).T
    pair = middle_pass(values, grid_one, turned, potential, across)
    pair = lax.all_to_all(
        pair.reshape(n_wide * n_narrow, inner, 2 * width), both, 0, 0, tiled=True
    )

    kept, moved = applied_pass(own, mate, half_ham)
    moved = lax.ppermute(moved, "narrow", narrow_pairs)
    energy = jnp.repeat(third_energy, inner)[:, None]
    target = jnp.arange(height)
    source = target % states * inner + target // states
    swap = (source[:, None] == jnp.arange(height)[None, :]).astype(jnp.bfloat16)
    out = final_pass(
        half[None],
        pair.reshape(n_wide, n_narrow, inner, 2 * width),
        near, far, kept, moved, own, energy, swap, piece,
    )
    return out[None]


def solution(mesh):
    return jax.shard_map(
        on_device,
        mesh=mesh,
        in_specs=(
            P(None, "wide", None, "narrow"),
            P(),
            P(),
            P("wide", None),
            P("wide", None),
            P(None, ("wide", "narrow")),
            P(),
        ),
        out_specs=P(None, ("wide", "narrow"), None, None),
        check_vma=False,
    )
```
